32 devices in a mesh: seq: 8 (over z, x), chan: 4 (over y, core).
Axes of the slice: x: 2, y: 2, z: 4, core: 2. Of those that a mesh axis runs over, the one named last changes fastest.
Arguments:
- tokens: bfloat16 [4, 512, 1024], P(None, 'chan', 'seq'), may hold values from -6 to 6
- lengths: int32 [4, 1], replicated, may hold values from 256 to 1024, as said below
- ln_gain: float32 [512], P('chan'), may hold values from 0.5 to 1.5
- ln_bias: float32 [512], P('chan'), may hold values from -4 to 4
- b_coef: float32 [2, 512, 64], P(None, 'chan'), may hold values from -0.75 to 0.75
- e_coef: float32 [2, 512, 64], P(None, 'chan'), may hold values from -0.75 to 0.75
- c_coef: float32 [2, 512, 64], P(None, 'chan'), may hold values from -0.875 to 0.875
- skip_gain: float32 [512], P('chan'), may hold values from 0.5 to 1.5
- decay_rate: float32 [512, 64], P('chan'), may hold values from 0.0001953125 to 0.05
- rotation: float32 [512, 64], P('chan'), may hold values from -3.140625 to 3.140625
- w_value: bfloat16 [512, 512], P(None, 'chan'), may hold values from -0.5 to 0.5
- w_gate: bfloat16 [512, 512], P(None, 'chan'), may hold values from -0.25 to 0.25
- bias_value: float32 [512], P('chan'), may hold values from -4 to 4
- bias_gate: float32 [512], P('chan'), may hold values from -4 to 4
- out_cotangent: bfloat16 [4, 512, 1024], P(None, 'chan', 'seq'), may hold values from -6 to 6
Outputs:
- out: bfloat16 [4, 512, 1024], P(None, 'chan', 'seq')
- input_grad: float32 [4, 512, 1024], P(None, 'chan', 'seq')
- d_ln_gain: float32 [512], P('chan')
- d_ln_bias: float32 [512], P('chan')
- d_b_coef: float32 [2, 512, 64], P(None, 'chan')
- d_e_coef: float32 [2, 512, 64], P(None, 'chan')
- d_c_coef: float32 [2, 512, 64], P(None, 'chan')
- d_skip_gain: float32 [512], P('chan')
- d_w_value: float32 [512, 512], P('seq', 'chan')
- d_w_gate: float32 [512, 512], P('seq', 'chan')
- d_bias_value: float32 [512], P('chan')
- d_bias_gate: float32 [512], P('chan')
The draws below stay inside these ranges and needn't reach their ends.
Inputs may be any that keep to these rules, and one draw needn't show every extreme that they name: `lengths`: in every draw the sequence of one micro-batch, which one drawn from the seed, fills its whole slot of 1024.
All inputs are finite; a program needn't handle non-finite values.
Results may differ from the reference program's by a relative error of at most 0.005.
The reference program's roundings to bfloat16 on the way count: a program that leaves them out, or rounds other values in their place, can miss the bound.
Values may be sent and summed in bfloat16 or wider, within the bound.
No kernel may reach another device: no remote copies, remote signals or barrier semaphores. Data moves between devices by JAX's collectives and lax.ppermute only.
A program may use at most 192 MiB of HBM per device.

```python
import math
import jax
import jax.numpy as jnp
from jax import lax

H = 512
N = 64
MICRO = 4
ROWS = 1024
SLOT = 1024
SEQS = 1


def draw_lengths(key, part):
    first_key, second_key = jax.random.split(key)
    drawn_lens = jax.random.randint(first_key, (MICRO, SEQS), SLOT // 4, SLOT + 1)
    chosen = jax.random.randint(second_key, (), 0, MICRO * SEQS)
    flat_ids = jnp.arange(MICRO * SEQS, dtype=jnp.int32).reshape(MICRO, SEQS)
    return jnp.where(flat_ids == chosen, SLOT, drawn_lens).astype(jnp.int32)


def block_scale(rng, dims, shards, smallest, high):
    gain = 1.0
    for axis_at, parts in shards:
        steps = jax.random.uniform(jax.random.fold_in(jax.random.fold_in(rng, 6), axis_at), (parts,), jnp.float32, smallest / len(shards), high / len(shards))
        gain = gain * jnp.repeat(jnp.exp(steps), dims[axis_at] // parts).reshape((-1,) + (1,) * (len(dims) - 1 - axis_at))
    return gain


def normal_values(key, shape, spread, bound, pieces=(), kind=jnp.bfloat16):
    result = spread * jax.random.normal(key, shape, jnp.float32)
    if pieces:
        result = result * block_scale(key, shape, pieces, -0.22, 0.18)
    return jnp.clip(result, -bound, bound).astype(kind)


def setup_inputs(seed: int = 0) -> dict:
    streams_of = jax.random.split(jax.random.key(seed), 16)
    return {
        "tokens": normal_values(streams_of[0], (MICRO, H, ROWS), 1.0, 6.0, ((1, 4), (2, 8))),
        "lengths": draw_lengths(jax.random.fold_in(streams_of[15], 71), 0),
        "ln_gain": jnp.clip(1.0 + 0.1 * jax.random.normal(streams_of[2], (H,), jnp.float32), 0.5, 1.5),
        "ln_bias": normal_values(streams_of[3], (H,), 0.3, 4.0, ((0, 4),), jnp.float32),
        "b_coef": normal_values(streams_of[4], (2, H, N), 0.05, 0.75, ((1, 4),), jnp.float32),
        "e_coef": normal_values(streams_of[5], (2, H, N), 0.05, 0.75, ((1, 4),), jnp.float32),
        "c_coef": normal_values(streams_of[6], (2, H, N), 0.06, 0.875, ((1, 4),), jnp.float32),
        "skip_gain": jnp.clip(1.0 + 0.1 * jax.random.normal(streams_of[7], (H,), jnp.float32), 0.5, 1.5),
        "decay_rate": jnp.clip(jnp.exp(math.log(0.05) - 5.5451774 * jax.random.uniform(streams_of[8], (H, N), jnp.float32) ** block_scale(streams_of[8], (H, N), ((0, 4),), -0.2, 0.2)), 0.0001953125, 0.05),
        "rotation": jnp.clip(jax.random.uniform(streams_of[9], (H, N), jnp.float32, -3.140625, 3.140625), -3.140625, 3.140625),
        "w_value": normal_values(streams_of[10], (H, H), (H // 4) ** -0.5, 0.5, ((1, 4),)),
        "w_gate": normal_values(streams_of[11], (H, H), H ** -0.5, 0.25, ((1, 4),)),
        "bias_value": normal_values(streams_of[12], (H,), 0.3, 4.0, ((0, 4),), jnp.float32),
        "bias_gate": normal_values(streams_of[13], (H,), 0.3, 4.0, ((0, 4),), jnp.float32),
        "out_cotangent": normal_values(streams_of[14], (MICRO, H, ROWS), 1.0, 6.0, ((1, 4), (2, 8))),
    }


highest = lax.Precision.HIGHEST
epsilon = 1e-05

@jax.custom_vjp
def low(v):
    return lax.optimization_barrier(v.astype(jnp.bfloat16)).astype(jnp.float32)

@jax.custom_vjp
def low_back(v):
    return v

def low_keep(v):
    return (low(v), None)

def low_pass(kept, grad):
    return (grad,)

def back_keep(v):
    return (v, None)

def back_low(kept, grad):
    return (low(grad),)
low.defvjp(low_keep, low_pass)
low_back.defvjp(back_keep, back_low)

def mixer(u_in, v_in, b_coef, e_coef, c_coef, step_re, step_im):
    block_len = math.gcd(SLOT, 64)

    def one_step(carried, inputs):
        u_row, v_row = inputs
        new_re = step_re * carried[0] - step_im * carried[1] + b_coef[0] * u_row[:, None] + e_coef[0] * v_row[:, None]
        new_im = step_re * carried[1] + step_im * carried[0] + b_coef[1] * u_row[:, None] + e_coef[1] * v_row[:, None]
        return ((new_re, new_im), lax.optimization_barrier(jnp.sum(c_coef[0] * new_re - c_coef[1] * new_im, axis=1)))

    def one_block(carried, inputs):
        return lax.scan(one_step, carried, inputs)
    zero_state = jnp.zeros((H, N), jnp.float32)
    shaped = (u_in.reshape(SLOT // block_len, block_len, H), v_in.reshape(SLOT // block_len, block_len, H))
    unused, y_rows = lax.scan(jax.checkpoint(one_block), (zero_state, zero_state), shaped)
    return y_rows.reshape(SLOT, H)

def forward(x_seq, live_rows, weights, step_re, step_im):
    ln_gain, ln_bias, b_coef, e_coef, c_coef, skip_gain, w_value, w_gate, bias_value, bias_gate = weights
    row_mean = lax.optimization_barrier(jnp.mean(x_seq, axis=-1, keepdims=True))
    centered = x_seq - row_mean
    row_var = lax.optimization_barrier(jnp.mean(centered * centered, axis=-1, keepdims=True))
    x_hat = centered * lax.rsqrt(row_var + epsilon)
    u_in = live_rows[:, None] * (x_hat * ln_gain + ln_bias)
    u_prev = jnp.concatenate([jnp.zeros((1, H), jnp.float32), u_in[:-1]], axis=0)
    v_in = u_in * u_prev
    pre_act = mixer(u_in, v_in, b_coef, e_coef, c_coef, step_re, step_im) + skip_gain * u_in
    act_low = low(jax.nn.gelu(pre_act, approximate=False))
    value_pre = low_back(jnp.dot(act_low, w_value, precision=highest, preferred_element_type=jnp.float32) + bias_value)
    gate_pre = low_back(jnp.dot(act_low, w_gate, precision=highest, preferred_element_type=jnp.float32) + bias_gate)
    return live_rows[:, None] * (x_seq + value_pre * jax.nn.sigmoid(gate_pre))

def reference(tokens, lengths, ln_gain, ln_bias, b_coef, e_coef, c_coef, skip_gain, decay_rate, rotation, w_value, w_gate, bias_value, bias_gate, out_cotangent):
    magnitude = jnp.exp(-decay_rate)
    step_re = magnitude * jnp.cos(rotation)
    step_im = magnitude * jnp.sin(rotation)
    params = (ln_gain, ln_bias, b_coef, e_coef, c_coef, skip_gain, w_value.astype(jnp.float32), w_gate.astype(jnp.float32), bias_value, bias_gate)
    seq_tokens = jnp.transpose(tokens.astype(jnp.float32), (0, 2, 1)).reshape(MICRO * SEQS, SLOT, H)
    seq_cots = jnp.transpose(out_cotangent.astype(jnp.float32), (0, 2, 1)).reshape(MICRO * SEQS, SLOT, H)
    seq_lengths = lengths.reshape(MICRO * SEQS)

    def one_sequence(totals, inputs):
        x_seq, cot_seq, length = inputs
        live_rows = (jnp.arange(SLOT, dtype=jnp.int32) < length).astype(jnp.float32)

        def forward_seq(x_in, *weights):
            return forward(x_in, live_rows, weights, step_re, step_im)
        out_seq, pullback = jax.vjp(forward_seq, x_seq, *params)
        gradients = pullback(cot_seq)
        totals = jax.tree.map(jnp.add, totals, tuple(gradients[1:]))
        return (totals, (out_seq.astype(jnp.bfloat16), gradients[0]))
    zero_grads = jax.tree.map(jnp.zeros_like, params)
    totals, (seq_outs, seq_grads) = lax.scan(one_sequence, zero_grads, (seq_tokens, seq_cots, seq_lengths))
    out_all = jnp.transpose(seq_outs.reshape(MICRO, ROWS, H), (0, 2, 1))
    grad_all = jnp.transpose(seq_grads.reshape(MICRO, ROWS, H), (0, 2, 1))
    return (out_all, grad_all, totals[0], totals[1], totals[2], totals[3], totals[4], totals[5], totals[6], totals[7], totals[8], totals[9])
```

```python
import functools
import math

import jax
import jax.numpy as jnp
from jax import lax
from jax.experimental import pallas as pl
from jax.experimental.pallas import tpu as pltpu
from jax.sharding import PartitionSpec as P

f32 = jnp.float32
bf16 = jnp.bfloat16
epsilon = 1e-05
NN = (((1,), (0,)), ((), ()))
NT = (((1,), (1,)), ((), ()))
TN = (((0,), (0,)), ((), ()))


def mm(left, right, dims=NN):
    return lax.dot_general(left, right, dims, preferred_element_type=f32)


def split(x):
    high = x.astype(bf16)
    return high, (x - high.astype(f32)).astype(bf16)


def swap(x, half):
    return pltpu.roll(x, half, axis=x.ndim - 1)


def lanes(shape):
    return lax.broadcasted_iota(jnp.int32, shape, len(shape) - 1)


def pair(z, half):
    low = lanes(z.shape) < half
    turned = swap(z, half)
    return jnp.where(low, z, turned), jnp.where(low, -turned, z)


def cmul(x, z, half):
    return x * z[0] + swap(x, half) * z[1]


def normal_cdf(y):
    return 0.5 * (1.0 + lax.erf(y * (1.0 / math.sqrt(2.0))))


def live_rows(lens_ref, micros, chunks, width):
    shape = (chunks, width)
    at = lax.broadcasted_iota(jnp.int32, shape, 0) * width + lanes(shape)
    rows = [(at < lens_ref[m, 0]).astype(f32) for m in range(micros)]
    return jnp.concatenate(rows, axis=0)


def channel_rows(ref, channel, micros, chunks, chans):
    rows = [
        ref[pl.ds(m * chans + channel, chunks, stride=micros * chans), :] for m in range(micros)
    ]
    return jnp.concatenate(rows, axis=0)


def shift_chunks(x, by, micros, chunks):
    cube = x.reshape(micros, chunks, x.shape[-1])
    place = lax.broadcasted_iota(jnp.int32, cube.shape, 1)
    if by > 0:
        moved = jnp.where(place >= by, pltpu.roll(cube, by, axis=1), 0.0)
    else:
        moved = jnp.where(place < chunks + by, pltpu.roll(cube, chunks + by, axis=1), 0.0)
    return moved.reshape(x.shape)


def previous(u, micros, chunks):
    turned = pltpu.roll(u, 1, axis=1)
    return jnp.where(lanes(u.shape) == 0, shift_chunks(turned, 1, micros, chunks), turned)


def following(u, micros, chunks):
    width = u.shape[1]
    turned = pltpu.roll(u, width - 1, axis=1)
    return jnp.where(
        lanes(u.shape) == width - 1, shift_chunks(turned, -1, micros, chunks), turned
    )


def mode_rows(ref, base, chans, half):
    if len(ref.shape) == 3:
        return jnp.concatenate(
            [ref[0, pl.ds(base, chans), :], ref[1, pl.ds(base, chans), :]], axis=1
        )
    part = ref[pl.ds(base, chans), :]
    return jnp.concatenate([part, part], axis=1)


def forward_kernel(
    micros,
    chunks,
    chans,
    group,
    rank_ref,
    lens_ref,
    gain_ref,
    bias_ref,
    skip_ref,
    b_ref,
    e_ref,
    c_ref,
    decay_ref,
    turn_ref,
    xhat_ref,
    act_ref,
    y_ref,
    uq_ref,
    vq_ref,
    st_ref,
    th_ref,
    tl_ref,
    dh_ref,
    dl_ref,
    ph_ref,
    pl_ref,
    jump_ref,
    rise,
    fall,
    consts,
    jumps,
    act_keep,
):
    width = xhat_ref.shape[1]
    half = decay_ref.shape[1]
    base = rank_ref[0] * chans
    levels = int(math.log2(width)) - 3
    spans = int(math.log2(chunks))

    @pl.when(pl.program_id(0) == 0)
    def _():
        decay = mode_rows(decay_ref, base, chans, half)
        turn = mode_rows(turn_ref, base, chans, half)
        b = mode_rows(b_ref, base, chans, half)
        e = mode_rows(e_ref, base, chans, half)
        c = mode_rows(c_ref, base, chans, half)
        low = lanes(decay.shape) < half
        size = jnp.exp(-decay)
        turned = jnp.where(low, jnp.cos(turn), jnp.sin(turn))
        a = size * turned
        inverse = jnp.exp(decay) * jnp.where(low, turned, -turned)
        a_pair = pair(a, half)
        power = jnp.where(low, 1.0, 0.0)
        fall[pl.ds(7 * chans, chans), :] = power
        power = a
        for k in range(8):
            rise[pl.ds(k * chans, chans), :] = power
            if k < 7:
                fall[pl.ds((6 - k) * chans, chans), :] = power
                power = cmul(power, a_pair, half)
        sign = jnp.where(low, 1.0, -1.0)
        c_pair = pair(c, half)
        ca = cmul(inverse, c_pair, half)
        b_pair = pair(b, half)
        e_pair = pair(e, half)
        consts[0] = b_pair[0]
        consts[1] = b_pair[1]
        consts[2] = e_pair[0]
        consts[3] = e_pair[1]
        consts[4] = c_pair[0]
        consts[5] = c_pair[1]
        consts[6] = cmul(ca, b_pair, half) * sign
        consts[7] = cmul(ca, e_pair, half) * sign
        for k in range(levels):
            power_pair = pair(power, half)
            consts[8 + 2 * k] = power_pair[0]
            consts[9 + 2 * k] = power_pair[1]
            power = cmul(power, power_pair, half)
        for k in range(spans):
            power_pair = pair(power, half)
            jumps[2 * k] = power_pair[0]
            jumps[2 * k + 1] = power_pair[1]
            power = cmul(power, power_pair, half)
        jump_ref[...] = jumps[...]

    live = live_rows(lens_ref, micros, chunks, width)
    rows = micros * chunks
    for g in range(group):
        channel = pl.program_id(0) * group + g

        def const(k):
            return consts[k, pl.ds(channel, 1), :]

        def jump(k):
            return (jumps[2 * k, pl.ds(channel, 1), :], jumps[2 * k + 1, pl.ds(channel, 1), :])

        up = rise[pl.ds(channel, 8, stride=chans), :]
        down = fall[pl.ds(channel, 8, stride=chans), :]
        for k in range(levels):
            step = (const(8 + 2 * k), const(9 + 2 * k))
            up = jnp.concatenate([up, cmul(up, step, half)], axis=0)
            down = jnp.concatenate([cmul(down, step, half), down], axis=0)
        up_hi, up_lo = split(up)
        down_hi, down_lo = split(down)
        ph_ref[g] = up_hi
        pl_ref[g] = up_lo
        dh_ref[g] = down_hi
        dl_ref[g] = down_lo
        row = lax.broadcasted_iota(jnp.int32, (8, width), 0)
        coefs = jnp.where(row == 0, const(6), jnp.where(row == 1, const(7), 0.0))
        coef_hi = coefs.astype(bf16).astype(f32)
        coef_both = jnp.concatenate([coef_hi, coefs - coef_hi], axis=0).astype(bf16)
        taps = mm(coef_both, up_hi, NT) + mm(coef_both, up_lo, NT)
        taps = taps[:8] + taps[8:]
        shape = (width, width)
        ahead = lanes(shape) >= lax.broadcasted_iota(jnp.int32, shape, 0)
        toeplitz = []
        for k in range(2):
            spread = jnp.broadcast_to(taps[k : k + 1], shape)
            spread = pltpu.roll(spread, 0, axis=1, stride=1, stride_axis=0)
            toeplitz.append(jnp.where(ahead, spread, 0.0))
        t_hi, t_lo = split(jnp.concatenate(toeplitz, axis=0))
        th_ref[g] = t_hi
        tl_ref[g] = t_lo

        at = base + channel
        x_hat = channel_rows(xhat_ref, channel, micros, chunks, chans)
        u = live * (x_hat * gain_ref[at] + bias_ref[at])
        v = u * previous(u, micros, chunks)
        uv_hi, uv_lo = split(jnp.concatenate([u, v], axis=0))
        q = mm(jnp.concatenate([uv_hi, uv_lo], axis=0), down_hi)
        q = q[: 2 * rows] + q[2 * rows :] + mm(uv_hi, down_lo)
        uq, vq = q[:rows], q[rows:]
        uq_ref[g] = uq
        vq_ref[g] = vq
        wide_hi = jnp.concatenate([uv_hi[:rows], uv_hi[rows:]], axis=1)
        wide_lo = jnp.concatenate([uv_lo[:rows], uv_lo[rows:]], axis=1)
        y = mm(jnp.concatenate([wide_hi, wide_lo], axis=0), t_hi)
        y = y[:rows] + y[rows:] + mm(wide_hi, t_lo)
        state = cmul(uq, (const(0), const(1)), half) + cmul(vq, (const(2), const(3)), half)
        for k in range(spans):
            state = state + cmul(shift_chunks(state, 2**k, micros, chunks), jump(k), half)
        start = shift_chunks(state, 1, micros, chunks)
        st_ref[g] = start
        sent = cmul(start, (const(4), const(5)), half)
        sent = jnp.where(lanes(sent.shape) < half, sent, -sent)
        sent_hi, sent_lo = split(sent)
        cross = mm(jnp.concatenate([sent_hi, sent_lo], axis=0), up_hi, NT)
        y = y + cross[:rows] + cross[rows:] + mm(sent_hi, up_lo, NT) + skip_ref[at] * u
        y_ref[g] = y
        act = y * normal_cdf(y)
        for m in range(micros):
            act_keep[pl.ds(m * chunks * chans + channel, chunks, stride=chans), :] = act[
                m * chunks : (m + 1) * chunks
            ]

    @pl.when(pl.program_id(0) == pl.num_programs(0) - 1)
    def _():
        act_ref[...] = act_keep[...].astype(bf16)


def backward_kernel(
    micros,
    chunks,
    chans,
    group,
    rank_ref,
    lens_ref,
    gain_ref,
    bias_ref,
    skip_ref,
    b_ref,
    e_ref,
    c_ref,
    xhat_ref,
    dact_ref,
    y_ref,
    uq_ref,
    vq_ref,
    st_ref,
    th_ref,
    tl_ref,
    dh_ref,
    dl_ref,
    ph_ref,
    pl_ref,
    jump_ref,
    dh_out,
    gb_ref,
    ge_ref,
    gc_ref,
    gs_ref,
    gg_ref,
    gn_ref,
    consts,
):
    width = xhat_ref.shape[1]
    half = b_ref.shape[2]
    base = rank_ref[0] * chans
    spans = int(math.log2(chunks))

    @pl.when(pl.program_id(0) == 0)
    def _():
        for k, ref in enumerate((b_ref, e_ref, c_ref)):
            both = pair(mode_rows(ref, base, chans, half), half)
            consts[2 * k] = both[0]
            consts[2 * k + 1] = both[1]

    live = live_rows(lens_ref, micros, chunks, width)
    rows = micros * chunks
    shape = (width, width)
    sub = lax.broadcasted_iota(jnp.int32, shape, 0)
    mirror = (lanes(shape) + sub == width - 1).astype(f32).astype(bf16)
    ahead = lanes(shape) >= sub
    for g in range(group):
        channel = pl.program_id(0) * group + g

        def const(k):
            return (consts[2 * k, pl.ds(channel, 1), :], consts[2 * k + 1, pl.ds(channel, 1), :])

        def jump(k):
            return (
                jump_ref[2 * k, pl.ds(channel, 1), :],
                jump_ref[2 * k + 1, pl.ds(channel, 1), :],
            )

        at = base + channel
        gain = gain_ref[at]
        x_hat = channel_rows(xhat_ref, channel, micros, chunks, chans)
        u = live * (x_hat * gain + bias_ref[at])
        u_prev = previous(u, micros, chunks)
        v = u * u_prev
        y = y_ref[g]
        d_act = dact_ref[pl.ds(channel, rows, stride=chans), :]
        density = jnp.exp(-0.5 * y * y) * (1.0 / math.sqrt(2.0 * math.pi))
        d_y = d_act * (normal_cdf(y) + y * density)
        dy_hi, dy_lo = split(d_y)
        dy_both = jnp.concatenate([dy_hi, dy_lo], axis=0)
        up_hi = ph_ref[g]
        down_hi = dh_ref[g]
        down_lo = dl_ref[g]
        t_hi = th_ref[g]
        t_lo = tl_ref[g]
        first = mm(dy_both, jnp.concatenate([up_hi, mirror], axis=1))
        yd = first[:rows, :width] + first[rows:, :width] + mm(dy_hi, pl_ref[g])
        back_hi = first[:rows, width:].astype(bf16)
        back_lo = first[rows:, width:].astype(bf16)
        duv = mm(dy_both, t_hi, NT)
        duv = duv[:rows] + duv[rows:] + mm(dy_hi, t_lo, NT)
        d_u, d_v = duv[:, :width], duv[:, width:]

        wide_hi, wide_lo = split(jnp.concatenate([u, v], axis=1))
        outer = mm(
            jnp.concatenate([back_hi, back_lo, back_hi], axis=0),
            jnp.concatenate([wide_hi, wide_hi, wide_lo], axis=0),
            TN,
        )
        sums = []
        for k in range(2):
            turned = pltpu.roll(
                outer[:, k * width : (k + 1) * width], 0, axis=1, stride=1, stride_axis=0
            )
            sums.append(jnp.sum(jnp.where(ahead, turned, 0.0), axis=0, keepdims=True))
        row = lax.broadcasted_iota(jnp.int32, (8, width), 0)
        lags = jnp.where(row == 0, sums[0], jnp.where(row == 1, sums[1], 0.0))
        lag_hi = lags.astype(bf16).astype(f32)
        lag_both = jnp.concatenate([lag_hi, lags - lag_hi], axis=0).astype(bf16)
        tops = mm(lag_both, down_hi) + mm(lag_both, down_lo)
        tops = tops[:8] + tops[8:]
        top_u, top_v = tops[0:1], tops[1:2]

        adj = cmul(yd, const(2), half)
        for k in range(spans):
            adj = adj + cmul(shift_chunks(adj, -(2**k), micros, chunks), jump(k), half)
        adj = shift_chunks(adj, -1, micros, chunks)
        sent = jnp.concatenate([cmul(adj, const(0), half), cmul(adj, const(1), half)], axis=0)
        sent = jnp.where(lanes(sent.shape) < half, sent, -sent)
        sent_hi, sent_lo = split(sent)
        cross = mm(jnp.concatenate([sent_hi, sent_lo], axis=0), down_hi, NT)
        cross = cross[: 2 * rows] + cross[2 * rows :] + mm(sent_hi, down_lo, NT)
        d_v = d_v + cross[rows:]
        d_u = d_u + cross[:rows] + skip_ref[at] * d_y + d_v * u_prev
        d_u = d_u + following(d_v * u, micros, chunks)

        def total(x):
            return jnp.sum(x, axis=0, keepdims=True)

        adj_pair = pair(adj, half)
        flip = jnp.where(lanes((1, width)) < half, 1.0, -1.0)
        gb_ref[pl.ds(channel, 1), :] = flip * (
            cmul(top_u, const(2), half) + total(cmul(uq_ref[g], adj_pair, half))
        )
        ge_ref[pl.ds(channel, 1), :] = flip * (
            cmul(top_v, const(2), half) + total(cmul(vq_ref[g], adj_pair, half))
        )
        gc_ref[pl.ds(channel, 1), :] = flip * (
            cmul(top_u, const(0), half)
            + cmul(top_v, const(1), half)
            + total(cmul(st_ref[g], pair(yd, half), half))
        )
        gs_ref[pl.ds(channel, 1), :] = total(d_y * u)
        d_q = live * d_u
        gg_ref[pl.ds(channel, 1), :] = total(d_q * x_hat)
        gn_ref[pl.ds(channel, 1), :] = total(d_q)
        d_h = d_q * gain
        for m in range(micros):
            dh_out[pl.ds(m * chans + channel, chunks, stride=micros * chans), :] = d_h[
                m * chunks : (m + 1) * chunks
            ]


def project_kernel(
    width,
    place_ref,
    lens_ref,
    act_ref,
    xc_ref,
    wv_ref,
    wg_ref,
    bias_ref,
    out_ref,
    dact_ref,
):
    peers, _, chans, rows = xc_ref.shape
    full = peers * chans
    x = xc_ref[:, 0].reshape(full, rows).astype(f32)
    cot = xc_ref[:, 1].reshape(full, rows).astype(f32)
    start = place_ref[1] * rows
    at = place_ref[0] * width + lax.rem(start, width) + lanes((1, rows))
    live = (at < lens_ref[start // width, 0]).astype(f32)
    act = act_ref[...]
    wv = wv_ref[...]
    wg = wg_ref[...]
    value = mm(wv, act, TN) + bias_ref[:, 0:1]
    gate = jax.nn.sigmoid(mm(wg, act, TN) + bias_ref[:, 1:2])
    g = live * cot
    d_value = (g * gate).astype(bf16)
    d_gate = (g * value * gate * (1.0 - gate)).astype(bf16)
    out = (live * (x + value * gate)).astype(bf16)
    out_ref[:, 0] = out.reshape(peers, chans, rows)
    out_ref[:, 1] = d_value.reshape(peers, chans, rows)
    out_ref[:, 2] = d_gate.reshape(peers, chans, rows)
    dact_ref[...] = mm(wv, d_value) + mm(wg, d_gate)


def smem():
    return pl.BlockSpec(memory_space=pltpu.SMEM)


def whole(shape):
    return pl.BlockSpec(shape, lambda i: (0,) * len(shape))


def piece(shape):
    return pl.BlockSpec(shape, lambda i: (i,) + (0,) * (len(shape) - 1))


def shards(
    tokens,
    lengths,
    ln_gain,
    ln_bias,
    b_coef,
    e_coef,
    c_coef,
    skip_gain,
    decay_rate,
    rotation,
    w_value,
    w_gate,
    bias_value,
    bias_gate,
    out_cotangent,
):
    micros, wide, width = tokens.shape
    modes = decay_rate.shape[1]
    full = w_value.shape[0]
    seqs = lax.axis_size("seq")
    peers = lax.axis_size("chan")
    seq_rank = lax.axis_index("seq").astype(jnp.int32)
    chan_rank = lax.axis_index("chan").astype(jnp.int32)
    chans = wide // seqs
    rows = micros * seqs
    own = micros * width // peers
    parts = width // own
    both = ("chan", "seq")
    group = min(4, chans)
    steps = chans // group

    def to_own(x):
        return x.reshape(micros, -1, parts, own).transpose(0, 2, 1, 3).reshape(peers, -1, own)

    def from_own(x):
        return x.reshape(micros, parts, -1, own).transpose(0, 2, 1, 3).reshape(micros, -1, width)

    xc = jnp.stack([to_own(tokens), to_own(out_cotangent)], axis=1)
    xc = lax.all_to_all(xc, "chan", 0, 0, tiled=True)
    weights = lax.all_gather(jnp.stack([w_value, w_gate]), "chan", axis=2, tiled=True)

    x_full = tokens.astype(f32)
    part_mean = jnp.mean(x_full, axis=1)
    part_square = jnp.sum(jnp.square(x_full - part_mean[:, None, :]), axis=1)
    biases = jnp.stack([bias_value, bias_gate])
    stats = lax.all_gather(
        jnp.concatenate([part_mean, part_square, jnp.pad(biases, ((0, 0), (0, width - wide)))]),
        "chan",
    )
    means = stats[:, :micros]
    row_mean = jnp.mean(means, axis=0)
    row_var = (
        jnp.sum(stats[:, micros : 2 * micros], axis=0)
        + wide * jnp.sum(jnp.square(means - row_mean), axis=0)
    ) / full
    inv_std = lax.rsqrt(row_var + epsilon)
    x_hat = (x_full - row_mean[:, None, :]) * inv_std[:, None, :]
    bias_cols = stats[:, 2 * micros :, :wide].transpose(0, 2, 1).reshape(full, 2)

    x_mine = lax.all_to_all(
        x_hat.reshape(micros, seqs, chans, width).transpose(1, 0, 2, 3),
        "seq",
        0,
        0,
        tiled=True,
    ).reshape(seqs * micros * chans, width)

    rank = seq_rank.reshape(1)
    levels = int(math.log2(width)) - 3
    spans = int(math.log2(seqs))
    lane = 2 * modes
    kept = [
        jax.ShapeDtypeStruct((chans, rows, width), f32),
        jax.ShapeDtypeStruct((chans, rows, lane), f32),
        jax.ShapeDtypeStruct((chans, rows, lane), f32),
        jax.ShapeDtypeStruct((chans, rows, lane), f32),
        jax.ShapeDtypeStruct((chans, 2 * width, width), bf16),
        jax.ShapeDtypeStruct((chans, 2 * width, width), bf16),
        jax.ShapeDtypeStruct((chans, width, lane), bf16),
        jax.ShapeDtypeStruct((chans, width, lane), bf16),
        jax.ShapeDtypeStruct((chans, width, lane), bf16),
        jax.ShapeDtypeStruct((chans, width, lane), bf16),
    ]
    kept_specs = [piece((group,) + k.shape[1:]) for k in kept]
    jump_shape = (2 * spans, chans, lane)
    limits = pltpu.CompilerParams(vmem_limit_bytes=48 * 1024 * 1024)
    act, *saved = pl.pallas_call(
        functools.partial(forward_kernel, micros, seqs, chans, group),
        grid=(steps,),
        in_specs=[smem()] * 5
        + [whole(b_coef.shape)] * 3
        + [whole(decay_rate.shape)] * 2
        + [whole(x_mine.shape)],
        out_specs=[whole((rows * chans, width))] + kept_specs + [whole(jump_shape)],
        out_shape=[jax.ShapeDtypeStruct((rows * chans, width), bf16)]
        + kept
        + [jax.ShapeDtypeStruct(jump_shape, f32)],
        scratch_shapes=[
            pltpu.VMEM((8 * chans, lane), f32),
            pltpu.VMEM((8 * chans, lane), f32),
            pltpu.VMEM((8 + 2 * levels, chans, lane), f32),
            pltpu.VMEM(jump_shape, f32),
            pltpu.VMEM((rows * chans, width), f32),
        ],
        compiler_params=limits,
        name="mixer_forward",
    )(
        rank,
        lengths,
        ln_gain,
        ln_bias,
        skip_gain,
        b_coef,
        e_coef,
        c_coef,
        decay_rate,
        rotation,
        x_mine,
    )

    act = (
        act.reshape(micros, seqs, chans, parts, own)
        .transpose(0, 3, 1, 2, 4)
        .reshape(peers * seqs, chans, own)
    )
    act = lax.all_to_all(act, both, 0, 0, tiled=True).reshape(full, own)
    place = jnp.stack([seq_rank, chan_rank])
    sent, d_act = pl.pallas_call(
        functools.partial(project_kernel, width),
        in_specs=[smem()] * 2 + [pl.BlockSpec(memory_space=pltpu.VMEM)] * 5,
        out_specs=[pl.BlockSpec(memory_space=pltpu.VMEM)] * 2,
        out_shape=[
            jax.ShapeDtypeStruct((peers, 3, wide, own), bf16),
            jax.ShapeDtypeStruct((full, own), f32),
        ],
        compiler_params=limits,
        name="project",
    )(place, lengths, act, xc, weights[0], weights[1], bias_cols)

    d_act = lax.all_to_all(
        d_act.reshape(peers * seqs, chans, own), both, 0, 0, tiled=True
    )
    d_act = (
        d_act.reshape(micros, parts, seqs, chans, own)
        .transpose(0, 2, 3, 1, 4)
        .reshape(rows * chans, width)
    )
    small = jax.ShapeDtypeStruct((chans, lane), f32)
    d_hat_mine, *grads = pl.pallas_call(
        functools.partial(backward_kernel, micros, seqs, chans, group),
        grid=(steps,),
        in_specs=[smem()] * 5
        + [whole(b_coef.shape)] * 3
        + [whole(x_mine.shape)] * 2
        + kept_specs
        + [whole(jump_shape)],
        out_specs=[whole(x_mine.shape)] + [whole(small.shape)] * 6,
        out_shape=[jax.ShapeDtypeStruct(x_mine.shape, f32)] + [small] * 6,
        scratch_shapes=[pltpu.VMEM((6, chans, lane), f32)],
        compiler_params=limits,
        name="mixer_backward",
    )(
        rank,
        lengths,
        ln_gain,
        ln_bias,
        skip_gain,
        b_coef,
        e_coef,
        c_coef,
        x_mine,
        d_act,
        *saved,
    )

    sent = lax.all_to_all(sent, "chan", 0, 0, tiled=True)
    out = from_own(sent[:, 0])
    act_all = lax.all_gather(act, "chan")
    d_both = sent[:, 1:].reshape(peers, 2 * wide, own)
    grad_w = jnp.einsum("pkr,pdr->kd", act_all, d_both, preferred_element_type=f32)
    grad_bias = jnp.sum(sent[:, 1:].astype(f32), axis=(0, 3)).reshape(1, 2, wide)
    grad_w = grad_w.reshape(seqs, full // seqs, 2, wide).transpose(0, 2, 1, 3)

    sums = jnp.stack([jnp.sum(g, axis=1) for g in grads[3:]])
    shared = jnp.concatenate(
        [
            jnp.stack(grads[:3]).reshape(-1),
            sums.reshape(-1),
            grad_bias.reshape(-1),
        ]
    )
    pad = -shared.shape[0] % width
    shared = jnp.pad(shared, (0, pad)).reshape(1, -1, width)
    tail = jnp.concatenate(
        [
            d_hat_mine.reshape(seqs, micros * chans, width),
            jnp.broadcast_to(shared, (seqs,) + shared.shape[1:]),
            grad_w.reshape(seqs, -1, width),
        ],
        axis=1,
    )
    tail = lax.all_to_all(tail, "seq", 0, 0, tiled=True)
    cut = micros * chans
    d_hat = (
        tail[:, :cut]
        .reshape(seqs, micros, chans, width)
        .transpose(1, 0, 2, 3)
        .reshape(micros, wide, width)
    )
    last = cut + shared.shape[1]
    got = tail[:, cut:last].reshape(seqs, -1)
    modes_end = 3 * chans * lane
    got_modes = (
        got[:, :modes_end]
        .reshape(seqs, 3, chans, 2, modes)
        .transpose(1, 3, 0, 2, 4)
        .reshape(3, 2, wide, modes)
    )
    got_sums = (
        got[:, modes_end : modes_end + 3 * chans]
        .reshape(seqs, 3, chans)
        .transpose(1, 0, 2)
        .reshape(3, wide)
    )
    bias_at = modes_end + 3 * chans
    got_bias = jnp.sum(got[:, bias_at : bias_at + 2 * wide].reshape(seqs, 2, wide), axis=0)
    got_w = jnp.sum(tail[:, last:], axis=0).reshape(2, full // seqs, wide)

    own_sums = lax.all_gather(
        jnp.concatenate([jnp.sum(d_hat, axis=1), jnp.sum(d_hat * x_hat, axis=1)]), "chan"
    )
    hat_sums = jnp.sum(own_sums, axis=0) / full
    positions = seq_rank * width + jnp.arange(width, dtype=jnp.int32)
    live = (positions[None, :] < lengths).astype(f32)
    d_input = live[:, None, :] * out_cotangent.astype(f32) + inv_std[:, None, :] * (
        d_hat - hat_sums[:micros, None, :] - x_hat * hat_sums[micros:, None, :]
    )
    return (
        out,
        d_input,
        got_sums[1],
        got_sums[2],
        got_modes[0],
        got_modes[1],
        got_modes[2],
        got_sums[0],
        got_w[0],
        got_w[1],
        got_bias[0],
        got_bias[1],
    )


def solution(mesh):
    chan = P("chan")
    modes = P(None, "chan", None)
    table = P("chan", None)
    weight = P(None, "chan")
    rows = P(None, "chan", "seq")
    spread = P("seq", "chan")
    return jax.shard_map(
        shards,
        mesh=mesh,
        in_specs=(
            rows,
            P(),
            chan,
            chan,
            modes,
            modes,
            modes,
            chan,
            table,
            table,
            weight,
            weight,
            chan,
            chan,
            rows,
        ),
        out_specs=(
            rows,
            rows,
            chan,
            chan,
            modes,
            modes,
            modes,
            chan,
            spread,
            spread,
            chan,
            chan,
        ),
        check_vma=False,
    )
```

```python
import functools
import math

import jax
import jax.numpy as jnp
from jax import lax
from jax.experimental import pallas as pl
from jax.experimental.pallas import tpu as pltpu
from jax.sharding import PartitionSpec as P

f32 = jnp.float32
bf16 = jnp.bfloat16
epsilon = 1e-05
NN = (((1,), (0,)), ((), ()))
NT = (((1,), (1,)), ((), ()))
TN = (((0,), (0,)), ((), ()))


def mm(left, right, dims=NN):
    return lax.dot_general(left, right, dims, preferred_element_type=f32)


def split(x):
    high = x.astype(bf16)
    return high, (x - high.astype(f32)).astype(bf16)


def swap(x, half):
    return pltpu.roll(x, half, axis=x.ndim - 1)


def lanes(shape):
    return lax.broadcasted_iota(jnp.int32, shape, len(shape) - 1)


def pair(z, half):
    low = lanes(z.shape) < half
    turned = swap(z, half)
    return jnp.where(low, z, turned), jnp.where(low, -turned, z)


def cmul(x, z, half):
    return x * z[0] + swap(x, half) * z[1]


def normal_cdf(y):
    return 0.5 * (1.0 + lax.erf(y * (1.0 / math.sqrt(2.0))))


def live_rows(lens_ref, micros, chunks, width):
    shape = (chunks, width)
    at = lax.broadcasted_iota(jnp.int32, shape, 0) * width + lanes(shape)
    rows = [(at < lens_ref[m, 0]).astype(f32) for m in range(micros)]
    return jnp.concatenate(rows, axis=0)


def channel_rows(ref, channel, micros, chunks, chans):
    rows = [
        ref[pl.ds(m * chans + channel, chunks, stride=micros * chans), :] for m in range(micros)
    ]
    return jnp.concatenate(rows, axis=0)


def shift_chunks(x, by, micros, chunks):
    cube = x.reshape(micros, chunks, x.shape[-1])
    place = lax.broadcasted_iota(jnp.int32, cube.shape, 1)
    if by > 0:
        moved = jnp.where(place >= by, pltpu.roll(cube, by, axis=1), 0.0)
    else:
        moved = jnp.where(place < chunks + by, pltpu.roll(cube, chunks + by, axis=1), 0.0)
    return moved.reshape(x.shape)


def previous(u, micros, chunks):
    turned = pltpu.roll(u, 1, axis=1)
    return jnp.where(lanes(u.shape) == 0, shift_chunks(turned, 1, micros, chunks), turned)


def following(u, micros, chunks):
    width = u.shape[1]
    turned = pltpu.roll(u, width - 1, axis=1)
    return jnp.where(
        lanes(u.shape) == width - 1, shift_chunks(turned, -1, micros, chunks), turned
    )


def gather_kernel(rank_ref, cot_ref, wv_ref, wg_ref, bv_ref, bg_ref, *outs):
    peers, wide, _ = cot_ref.shape
    full = wv_ref.shape[0]
    pieces = []
    for value in (bv_ref[...], bg_ref[...]):
        for _ in range(3):
            high = value.astype(bf16).astype(f32)
            pieces.append(high)
            value = value - high
    pieces.append(jnp.zeros((10, wide), f32))
    biases = jnp.concatenate(pieces, axis=0).astype(bf16)
    for k, out in enumerate(outs):
        out[pl.ds(0, wide), :] = cot_ref[rank_ref[0] ^ k]
        out[pl.ds(wide, full), :] = wv_ref[...]
        out[pl.ds(wide + full, full), :] = wg_ref[...]
        out[pl.ds(wide + 2 * full, 16), :] = biases


def stats_kernel(tokens_ref, out_ref):
    micros, wide, width = tokens_ref.shape
    x = tokens_ref[...].astype(f32)
    mean = jnp.sum(x, axis=1) * (1.0 / wide)
    out_ref[pl.ds(0, micros), :] = mean
    out_ref[pl.ds(micros, micros), :] = jnp.sum(jnp.square(x - mean[:, None, :]), axis=1)


def normal_kernel(seqs, tokens_ref, stats_ref, xhat_ref, norm_ref):
    micros, wide, width = tokens_ref.shape
    peers = stats_ref.shape[0]
    chans = wide // seqs
    means = stats_ref[:, :micros]
    mean = jnp.sum(means, axis=0) * (1.0 / peers)
    square = jnp.sum(stats_ref[:, micros:], axis=0)
    square = square + wide * jnp.sum(jnp.square(means - mean[None]), axis=0)
    inverse = lax.rsqrt(square * (1.0 / (peers * wide)) + epsilon)
    norm_ref[pl.ds(0, micros), :] = mean
    norm_ref[pl.ds(micros, micros), :] = inverse
    for m in range(micros):
        x = tokens_ref[m].astype(f32)
        x_hat = (x - mean[m : m + 1]) * inverse[m : m + 1]
        xhat_ref[:, m] = x_hat.reshape(seqs, chans, width)


def table_kernel(
    chans,
    seqs,
    width,
    rank_ref,
    b_ref,
    e_ref,
    c_ref,
    decay_ref,
    turn_ref,
    tab_ref,
    const_ref,
    turned_keep,
    rise,
    fall,
    steps,
):
    half = decay_ref.shape[0]
    base = rank_ref[0] * chans
    levels = int(math.log2(width)) - 3
    spans = int(math.log2(seqs))
    group = tab_ref.shape[0]

    def own(value):
        turned_keep[...] = value.T
        return turned_keep[pl.ds(base, chans), :]

    @pl.when(pl.program_id(0) == 0)
    def _():
        b = own(b_ref[...].reshape(2 * half, -1))
        e = own(e_ref[...].reshape(2 * half, -1))
        c = own(c_ref[...].reshape(2 * half, -1))
        mixed = own(jnp.concatenate([decay_ref[...], turn_ref[...]], axis=0))
        low = lanes(mixed.shape) < half
        other = swap(mixed, half)
        decay = jnp.where(low, mixed, other)
        turn = jnp.where(low, other, mixed)
        turned = jnp.where(low, jnp.cos(turn), jnp.sin(turn))
        a = jnp.exp(-decay) * turned
        inverse = jnp.exp(decay) * jnp.where(low, turned, -turned)
        a_pair = pair(a, half)
        fall[pl.ds(7 * chans, chans), :] = jnp.where(low, 1.0, 0.0)
        power = a
        for k in range(8):
            rise[pl.ds(k * chans, chans), :] = power
            if k < 7:
                fall[pl.ds((6 - k) * chans, chans), :] = power
                power = cmul(power, a_pair, half)
        sign = jnp.where(low, 1.0, -1.0)
        pairs = [pair(z, half) for z in (b, e, c)]
        for k in range(3):
            const_ref[2 * k] = pairs[k][0]
            const_ref[2 * k + 1] = pairs[k][1]
        ca = cmul(inverse, pairs[2], half)
        steps[0] = cmul(ca, pairs[0], half) * sign
        steps[1] = cmul(ca, pairs[1], half) * sign
        for k in range(levels):
            power_pair = pair(power, half)
            steps[2 + 2 * k] = power_pair[0]
            steps[3 + 2 * k] = power_pair[1]
            power = cmul(power, power_pair, half)
        for k in range(spans):
            power_pair = pair(power, half)
            const_ref[6 + 2 * k] = power_pair[0]
            const_ref[7 + 2 * k] = power_pair[1]
            power = cmul(power, power_pair, half)

    for g in range(group):
        channel = pl.program_id(0) * group + g

        def step(k):
            return steps[k, pl.ds(channel, 1), :]

        up = rise[pl.ds(channel, 8, stride=chans), :]
        down = fall[pl.ds(channel, 8, stride=chans), :]
        for k in range(levels):
            by = (step(2 + 2 * k), step(3 + 2 * k))
            up = jnp.concatenate([up, cmul(up, by, half)], axis=0)
            down = jnp.concatenate([cmul(down, by, half), down], axis=0)
        up_hi, up_lo = split(up)
        down_hi, down_lo = split(down)
        row = lax.broadcasted_iota(jnp.int32, (8, width), 0)
        coefs = jnp.where(row == 0, step(0), jnp.where(row == 1, step(1), 0.0))
        coef_hi = coefs.astype(bf16).astype(f32)
        coef_both = jnp.concatenate([coef_hi, coefs - coef_hi], axis=0).astype(bf16)
        taps = mm(coef_both, up_hi, NT) + mm(coef_both, up_lo, NT)
        taps = taps[:8] + taps[8:]
        shape = (width, width)
        ahead = lanes(shape) >= lax.broadcasted_iota(jnp.int32, shape, 0)
        for k in range(2):
            spread = jnp.broadcast_to(taps[k : k + 1], shape)
            spread = pltpu.roll(spread, 0, axis=1, stride=1, stride_axis=0)
            t_hi, t_lo = split(jnp.where(ahead, spread, 0.0))
            tab_ref[g, pl.ds(k * width, width), :] = t_hi
            tab_ref[g, pl.ds((2 + k) * width, width), :] = t_lo
        for k, value in enumerate((down_hi, down_lo, up_hi, up_lo)):
            tab_ref[g, pl.ds((4 + k) * width, width), :] = value


def forward_kernel(
    micros,
    chunks,
    chans,
    group,
    rank_ref,
    lens_ref,
    gain_ref,
    bias_ref,
    skip_ref,
    xhat_ref,
    tab_ref,
    const_ref,
    act_ref,
    kept_ref,
    act_keep,
):
    width = xhat_ref.shape[1]
    half = const_ref.shape[2] // 2
    base = rank_ref[0] * chans
    spans = int(math.log2(chunks))
    live = live_rows(lens_ref, micros, chunks, width)
    rows = micros * chunks
    for g in range(group):
        channel = pl.program_id(0) * group + g

        def const(k):
            return (
                const_ref[2 * k, pl.ds(channel, 1), :],
                const_ref[2 * k + 1, pl.ds(channel, 1), :],
            )

        t_hi = tab_ref[g, : 2 * width]
        t_lo = tab_ref[g, 2 * width : 4 * width]
        down_hi, down_lo, up_hi, up_lo = [
            tab_ref[g, k * width : (k + 1) * width] for k in range(4, 8)
        ]
        at = base + channel
        x_hat = channel_rows(xhat_ref, channel, micros, chunks, chans)
        u = live * (x_hat * gain_ref[at] + bias_ref[at])
        v = u * previous(u, micros, chunks)
        uv_hi, uv_lo = split(jnp.concatenate([u, v], axis=0))
        q = mm(jnp.concatenate([uv_hi, uv_lo], axis=0), down_hi)
        q = q[: 2 * rows] + q[2 * rows :] + mm(uv_hi, down_lo)
        uq, vq = q[:rows], q[rows:]
        wide_hi = jnp.concatenate([uv_hi[:rows], uv_hi[rows:]], axis=1)
        wide_lo = jnp.concatenate([uv_lo[:rows], uv_lo[rows:]], axis=1)
        y = mm(jnp.concatenate([wide_hi, wide_lo], axis=0), t_hi)
        y = y[:rows] + y[rows:] + mm(wide_hi, t_lo)
        state = cmul(uq, const(0), half) + cmul(vq, const(1), half)
        for k in range(spans):
            state = state + cmul(shift_chunks(state, 2**k, micros, chunks), const(3 + k), half)
        start = shift_chunks(state, 1, micros, chunks)
        sent = cmul(start, const(2), half)
        sent = jnp.where(lanes(sent.shape) < half, sent, -sent)
        sent_hi, sent_lo = split(sent)
        cross = mm(jnp.concatenate([sent_hi, sent_lo], axis=0), up_hi, NT)
        y = y + cross[:rows] + cross[rows:] + mm(sent_hi, up_lo, NT) + skip_ref[at] * u
        for k, value in enumerate((y, uq, vq, start)):
            kept_ref[g, pl.ds(k * rows, rows), :] = value
        act = y * normal_cdf(y)
        for m in range(micros):
            act_keep[pl.ds(m * chunks * chans + channel, chunks, stride=chans), :] = act[
                m * chunks : (m + 1) * chunks
            ]

    @pl.when(pl.program_id(0) == pl.num_programs(0) - 1)
    def _():
        act_ref[...] = act_keep[...].astype(bf16)


def backward_kernel(
    micros,
    chunks,
    chans,
    group,
    rank_ref,
    lens_ref,
    gain_ref,
    bias_ref,
    skip_ref,
    xhat_ref,
    dact_ref,
    tab_ref,
    const_ref,
    kept_ref,
    weights_ref,
    out_ref,
    sums_keep,
    modes_keep,
    head,
):
    width = xhat_ref.shape[1]
    half = const_ref.shape[2] // 2
    base = rank_ref[0] * chans
    spans = int(math.log2(chunks))
    live = live_rows(lens_ref, micros, chunks, width)
    rows = micros * chunks
    stride = head.shape[0] // chunks
    shape = (width, width)
    sub = lax.broadcasted_iota(jnp.int32, shape, 0)
    mirror = (lanes(shape) + sub == width - 1).astype(f32).astype(bf16)
    ahead = lanes(shape) >= sub
    for g in range(group):
        channel = pl.program_id(0) * group + g

        def const(k):
            return (
                const_ref[2 * k, pl.ds(channel, 1), :],
                const_ref[2 * k + 1, pl.ds(channel, 1), :],
            )

        t_hi = tab_ref[g, : 2 * width]
        t_lo = tab_ref[g, 2 * width : 4 * width]
        down_hi, down_lo, up_hi, up_lo = [
            tab_ref[g, k * width : (k + 1) * width] for k in range(4, 8)
        ]
        y, uq, vq, start = [kept_ref[g, pl.ds(k * rows, rows), :] for k in range(4)]
        at = base + channel
        gain = gain_ref[at]
        x_hat = channel_rows(xhat_ref, channel, micros, chunks, chans)
        u = live * (x_hat * gain + bias_ref[at])
        u_prev = previous(u, micros, chunks)
        v = u * u_prev
        d_act = dact_ref[pl.ds(channel, rows, stride=chans), :]
        density = jnp.exp(-0.5 * y * y) * (1.0 / math.sqrt(2.0 * math.pi))
        d_y = d_act * (normal_cdf(y) + y * density)
        dy_hi, dy_lo = split(d_y)
        dy_both = jnp.concatenate([dy_hi, dy_lo], axis=0)
        first = mm(dy_both, jnp.concatenate([up_hi, mirror], axis=1))
        yd = first[:rows, :width] + first[rows:, :width] + mm(dy_hi, up_lo)
        back_hi = first[:rows, width:].astype(bf16)
        back_lo = first[rows:, width:].astype(bf16)
        duv = mm(dy_both, t_hi, NT)
        duv = duv[:rows] + duv[rows:] + mm(dy_hi, t_lo, NT)
        d_u, d_v = duv[:, :width], duv[:, width:]

        wide_hi, wide_lo = split(jnp.concatenate([u, v], axis=1))
        outer = mm(
            jnp.concatenate([back_hi, back_lo, back_hi], axis=0),
            jnp.concatenate([wide_hi, wide_hi, wide_lo], axis=0),
            TN,
        )
        sums = []
        for k in range(2):
            turned = pltpu.roll(
                outer[:, k * width : (k + 1) * width], 0, axis=1, stride=1, stride_axis=0
            )
            sums.append(jnp.sum(jnp.where(ahead, turned, 0.0), axis=0, keepdims=True))
        row = lax.broadcasted_iota(jnp.int32, (8, width), 0)
        lags = jnp.where(row == 0, sums[0], jnp.where(row == 1, sums[1], 0.0))
        lag_hi = lags.astype(bf16).astype(f32)
        lag_both = jnp.concatenate([lag_hi, lags - lag_hi], axis=0).astype(bf16)
        tops = mm(lag_both, down_hi) + mm(lag_both, down_lo)
        tops = tops[:8] + tops[8:]
        top_u, top_v = tops[0:1], tops[1:2]

        adj = cmul(yd, const(2), half)
        for k in range(spans):
            adj = adj + cmul(shift_chunks(adj, -(2**k), micros, chunks), const(3 + k), half)
        adj = shift_chunks(adj, -1, micros, chunks)
        sent = jnp.concatenate([cmul(adj, const(0), half), cmul(adj, const(1), half)], axis=0)
        sent = jnp.where(lanes(sent.shape) < half, sent, -sent)
        sent_hi, sent_lo = split(sent)
        cross = mm(jnp.concatenate([sent_hi, sent_lo], axis=0), down_hi, NT)
        cross = cross[: 2 * rows] + cross[2 * rows :] + mm(sent_hi, down_lo, NT)
        d_v = d_v + cross[rows:]
        d_u = d_u + cross[:rows] + skip_ref[at] * d_y + d_v * u_prev
        d_u = d_u + following(d_v * u, micros, chunks)

        def total(x):
            return jnp.sum(x, axis=0, keepdims=True)

        adj_pair = pair(adj, half)
        flip = jnp.where(lanes((1, 2 * half)) < half, 1.0, -1.0)
        modes_keep[pl.ds(channel, 1), :] = flip * (
            cmul(top_u, const(2), half) + total(cmul(uq, adj_pair, half))
        )
        modes_keep[pl.ds(chans + channel, 1), :] = flip * (
            cmul(top_v, const(2), half) + total(cmul(vq, adj_pair, half))
        )
        modes_keep[pl.ds(2 * chans + channel, 1), :] = flip * (
            cmul(top_u, const(0), half)
            + cmul(top_v, const(1), half)
            + total(cmul(start, pair(yd, half), half))
        )
        d_q = live * d_u
        for k, value in enumerate((d_y * u, d_q * x_hat, d_q)):
            sums_keep[pl.ds(k * chans + channel, 1), :] = total(value)
        d_h = d_q * gain
        for m in range(micros):
            head[pl.ds(m * chans + channel, chunks, stride=stride), :] = d_h[
                m * chunks : (m + 1) * chunks
            ]

    @pl.when(pl.program_id(0) == pl.num_programs(0) - 1)
    def _():
        sums = jnp.sum(sums_keep[...].T, axis=0, keepdims=True)
        modes = modes_keep[...]
        modes_hi = modes.astype(bf16).astype(f32)
        sums_hi = sums.astype(bf16).astype(f32)
        cut = micros * chans
        count, wide = weights_ref.shape[1:]
        bias = weights_ref[chunks, pl.ds(0, 16), :].astype(f32)
        for k in range(chunks):
            at = k * stride + cut
            head[pl.ds(at, 3 * chans), :] = modes_hi
            head[pl.ds(at + 3 * chans, 3 * chans), :] = modes - modes_hi
            head[pl.ds(at + 6 * chans, 1), pl.ds(0, 3 * chans)] = sums_hi
            head[pl.ds(at + 6 * chans + 1, 1), pl.ds(0, 3 * chans)] = sums - sums_hi
            for j in range(4):
                head[pl.ds(at + 6 * chans + 2 + j, 1), pl.ds(0, wide)] = bias[4 * j : 4 * j + 1]
            out_ref[k, pl.ds(0, stride), :] = head[pl.ds(k * stride, stride), :].astype(bf16)
            out_ref[k, pl.ds(stride, count), pl.ds(0, wide)] = weights_ref[k]


def project_kernel(width, place_ref, lens_ref, act_ref, *refs):
    dact_ref = refs[-1]
    full, rows = act_ref.shape
    peers = len(refs) - 1
    wide = full // peers
    start = place_ref[1] * rows
    at = place_ref[0] * width + lax.rem(start, width) + lanes((1, rows))
    live = (at < lens_ref[start // width, 0]).astype(f32)
    act = act_ref[...]
    d_act = None
    for ref in refs[:-1]:
        g = live * ref[pl.ds(0, wide), :].astype(f32)
        wv = ref[pl.ds(wide, full), :]
        wg = ref[pl.ds(wide + full, full), :]
        bias = ref[pl.ds(wide + 2 * full, 16), :].astype(f32).T
        both = mm(jnp.concatenate([wv, wg], axis=1), act, TN)
        value = both[:wide] + (bias[:, 0:1] + bias[:, 1:2] + bias[:, 2:3])
        gate = jax.nn.sigmoid(both[wide:] + (bias[:, 3:4] + bias[:, 4:5] + bias[:, 5:6]))
        d_value = (g * gate).astype(bf16)
        d_gate = (g * value * gate * (1.0 - gate)).astype(bf16)
        part = mm(wv, d_value) + mm(wg, d_gate)
        d_act = part if d_act is None else d_act + part
    dact_ref[...] = d_act


def output_kernel(
    seqs,
    rank_ref,
    lens_ref,
    order_ref,
    tokens_ref,
    cot_ref,
    wv_ref,
    wg_ref,
    bv_ref,
    bg_ref,
    *refs,
):
    acts_in, (out_ref, grad_ref) = refs[:-2], refs[-2:]
    micros, wide, width = tokens_ref.shape
    full = wv_ref.shape[0]
    at = rank_ref[0] * width + lanes((1, width))
    weights = jnp.concatenate([wv_ref[...], wg_ref[...]], axis=1)
    bias = jnp.concatenate([bv_ref[...], bg_ref[...]], axis=1)
    bias = jnp.broadcast_to(bias, (8, 2 * wide)).T[:, 0:1]
    acts, grads = [], []
    for k in range(micros):
        m = order_ref[k]
        live = (at < lens_ref[m, 0]).astype(f32)
        act = acts_in[k][...]
        both = mm(weights, act, TN) + bias
        value = both[:wide]
        gate = jax.nn.sigmoid(both[wide:])
        out_ref[m] = (live * (tokens_ref[m].astype(f32) + value * gate)).astype(bf16)
        g = live * cot_ref[m].astype(f32)
        d_value = (g * gate).astype(bf16)
        d_gate = (g * value * gate * (1.0 - gate)).astype(bf16)
        acts.append(act)
        grads.append(jnp.concatenate([d_value, d_gate], axis=0))
    grads = jnp.concatenate(grads, axis=1)
    grad_w = mm(jnp.concatenate(acts, axis=1), grads, NT)
    ones = jnp.ones((8, grads.shape[1]), bf16)
    grad_b = mm(ones, grads, NT)
    count = full // seqs
    for k in range(seqs):
        part = grad_w[k * count : (k + 1) * count]
        grad_ref[k, pl.ds(0, count), :] = part[:, :wide].astype(bf16)
        grad_ref[k, pl.ds(count, count), :] = part[:, wide:].astype(bf16)
    high, low = split(jnp.concatenate([grad_b[:4, :wide], grad_b[:4, wide:]], axis=0))
    grad_ref[seqs, pl.ds(0, 16), :] = jnp.concatenate([high, low], axis=0)


def normal(tokens_ref, norm_ref, m):
    micros = tokens_ref.shape[0]
    return (tokens_ref[m].astype(f32) - norm_ref[m : m + 1]) * norm_ref[
        micros + m : micros + m + 1
    ]


def sums_kernel(got_ref, tokens_ref, norm_ref, out_ref, head_ref):
    micros, wide, width = tokens_ref.shape
    seqs, stride, _ = head_ref.shape
    chans = wide // seqs
    head_ref[...] = got_ref[:, pl.ds(0, stride), :].astype(f32)
    for m in range(micros):
        d_hat = head_ref[:, pl.ds(m * chans, chans), :].reshape(wide, width)
        x_hat = normal(tokens_ref, norm_ref, m)
        out_ref[pl.ds(m, 1), :] = jnp.sum(d_hat, axis=0, keepdims=True)
        out_ref[pl.ds(micros + m, 1), :] = jnp.sum(d_hat * x_hat, axis=0, keepdims=True)


def final_kernel(
    rank_ref,
    lens_ref,
    got_ref,
    head_ref,
    hat_ref,
    tokens_ref,
    cot_ref,
    norm_ref,
    d_in_ref,
    b_ref,
    e_ref,
    c_ref,
    skip_ref,
    gain_ref,
    norm_bias_ref,
    wv_ref,
    wg_ref,
    bv_ref,
    bg_ref,
):
    micros, wide, width = tokens_ref.shape
    seqs, stride, _ = head_ref.shape
    peers = hat_ref.shape[0]
    chans = wide // seqs
    hat = jnp.sum(hat_ref[...], axis=0) * (1.0 / (peers * wide))
    at = rank_ref[0] * width + lanes((1, width))
    for m in range(micros):
        live = (at < lens_ref[m, 0]).astype(f32)
        d_hat = head_ref[:, pl.ds(m * chans, chans), :].reshape(wide, width)
        x_hat = normal(tokens_ref, norm_ref, m)
        inside = d_hat - hat[m : m + 1] - x_hat * hat[micros + m : micros + m + 1]
        d_in_ref[m] = (
            live * cot_ref[m].astype(f32) + norm_ref[micros + m : micros + m + 1] * inside
        )
    cut = micros * chans
    for k, ref in enumerate((b_ref, e_ref, c_ref)):
        modes = (
            head_ref[:, pl.ds(cut + k * chans, chans), :]
            + head_ref[:, pl.ds(cut + (3 + k) * chans, chans), :]
        )
        ref[...] = modes.reshape(wide, -1).T.reshape(ref.shape)
    place = lanes((1, wide)) // chans
    last = cut + 6 * chans
    for k, ref in enumerate((skip_ref, gain_ref, norm_bias_ref)):
        line = jnp.zeros((1, wide), f32)
        for s in range(seqs):
            own = head_ref[s, pl.ds(last, 1), :] + head_ref[s, pl.ds(last + 1, 1), :]
            own = pltpu.roll(own, (s - k) * chans % own.shape[1], axis=1)[:, :wide]
            line = jnp.where(place == s, own, line)
        ref[...] = line
    count = wv_ref.shape[0]
    for k, ref in enumerate((wv_ref, wg_ref)):
        parts = got_ref[:, pl.ds(stride + k * count, count), pl.ds(0, wide)]
        ref[...] = jnp.sum(parts.astype(f32), axis=0)
    for k, ref in enumerate((bv_ref, bg_ref)):
        line = jnp.zeros((1, wide), f32)
        for s in range(seqs):
            line = line + head_ref[s, pl.ds(last + 2 + k, 1), pl.ds(0, wide)]
            line = line + head_ref[s, pl.ds(last + 4 + k, 1), pl.ds(0, wide)]
        ref[...] = line


def smem():
    return pl.BlockSpec(memory_space=pltpu.SMEM)


def vmem():
    return pl.BlockSpec(memory_space=pltpu.VMEM)


def whole(shape):
    return pl.BlockSpec(shape, lambda i: (0,) * len(shape))


def piece(shape):
    return pl.BlockSpec(shape, lambda i: (i,) + (0,) * (len(shape) - 1))


def shape_of(shape, kind=f32):
    return jax.ShapeDtypeStruct(shape, kind)


def kernel_call(kernel, name, scalars, arrays, outs, micros_of_time, limit=8, **more):
    ins = [smem()] * len(scalars) + [vmem()] * len(arrays)
    return pl.pallas_call(
        kernel,
        in_specs=ins,
        out_specs=[vmem()] * len(outs),
        out_shape=outs,
        compiler_params=pltpu.CompilerParams(vmem_limit_bytes=limit * 1024 * 1024),
        cost_estimate=cost(micros_of_time),
        name=name,
        **more,
    )(*scalars, *arrays)


def cost(micros_of_time):
    return pl.CostEstimate(
        flops=int(micros_of_time * 1e9), bytes_accessed=int(micros_of_time * 3e6), transcendentals=0
    )


def shards(
    tokens,
    lengths,
    ln_gain,
    ln_bias,
    b_coef,
    e_coef,
    c_coef,
    skip_gain,
    decay_rate,
    rotation,
    w_value,
    w_gate,
    bias_value,
    bias_gate,
    out_cotangent,
):
    micros, wide, width = tokens.shape
    modes = decay_rate.shape[1]
    full = w_value.shape[0]
    seqs = lax.axis_size("seq")
    peers = lax.axis_size("chan")
    seq_rank = lax.axis_index("seq").astype(jnp.int32)
    chan_rank = lax.axis_index("chan").astype(jnp.int32)
    chans = wide // seqs
    rows = micros * seqs
    own = micros * width // peers
    parts = width // own
    both = ("chan", "seq")
    group = min(4, chans)
    steps = chans // group
    lane = 2 * modes
    spans = int(math.log2(seqs))
    levels = int(math.log2(width)) - 3
    rank = seq_rank.reshape(1)
    place = jnp.stack([seq_rank, chan_rank])
    bias_rows = (bias_value.reshape(1, wide), bias_gate.reshape(1, wide))

    def exchange(x, axis):
        return lax.all_to_all(x, axis, 0, 0, tiled=True)

    def cross(x, by):
        return lax.ppermute(x, "chan", [(i, i ^ by) for i in range(peers)])

    (part_stats,) = kernel_call(
        stats_kernel, "stats", (), (tokens,), [shape_of((2 * micros, width))], 1
    )
    stats = lax.all_gather(part_stats, "chan")
    x_hat, norm = kernel_call(
        functools.partial(normal_kernel, seqs),
        "normal",
        (),
        (tokens, stats),
        [shape_of((seqs, micros, chans, width)), shape_of((2 * micros, width))],
        1,
    )

    x_mine = exchange(x_hat, "seq").reshape(seqs * micros * chans, width)

    cot, wv, wg, _ = lax.optimization_barrier((out_cotangent, w_value, w_gate, norm))
    cot_own = cot.reshape(micros, wide, parts, own).transpose(0, 2, 1, 3).reshape(peers, wide, own)
    weights = kernel_call(
        gather_kernel,
        "weights",
        (chan_rank.reshape(1),),
        (cot_own, wv, wg) + bias_rows,
        [shape_of((wide + 2 * full + 16, own), bf16)] * peers,
        1,
    )
    weights = [weights[0]] + [cross(weights[k], k) for k in range(1, peers)]

    turned = [jnp.transpose(z, (0, 2, 1)) for z in (b_coef, e_coef, c_coef)]
    tables = shape_of((chans, 8 * width, lane), bf16)
    consts = shape_of((6 + 2 * spans, chans, lane))
    tab, const = pl.pallas_call(
        functools.partial(table_kernel, chans, seqs, width),
        grid=(steps,),
        in_specs=[smem()]
        + [whole(turned[0].shape)] * 3
        + [whole(decay_rate.T.shape)] * 2,
        out_specs=[piece((group,) + tables.shape[1:]), whole(consts.shape)],
        out_shape=[tables, consts],
        scratch_shapes=[
            pltpu.VMEM((wide, lane), f32),
            pltpu.VMEM((8 * chans, lane), f32),
            pltpu.VMEM((8 * chans, lane), f32),
            pltpu.VMEM((2 + 2 * levels, chans, lane), f32),
        ],
        compiler_params=pltpu.CompilerParams(vmem_limit_bytes=12 * 1024 * 1024),
        cost_estimate=cost(4),
        name="tables",
    )(rank, *turned, decay_rate.T, rotation.T)
    tab = pltpu.with_memory_space_constraint(tab, pltpu.HBM)

    kept = shape_of((chans, 4 * rows, lane))
    act, saved = pl.pallas_call(
        functools.partial(forward_kernel, micros, seqs, chans, group),
        grid=(steps,),
        in_specs=[smem()] * 5
        + [whole(x_mine.shape), piece((group,) + tables.shape[1:]), whole(consts.shape)],
        out_specs=[whole((rows * chans, width)), piece((group,) + kept.shape[1:])],
        out_shape=[shape_of((rows * chans, width), bf16), kept],
        scratch_shapes=[pltpu.VMEM((rows * chans, width), f32)],
        compiler_params=pltpu.CompilerParams(vmem_limit_bytes=12 * 1024 * 1024),
        cost_estimate=cost(8),
        name="mixer_forward",
    )(rank, lengths, ln_gain, ln_bias, skip_gain, x_mine, tab, const)

    act = (
        act.reshape(micros, seqs, chans, parts, own)
        .transpose(0, 3, 1, 2, 4)
        .reshape(peers * seqs, chans, own)
    )
    act = exchange(act, both).reshape(full, own)
    (d_act,) = kernel_call(
        functools.partial(project_kernel, width),
        "project",
        (place, lengths),
        (act, *weights),
        [shape_of((full, own))],
        2,
        limit=12,
    )

    act, d_act = lax.optimization_barrier((act, d_act))
    acts = [act] + [cross(act, k) for k in range(1, peers)]
    if parts == 1:
        order = chan_rank ^ jnp.arange(peers, dtype=jnp.int32)
    else:
        stacked = jnp.stack(acts)[chan_rank ^ jnp.arange(peers, dtype=jnp.int32)]
        stacked = stacked.reshape(micros, parts, full, own).transpose(0, 2, 1, 3)
        stacked = stacked.reshape(micros, full, width)
        acts = [stacked[m] for m in range(micros)]
        order = jnp.arange(micros, dtype=jnp.int32)

    d_act = exchange(d_act.reshape(peers * seqs, chans, own), both)
    d_act = (
        d_act.reshape(micros, parts, seqs, chans, own)
        .transpose(0, 2, 3, 1, 4)
        .reshape(rows * chans, width)
    )
    count = full // seqs
    out, grad_w = kernel_call(
        functools.partial(output_kernel, seqs),
        "output",
        (rank, lengths, order),
        (tokens, out_cotangent, w_value, w_gate) + bias_rows + tuple(acts),
        [shape_of(tokens.shape, bf16), shape_of((seqs + 1, 2 * count, wide), bf16)],
        3,
        limit=12,
    )

    stride = -(-((micros + 6) * chans + 6) // 16) * 16
    send = shape_of((seqs, stride + 2 * count, width), bf16)
    d_hat = pl.pallas_call(
        functools.partial(backward_kernel, micros, seqs, chans, group),
        grid=(steps,),
        in_specs=[smem()] * 5
        + [whole(x_mine.shape)] * 2
        + [
            piece((group,) + tables.shape[1:]),
            whole(consts.shape),
            piece((group,) + kept.shape[1:]),
            whole(grad_w.shape),
        ],
        out_specs=whole(send.shape),
        out_shape=send,
        scratch_shapes=[pltpu.VMEM((3 * chans, lane), f32)] * 2
        + [pltpu.VMEM((seqs * stride, width), f32)],
        compiler_params=pltpu.CompilerParams(vmem_limit_bytes=16 * 1024 * 1024),
        cost_estimate=cost(9),
        name="mixer_backward",
    )(rank, lengths, ln_gain, ln_bias, skip_gain, x_mine, d_act, tab, const, saved, grad_w)
    got = exchange(d_hat, "seq")
    own_sums, head = kernel_call(
        sums_kernel,
        "sums",
        (),
        (got, tokens, norm),
        [shape_of((2 * micros, width)), shape_of((seqs, stride, width))],
        1,
    )
    hat_sums = lax.all_gather(own_sums, "chan")
    mode_grad = shape_of((2, modes, wide))
    d_input, d_b, d_e, d_c, d_skip, d_gain, d_bias, d_wv, d_wg, d_bv, d_bg = kernel_call(
        final_kernel,
        "final",
        (rank, lengths),
        (got, head, hat_sums, tokens, out_cotangent, norm),
        [shape_of(tokens.shape)]
        + [mode_grad] * 3
        + [shape_of((1, wide))] * 3
        + [shape_of((count, wide))] * 2
        + [shape_of((1, wide))] * 2,
        2,
    )
    d_b, d_e, d_c = [jnp.transpose(z, (0, 2, 1)) for z in (d_b, d_e, d_c)]
    d_skip, d_gain, d_bias, d_bv, d_bg = [
        z.reshape(wide) for z in (d_skip, d_gain, d_bias, d_bv, d_bg)
    ]
    return (out, d_input, d_gain, d_bias, d_b, d_e, d_c, d_skip, d_wv, d_wg, d_bv, d_bg)


def solution(mesh):
    chan = P("chan")
    modes = P(None, "chan", None)
    table = P("chan", None)
    weight = P(None, "chan")
    rows = P(None, "chan", "seq")
    spread = P("seq", "chan")
    return jax.shard_map(
        shards,
        mesh=mesh,
        in_specs=(
            rows,
            P(),
            chan,
            chan,
            modes,
            modes,
            modes,
            chan,
            table,
            table,
            weight,
            weight,
            chan,
            chan,
            rows,
        ),
        out_specs=(
            rows,
            rows,
            chan,
            chan,
            modes,
            modes,
            modes,
            chan,
            spread,
            spread,
            chan,
            chan,
        ),
        check_vma=False,
    )
```

```python
import functools
import math

import jax
import jax.numpy as jnp
from jax import lax
from jax.experimental import pallas as pl
from jax.experimental.pallas import tpu as pltpu
from jax.sharding import PartitionSpec as P

f32 = jnp.float32
bf16 = jnp.bfloat16
epsilon = 1e-05
NN = (((1,), (0,)), ((), ()))
NT = (((1,), (1,)), ((), ()))
TN = (((0,), (0,)), ((), ()))


def mm(left, right, dims=NN):
    return lax.dot_general(left, right, dims, preferred_element_type=f32)


def split(x):
    high = x.astype(bf16)
    return high, (x - high.astype(f32)).astype(bf16)


def swap(x, half):
    return pltpu.roll(x, half, axis=x.ndim - 1)


def lanes(shape):
    return lax.broadcasted_iota(jnp.int32, shape, len(shape) - 1)


def pair(z, half):
    low = lanes(z.shape) < half
    turned = swap(z, half)
    return jnp.where(low, z, turned), jnp.where(low, -turned, z)


def cmul(x, z, half):
    return x * z[0] + swap(x, half) * z[1]


def normal_cdf(y):
    return 0.5 * (1.0 + lax.erf(y * (1.0 / math.sqrt(2.0))))


def mirror(width):
    shape = (width, width)
    at = lanes(shape) + lax.broadcasted_iota(jnp.int32, shape, 0)
    return (at == width - 1).astype(f32).astype(bf16)


def live_rows(lens_ref, micros, chunks, width):
    shape = (chunks, width)
    at = lax.broadcasted_iota(jnp.int32, shape, 0) * width + (width - 1 - lanes(shape))
    rows = [(at < lens_ref[m]).astype(f32) for m in range(micros)]
    return jnp.concatenate(rows, axis=0)


def merge(means, squares, count):
    parts = len(means)
    mean = sum(means[1:], means[0]) * (1.0 / parts)
    square = sum(squares[1:], squares[0])
    for part in means:
        square = square + count * jnp.square(part - mean)
    return mean, lax.rsqrt(square * (1.0 / (parts * count)) + epsilon)


def fetch(copies):
    for copy in copies:
        copy.start()


def shift_chunks(x, by, micros, chunks):
    cube = x.reshape(micros, chunks, x.shape[-1])
    place = lax.broadcasted_iota(jnp.int32, cube.shape, 1)
    if by > 0:
        moved = jnp.where(place >= by, pltpu.roll(cube, by, axis=1), 0.0)
    else:
        moved = jnp.where(place < chunks + by, pltpu.roll(cube, chunks + by, axis=1), 0.0)
    return moved.reshape(x.shape)


def previous(u, micros, chunks):
    width = u.shape[1]
    turned = pltpu.roll(u, width - 1, axis=1)
    return jnp.where(
        lanes(u.shape) == width - 1, shift_chunks(turned, 1, micros, chunks), turned
    )


def following(u, micros, chunks):
    turned = pltpu.roll(u, 1, axis=1)
    return jnp.where(lanes(u.shape) == 0, shift_chunks(turned, -1, micros, chunks), turned)


def hankel(first, width):
    blocks = []
    for k in range(width // 8):
        by = width - 8 - 8 * k
        blocks.append(pltpu.roll(first, by, axis=1) if by else first)
    table = jnp.concatenate(blocks, axis=0)
    at = lanes(table.shape) + lax.broadcasted_iota(jnp.int32, table.shape, 0)
    return split(jnp.where(at >= width - 1, table, 0.0))


def gather_kernel(rank_ref, bv_ref, bg_ref, cot_hbm, wv_hbm, wg_hbm, *refs):
    outs, sems = refs[:-1], refs[-1]
    peers, wide, _ = cot_hbm.shape
    full = wv_hbm.shape[0]
    copies = []
    for k, out in enumerate(outs):
        for source, start, count in (
            (cot_hbm.at[rank_ref[0] ^ k], 0, wide),
            (wv_hbm, wide, full),
            (wg_hbm, wide + full, full),
        ):
            copies.append(
                pltpu.make_async_copy(
                    source, out.at[pl.ds(start, count), :], sems.at[len(copies)]
                )
            )
    fetch(copies)
    pieces = []
    for value in (bv_ref[...], bg_ref[...]):
        for _ in range(3):
            high = value.astype(bf16).astype(f32)
            pieces.append(high)
            value = value - high
    pieces.append(jnp.zeros((10, wide), f32))
    biases = jnp.concatenate(pieces, axis=0).astype(bf16)
    for out in outs:
        out[pl.ds(wide + 2 * full, 16), :] = biases
    for copy in copies:
        copy.wait()


def pack_kernel(seqs, tokens_hbm, send_ref, stats_ref, tokens, sems):
    micros, wide, width = tokens.shape
    chans = wide // seqs
    copies = [
        pltpu.make_async_copy(tokens_hbm.at[m], tokens.at[m], sems.at[m]) for m in range(micros)
    ]
    fetch(copies)
    turn = mirror(width)
    means, squares = [], []
    for m in range(micros):
        copies[m].wait()
        x = tokens[m].astype(f32)
        mean = jnp.sum(x, axis=0, keepdims=True) * (1.0 / wide)
        means.append(mean)
        squares.append(jnp.sum(jnp.square(x - mean), axis=0, keepdims=True))
        turned = mm(tokens[m], turn).astype(bf16)
        send_ref[:, pl.ds(m * chans, chans), :] = turned.reshape(seqs, chans, width)
    stats = jnp.concatenate(means + squares, axis=0)
    stats_ref[...] = stats
    high = stats.astype(bf16).astype(f32)
    tail = jnp.concatenate([high, stats - high], axis=0).astype(bf16)
    tail = mm(tail, turn).astype(bf16)
    for k in range(seqs):
        send_ref[k, pl.ds(micros * chans, 4 * micros), :] = tail


def table_kernel(
    chans,
    seqs,
    width,
    rank_ref,
    lens_ref,
    skip_ref,
    gain_ref,
    bias_ref,
    b_hbm,
    e_hbm,
    c_hbm,
    decay_hbm,
    turn_hbm,
    const_ref,
    power_ref,
    taps_ref,
    live_ref,
    b_ref,
    e_ref,
    c_ref,
    decay_ref,
    turn_ref,
    turned_keep,
    rise,
    coefs,
    steps,
    sems,
):
    half = decay_ref.shape[0]
    loads = [
        pltpu.make_async_copy(source, target, sems.at[k])
        for k, (source, target) in enumerate(
            (
                (b_hbm, b_ref),
                (e_hbm, e_ref),
                (c_hbm, c_ref),
                (decay_hbm, decay_ref),
                (turn_hbm, turn_ref),
            )
        )
    ]
    fetch(loads)
    for load in loads:
        load.wait()
    base = rank_ref[0] * chans
    levels = int(math.log2(width)) - 3
    spans = int(math.log2(seqs))

    def own(value):
        turned_keep[...] = value.T
        return turned_keep[pl.ds(base, chans), :]

    b = own(b_ref[...].reshape(2 * half, -1))
    e = own(e_ref[...].reshape(2 * half, -1))
    c = own(c_ref[...].reshape(2 * half, -1))
    mixed = own(jnp.concatenate([decay_ref[...], turn_ref[...]], axis=0))
    low = lanes(mixed.shape) < half
    other = swap(mixed, half)
    decay = jnp.where(low, mixed, other)
    turn = jnp.where(low, other, mixed)
    turned = jnp.where(low, jnp.cos(turn), jnp.sin(turn))
    a = jnp.exp(-decay) * turned
    inverse = pair(jnp.exp(decay) * jnp.where(low, turned, -turned), half)
    a_pair = pair(a, half)
    power = jnp.where(low, 1.0, 0.0)
    for k in range(8):
        rise[pl.ds(k * chans, chans), :] = power
        power = cmul(power, a_pair, half) if k else a
    for k in range(levels):
        power_pair = pair(power, half)
        steps[2 * k] = power_pair[0]
        steps[2 * k + 1] = power_pair[1]
        power = cmul(power, power_pair, half)
    kept = [pair(b, half), pair(e, half), pair(cmul(a, pair(c, half), half), half)]
    for k in range(spans):
        kept.append(pair(power, half))
        power = cmul(power, kept[-1], half)
    kept += [pair(c, half), a_pair]
    for k, both in enumerate(kept):
        const_ref[2 * k] = both[0]
        const_ref[2 * k + 1] = both[1]
    sign = jnp.where(low, 1.0, -1.0)
    for j in range(2):
        coef = cmul(c, kept[j], half)
        for k in range(7, -1, -1):
            coefs[pl.ds((8 * j + k) * chans, chans), :] = coef * sign
            coef = cmul(coef, inverse, half)

    live_ref[...] = live_rows(lens_ref, lens_ref.shape[0], seqs, width)
    for channel in range(chans):
        for k, ref in enumerate((gain_ref, bias_ref)):
            const_ref[2 * len(kept) + k, channel : channel + 1, :] = jnp.full(
                (1, 2 * half), ref[base + channel], f32
            )
        up = rise[pl.ds(channel, 8, stride=chans), :]
        for k in range(levels):
            by = (
                steps[2 * k, channel : channel + 1, :],
                steps[2 * k + 1, channel : channel + 1, :],
            )
            up = jnp.concatenate([up, cmul(up, by, half)], axis=0)
        high, low_part = split(up)
        power_ref[channel, pl.ds(0, width), :] = high
        power_ref[channel, pl.ds(width, width), :] = low_part
        coef = coefs[pl.ds(channel, 16, stride=chans), :]
        coef_hi = coef.astype(bf16).astype(f32)
        both = jnp.concatenate([coef_hi, coef - coef_hi], axis=0).astype(bf16)
        taps = mm(both, high, NT) + mm(both, low_part, NT)
        taps = taps[:16] + taps[16:]
        at = lanes(taps.shape) + lax.broadcasted_iota(jnp.int32, taps.shape, 0)
        taps_ref[channel] = taps + jnp.where(at == 7, skip_ref[base + channel], 0.0)


def own_rows(keep, at, stride, micros, chunks):
    return jnp.concatenate(
        [keep[pl.ds(at + m, chunks, stride=stride), :] for m in range(micros)], axis=0
    )


def channel_tokens(keep, channel, stride, micros, chunks, chans):
    return jnp.concatenate(
        [keep[pl.ds(m * chans + channel, chunks, stride=stride), :] for m in range(micros)],
        axis=0,
    )


def forward_kernel(
    micros,
    chunks,
    chans,
    peers,
    got_ref,
    const_ref,
    taps_ref,
    live_ref,
    *refs,
):
    stats_refs, refs = refs[: peers - 1], refs[peers - 1 :]
    power_hbm, refs = refs[0], refs[1:]
    act_ref, norm_ref, y_ref, kept_hbm, act_keep, x_keep, stats_keep = refs[:7]
    parts, wide_parts, sent_parts, kept_ref, power_ref, sem = refs[7:]
    load = pltpu.make_async_copy(power_hbm, power_ref, sem.at[0])
    load.start()
    width = got_ref.shape[2]
    half = const_ref.shape[2] // 2
    spans = int(math.log2(chunks))
    rows = micros * chunks
    stride = got_ref.shape[1]
    flip = jnp.where(lanes((1, 2 * half)) < half, 1.0, -1.0)

    def const(channel, k):
        return (
            const_ref[2 * k, channel : channel + 1, :],
            const_ref[2 * k + 1, channel : channel + 1, :],
        )

    live = live_ref[...]
    gain, bias = 2 * (5 + spans), 2 * (5 + spans) + 1
    for k in range(chunks):
        x_keep[pl.ds(k * stride, stride), :] = got_ref[k].astype(f32)
    means, squares = [], []
    for j in range(peers):
        keep, step, at = x_keep, stride, micros * chans
        if j:
            keep, step, at = stats_keep.at[j - 1], 4 * micros, 0
            for k in range(chunks):
                keep[pl.ds(k * step, step), :] = stats_refs[j - 1][k].astype(f32)
        lines = [own_rows(keep, at + q * micros, step, micros, chunks) for q in range(4)]
        means.append(lines[0] + lines[2])
        squares.append(lines[1] + lines[3])
    mean, inverse = merge(means, squares, chans * chunks)
    norm_ref[pl.ds(0, rows), :] = mean
    norm_ref[pl.ds(rows, rows), :] = inverse

    for channel in range(chans):
        x_hat = channel_tokens(x_keep, channel, stride, micros, chunks, chans) - mean
        line = slice(channel, channel + 1)
        u = live * (x_hat * inverse * const_ref[gain, line] + const_ref[bias, line])
        u_hi, u_lo = split(u)
        v_hi, v_lo = split(u * previous(u, micros, chunks))
        for k, part in enumerate((u_hi, v_hi, u_lo, v_lo)):
            parts[channel, k * rows : (k + 1) * rows] = part
        wide_parts[channel, :rows, :width] = u_hi
        wide_parts[channel, :rows, width:] = v_hi
        wide_parts[channel, rows:, :width] = u_lo
        wide_parts[channel, rows:, width:] = v_lo

    for channel in range(chans):
        tables = [hankel(taps_ref[channel, 8 * k : 8 * k + 8], width) for k in range(2)]
        both = wide_parts[channel]
        y = mm(both, jnp.concatenate([tables[0][0], tables[1][0]], axis=0))
        low_part = mm(both[:rows], jnp.concatenate([tables[0][1], tables[1][1]], axis=0))
        y_ref[channel] = y[:rows] + y[rows:] + low_part

    load.wait()
    for channel in range(chans):
        q = mm(parts[channel], power_ref[channel, :width])
        kept_ref[channel, : 2 * rows] = (
            q[: 2 * rows]
            + q[2 * rows :]
            + mm(parts[channel, : 2 * rows], power_ref[channel, width:])
        )

    for channel in range(chans):
        uq, vq = kept_ref[channel, :rows], kept_ref[channel, rows : 2 * rows]
        state = cmul(uq, const(channel, 0), half) + cmul(vq, const(channel, 1), half)
        for k in range(spans):
            moved = shift_chunks(state, 2**k, micros, chunks)
            state = state + cmul(moved, const(channel, 3 + k), half)
        start = shift_chunks(state, 1, micros, chunks)
        kept_ref[channel, 2 * rows :] = start
        high, low_part = split(cmul(start, const(channel, 2), half) * flip)
        sent_parts[channel, :rows] = high
        sent_parts[channel, rows:] = low_part
    store = pltpu.make_async_copy(kept_ref, kept_hbm, sem.at[1])
    store.start()

    for channel in range(chans):
        both = sent_parts[channel]
        cross = mm(both, power_ref[channel, :width], NT)
        y = y_ref[channel] + cross[:rows] + cross[rows:]
        y = y + mm(both[:rows], power_ref[channel, width:], NT)
        y_ref[channel] = y
        act = y * normal_cdf(y)
        for m in range(micros):
            act_keep[pl.ds(m * chunks * chans + channel, chunks, stride=chans), :] = act[
                m * chunks : (m + 1) * chunks
            ]
    act_ref[...] = act_keep[...].astype(bf16)
    store.wait()


def forward_scratch(micros, chunks, chans, peers, width, lane):
    rows = micros * chunks
    return [
        pltpu.VMEM((rows * chans, width), f32),
        pltpu.VMEM((chunks * micros * (chans + 4), width), f32),
        pltpu.VMEM((peers - 1, 4 * rows, width), f32),
        pltpu.VMEM((chans, 4 * rows, width), bf16),
        pltpu.VMEM((chans, 2 * rows, 2 * width), bf16),
        pltpu.VMEM((chans, 2 * rows, lane), bf16),
        pltpu.VMEM((chans, 3 * rows, lane), f32),
        pltpu.VMEM((chans, 2 * width, lane), bf16),
        pltpu.SemaphoreType.DMA((2,)),
    ]


def backward_kernel(
    micros,
    chunks,
    chans,
    got_ref,
    dact_ref,
    norm_ref,
    const_ref,
    taps_ref,
    live_ref,
    y_ref,
    power_hbm,
    kept_hbm,
    send_ref,
    sums_ref,
    sums_keep,
    head,
    x_keep,
    dact_keep,
    u_keep,
    prev_keep,
    dy_parts,
    uv_parts,
    yd_keep,
    duv_keep,
    lag_keep,
    adj_keep,
    sent_parts,
    dots,
    power_ref,
    kept_ref,
    sems,
):
    loads = [
        pltpu.make_async_copy(power_hbm, power_ref, sems.at[0]),
        pltpu.make_async_copy(kept_hbm, kept_ref, sems.at[1]),
    ]
    fetch(loads)
    width = got_ref.shape[2]
    half = const_ref.shape[2] // 2
    spans = int(math.log2(chunks))
    rows = micros * chunks
    stride = head.shape[0] // chunks
    got_stride = got_ref.shape[1]
    shape = (width, width)
    passed = lanes(shape) <= lax.broadcasted_iota(jnp.int32, shape, 0)
    low = lanes((1, 2 * half)) < half
    flip = jnp.where(low, 1.0, -1.0)
    live = live_ref[...]
    gain, bias = 2 * (5 + spans), 2 * (5 + spans) + 1
    for k in range(chunks):
        x_keep[pl.ds(k * got_stride, got_stride), :] = got_ref[k].astype(f32)
    dact_keep[...] = dact_ref[...].astype(f32)
    mean, inverse = norm_ref[:rows], norm_ref[rows:]

    def x_hat_of(channel):
        x = channel_tokens(x_keep, channel, got_stride, micros, chunks, chans)
        return (x - mean) * inverse

    def const(channel, k):
        return (
            const_ref[2 * k, channel : channel + 1, :],
            const_ref[2 * k + 1, channel : channel + 1, :],
        )

    def total(x):
        return jnp.sum(x, axis=0, keepdims=True)

    for channel in range(chans):
        line = slice(channel, channel + 1)
        u = live * (x_hat_of(channel) * const_ref[gain, line] + const_ref[bias, line])
        u_prev = previous(u, micros, chunks)
        u_keep[channel] = u
        prev_keep[channel] = u_prev
        u_hi, u_lo = split(u)
        v_hi, v_lo = split(u * u_prev)
        for k, (left, right) in enumerate(((u_hi, v_hi), (u_hi, v_hi), (u_lo, v_lo))):
            uv_parts[channel, k * rows : (k + 1) * rows, :width] = left
            uv_parts[channel, k * rows : (k + 1) * rows, width:] = right
        y = y_ref[channel]
        density = jnp.exp(-0.5 * y * y) * (1.0 / math.sqrt(2.0 * math.pi))
        d_y = dact_keep[pl.ds(channel, rows, stride=chans), :] * (normal_cdf(y) + y * density)
        high, low_part = split(d_y)
        dy_parts[channel, :rows] = high
        dy_parts[channel, rows : 2 * rows] = low_part
        dy_parts[channel, 2 * rows :] = high

    for channel in range(chans):
        tables = [hankel(taps_ref[channel, 8 * k : 8 * k + 8], width) for k in range(2)]
        both = dy_parts[channel, : 2 * rows]
        duv = mm(both, jnp.concatenate([tables[0][0], tables[1][0]], axis=1))
        low_part = mm(both[:rows], jnp.concatenate([tables[0][1], tables[1][1]], axis=1))
        duv_keep[channel] = duv[:rows] + duv[rows:] + low_part

    for channel in range(chans):
        outer = mm(dy_parts[channel], uv_parts[channel], TN)
        for k in range(2):
            rolled = pltpu.roll(
                outer[:, k * width : (k + 1) * width], 1, axis=1, stride=1, stride_axis=0
            )
            line = total(jnp.where(passed, rolled, 0.0))
            high = line.astype(bf16).astype(f32)
            lag_keep[channel, k : k + 1, :] = high
            lag_keep[channel, 2 + k : 3 + k, :] = line - high
            if k == 0:
                sums_keep[channel : channel + 1, :] = jnp.where(
                    lanes(line.shape) == 0, line, 0.0
                )

    for load in loads:
        load.wait()
    for channel in range(chans):
        both = dy_parts[channel, : 2 * rows]
        yd = mm(both, power_ref[channel, :width])
        low_part = mm(both[:rows], power_ref[channel, width:])
        yd_keep[channel] = yd[:rows] + yd[rows:] + low_part

    for channel in range(chans):
        adj = cmul(yd_keep[channel], const(channel, 2), half)
        for k in range(spans):
            moved = shift_chunks(adj, -(2**k), micros, chunks)
            adj = adj + cmul(moved, const(channel, 3 + k), half)
        adj = shift_chunks(adj, -1, micros, chunks)
        adj_keep[channel] = adj
        sent = jnp.concatenate(
            [cmul(adj, const(channel, 0), half), cmul(adj, const(channel, 1), half)], axis=0
        )
        high, low_part = split(sent * flip)
        sent_parts[channel, : 2 * rows] = high
        sent_parts[channel, 2 * rows :] = low_part

    for channel in range(chans):
        both = sent_parts[channel]
        cross = mm(both, power_ref[channel, :width], NT)
        cross = cross[: 2 * rows] + cross[2 * rows :]
        cross = cross + mm(both[: 2 * rows], power_ref[channel, width:], NT)
        d_v = duv_keep[channel, :, width:] + cross[rows:]
        d_u = duv_keep[channel, :, :width] + cross[:rows] + d_v * prev_keep[channel]
        d_u = d_u + following(d_v * u_keep[channel], micros, chunks)
        d_q = live * d_u
        sums_keep[chans + channel : chans + channel + 1, :] = total(d_q * x_hat_of(channel))
        sums_keep[2 * chans + channel : 2 * chans + channel + 1, :] = total(d_q)
        d_h = d_q * const_ref[gain, channel : channel + 1]
        for m in range(micros):
            head[pl.ds(m * chans + channel, chunks, stride=stride), :] = d_h[
                m * chunks : (m + 1) * chunks
            ]

    lag_keep[:, 4:, :] = jnp.zeros((chans, 12, width), f32)
    for channel in range(chans):
        lags = lag_keep[channel].astype(bf16)
        tops = mm(lags, power_ref[channel, :width]) + mm(lags, power_ref[channel, width:])
        dots[6, channel : channel + 1, :] = tops[0:1] + tops[2:3]
        dots[7, channel : channel + 1, :] = tops[1:2] + tops[3:4]
        adj, yd = adj_keep[channel], yd_keep[channel]
        adj_swap = swap(adj, half)
        uq, vq, start = [kept_ref[channel, k * rows : (k + 1) * rows] for k in range(3)]
        pairs = ((uq, adj), (uq, adj_swap), (vq, adj), (vq, adj_swap), (start, yd))
        for k, (left, right) in enumerate(pairs + ((start, swap(yd, half)),)):
            dots[k, channel : channel + 1, :] = total(left * right)

    def whole_const(k):
        return const_ref[2 * k], const_ref[2 * k + 1]

    def dot(k):
        same, other = dots[k], dots[k + 1]
        return jnp.where(low, same - swap(same, half), other + swap(other, half))

    top_u, top_v = dots[6], dots[7]
    c = whole_const(3 + spans)
    modes = jnp.concatenate(
        [
            flip * (cmul(top_u, c, half) + dot(0)),
            flip * (cmul(top_v, c, half) + dot(2)),
            flip
            * (
                cmul(top_u, whole_const(0), half)
                + cmul(top_v, whole_const(1), half)
                + cmul(dot(4), whole_const(4 + spans), half)
            ),
        ],
        axis=0,
    )
    sums = jnp.sum(sums_keep[...].T, axis=0, keepdims=True)
    sums_ref[:, pl.ds(0, 3 * chans)] = jnp.broadcast_to(sums, (8, 3 * chans))
    cut = micros * chans
    for k in range(chunks):
        head[pl.ds(k * stride + cut, 3 * chans), :] = modes
        send_ref[k] = head[pl.ds(k * stride, stride), :].astype(bf16)


def backward_scratch(micros, chunks, chans, stride, width, lane):
    rows = micros * chunks
    return [
        pltpu.VMEM((3 * chans, lane), f32),
        pltpu.VMEM((chunks * stride, width), f32),
        pltpu.VMEM((chunks * micros * (chans + 4), width), f32),
        pltpu.VMEM((rows * chans, width), f32),
        pltpu.VMEM((chans, rows, width), f32),
        pltpu.VMEM((chans, rows, width), f32),
        pltpu.VMEM((chans, 3 * rows, width), bf16),
        pltpu.VMEM((chans, 3 * rows, 2 * width), bf16),
        pltpu.VMEM((chans, rows, lane), f32),
        pltpu.VMEM((chans, rows, 2 * width), f32),
        pltpu.VMEM((chans, 16, width), f32),
        pltpu.VMEM((chans, rows, lane), f32),
        pltpu.VMEM((chans, 4 * rows, lane), bf16),
        pltpu.VMEM((8, chans, lane), f32),
        pltpu.VMEM((chans, 2 * width, lane), bf16),
        pltpu.VMEM((chans, 3 * rows, lane), f32),
        pltpu.SemaphoreType.DMA((2,)),
    ]


def gated(both, bias, g):
    wide = g.shape[1]
    value = both[:, :wide] + bias[:, :wide]
    gate = jax.nn.sigmoid(both[:, wide:] + bias[:, wide:])
    d_value = g * gate
    return value * gate, jnp.concatenate(
        [d_value.astype(bf16), (d_value * value * (1.0 - gate)).astype(bf16)], axis=1
    )


def project_kernel(width, place_ref, lens_ref, act_ref, *refs):
    refs, (dact_ref, d_keep) = refs[:-2], refs[-2:]
    full, rows = act_ref.shape
    peers = len(refs)
    wide = full // peers
    start = place_ref[1] * rows
    at = place_ref[0] * width + lax.rem(start, width)
    at = at + lax.broadcasted_iota(jnp.int32, (rows, wide), 0)
    live = (at < lens_ref[start // width]).astype(f32)
    act = act_ref[...].T

    def weight(ref):
        return jnp.concatenate(
            [ref[wide : wide + full, :], ref[wide + full : wide + 2 * full, :]], axis=1
        )

    for k, ref in enumerate(refs):
        g = live * ref[:wide, :].T.astype(f32)
        bias = ref[wide + 2 * full :, :].astype(f32)
        bias = jnp.concatenate(
            [bias[0:1] + bias[1:2] + bias[2:3], bias[3:4] + bias[4:5] + bias[5:6]], axis=1
        )
        d_both = gated(mm(act, weight(ref)), bias, g)[1]
        d_keep[:, 2 * k * wide : 2 * (k + 1) * wide] = d_both
    weights = jnp.concatenate([weight(ref) for ref in refs], axis=1)
    dact_ref[...] = mm(weights, d_keep[...], NT).astype(bf16)


def output_kernel(
    seqs,
    rank_ref,
    lens_ref,
    order_ref,
    tokens_ref,
    cot_ref,
    wv_ref,
    wg_ref,
    bv_ref,
    bg_ref,
    *refs,
):
    micros, wide, width = tokens_ref.shape
    acts_in, refs = refs[:micros], refs[micros:]
    sums_ref, head_ref, out_ref, send_hbm, d_keep, grad, sems = refs
    full = wv_ref.shape[0]
    stride = head_ref.shape[1]
    head = pltpu.make_async_copy(head_ref, send_hbm.at[:, pl.ds(0, stride), :], sems.at[0])
    head.start()
    at = rank_ref[0] * width + lax.broadcasted_iota(jnp.int32, (width, wide), 0)
    place = rank_ref[0] * width + lanes((1, width))
    weights = jnp.concatenate([wv_ref[...], wg_ref[...]], axis=1)
    bias = jnp.concatenate([bv_ref[...], bg_ref[...]], axis=1)
    for k in range(micros):
        m = order_ref[k]
        g = (at < lens_ref[m]).astype(f32) * cot_ref[m].T.astype(f32)
        added, d_both = gated(mm(acts_in[k][...].T, weights), bias, g)
        live = (place < lens_ref[m]).astype(f32)
        out_ref[m] = (live * (tokens_ref[m].astype(f32) + added.T)).astype(bf16)
        d_keep[k * width : (k + 1) * width] = d_both
    d_both = d_keep[...]
    acts = jnp.concatenate([ref[...] for ref in acts_in], axis=1)
    grad_w = mm(acts, d_both).astype(bf16)
    grad_b = mm(jnp.ones((8, micros * width), bf16), d_both)
    count = full // seqs
    for k in range(seqs):
        part = grad_w[k * count : (k + 1) * count]
        grad[k, pl.ds(16, count), pl.ds(0, wide)] = part[:, :wide]
        grad[k, pl.ds(16 + count, count), pl.ds(0, wide)] = part[:, wide:]
    rows = [grad_b[0:1, :wide], grad_b[0:1, wide:]]
    if wide < width:
        blank = jnp.zeros((1, width - wide), f32)
        rows = [jnp.concatenate([row, blank], axis=1) for row in rows]
    small = []
    for row in [sums_ref[0:1]] + rows:
        high = row.astype(bf16).astype(f32)
        small += [high, row - high]
    small = jnp.concatenate(small + [jnp.zeros((10, width), f32)], axis=0).astype(bf16)
    for k in range(seqs):
        grad[k, pl.ds(0, 16), :] = small
    tail = pltpu.make_async_copy(
        grad, send_hbm.at[:, pl.ds(stride, 16 + 2 * count), :], sems.at[1]
    )
    tail.start()
    tail.wait()
    head.wait()


def normal(tokens_ref, norm_ref, m):
    micros = tokens_ref.shape[0]
    return (tokens_ref[m].astype(f32) - norm_ref[m : m + 1]) * norm_ref[
        micros + m : micros + m + 1
    ]


def sums_kernel(got_ref, tokens_ref, *refs):
    stats_refs, (out_ref, head_ref, norm_ref) = refs[:-3], refs[-3:]
    micros, wide, width = tokens_ref.shape
    seqs, stride, _ = head_ref.shape
    chans = wide // seqs
    mean, inverse = merge(
        [ref[pl.ds(0, micros), :] for ref in stats_refs],
        [ref[pl.ds(micros, micros), :] for ref in stats_refs],
        wide,
    )
    norm_ref[pl.ds(0, micros), :] = mean
    norm_ref[pl.ds(micros, micros), :] = inverse
    cut = micros * chans
    turned = got_ref[:, pl.ds(0, cut), :].reshape(seqs * cut, width)
    head_ref[:, pl.ds(0, cut), :] = mm(turned, mirror(width)).reshape(seqs, cut, width)
    head_ref[:, pl.ds(cut, stride - cut), :] = got_ref[:, pl.ds(cut, stride - cut), :].astype(f32)
    for m in range(micros):
        d_hat = head_ref[:, pl.ds(m * chans, chans), :].reshape(wide, width)
        x_hat = normal(tokens_ref, norm_ref, m)
        out_ref[pl.ds(m, 1), :] = jnp.sum(d_hat, axis=0, keepdims=True)
        out_ref[pl.ds(micros + m, 1), :] = jnp.sum(d_hat * x_hat, axis=0, keepdims=True)


def final_kernel(
    rank_ref,
    lens_ref,
    got_ref,
    head_ref,
    tokens_ref,
    cot_ref,
    norm_ref,
    *refs,
):
    hat_refs, refs = refs[:-11], refs[-11:]
    d_in_ref, b_ref, e_ref, c_ref, skip_ref, gain_ref, norm_bias_ref = refs[:7]
    wv_ref, wg_ref, bv_ref, bg_ref = refs[7:]
    micros, wide, width = tokens_ref.shape
    seqs, stride, _ = head_ref.shape
    peers = len(hat_refs)
    chans = wide // seqs
    hats = [ref[...] for ref in hat_refs]
    hat = sum(hats[1:], hats[0]) * (1.0 / (peers * wide))
    at = rank_ref[0] * width + lanes((1, width))
    for m in range(micros):
        live = (at < lens_ref[m]).astype(f32)
        d_hat = head_ref[:, pl.ds(m * chans, chans), :].reshape(wide, width)
        x_hat = normal(tokens_ref, norm_ref, m)
        inside = d_hat - hat[m : m + 1] - x_hat * hat[micros + m : micros + m + 1]
        d_in_ref[m] = (
            live * cot_ref[m].astype(f32) + norm_ref[micros + m : micros + m + 1] * inside
        )
    cut = micros * chans
    for k, ref in enumerate((b_ref, e_ref, c_ref)):
        modes = head_ref[:, pl.ds(cut + k * chans, chans), :]
        ref[...] = modes.reshape(wide, -1).T.reshape(ref.shape)
    place = lanes((1, wide)) // chans
    last = stride - 16
    for k, ref in enumerate((skip_ref, gain_ref, norm_bias_ref)):
        line = jnp.zeros((1, wide), f32)
        for s in range(seqs):
            own = head_ref[s, pl.ds(last, 1), :] + head_ref[s, pl.ds(last + 1, 1), :]
            own = pltpu.roll(own, (s - k) * chans % own.shape[1], axis=1)[:, :wide]
            line = jnp.where(place == s, own, line)
        ref[...] = line
    count = wv_ref.shape[0]
    for k, ref in enumerate((wv_ref, wg_ref)):
        parts = got_ref[:, pl.ds(stride + k * count, count), pl.ds(0, wide)]
        ref[...] = jnp.sum(parts.astype(f32), axis=0)
    for k, ref in enumerate((bv_ref, bg_ref)):
        line = jnp.zeros((1, wide), f32)
        for s in range(seqs):
            line = line + head_ref[s, pl.ds(last + 2 + 2 * k, 1), pl.ds(0, wide)]
            line = line + head_ref[s, pl.ds(last + 3 + 2 * k, 1), pl.ds(0, wide)]
        ref[...] = line


def smem():
    return pl.BlockSpec(memory_space=pltpu.SMEM)


def vmem():
    return pl.BlockSpec(memory_space=pltpu.VMEM)


def in_hbm(x):
    return pltpu.with_memory_space_constraint(x, pltpu.HBM)


def shape_of(shape, kind=f32):
    return jax.ShapeDtypeStruct(shape, kind)


def kernel_call(kernel, name, scalars, arrays, outs, micros_of_time, limit=8, **more):
    ins = [smem()] * len(scalars) + [vmem()] * len(arrays)
    return pl.pallas_call(
        kernel,
        in_specs=ins,
        out_specs=[vmem()] * len(outs),
        out_shape=outs,
        compiler_params=pltpu.CompilerParams(vmem_limit_bytes=limit * 1024 * 1024),
        cost_estimate=cost(micros_of_time),
        name=name,
        **more,
    )(*scalars, *arrays)


def cost(micros_of_time):
    return pl.CostEstimate(
        flops=int(micros_of_time * 1e9), bytes_accessed=int(micros_of_time * 3e6), transcendentals=0
    )


def shards(
    tokens,
    lengths,
    ln_gain,
    ln_bias,
    b_coef,
    e_coef,
    c_coef,
    skip_gain,
    decay_rate,
    rotation,
    w_value,
    w_gate,
    bias_value,
    bias_gate,
    out_cotangent,
):
    micros, wide, width = tokens.shape
    modes = decay_rate.shape[1]
    full = w_value.shape[0]
    seqs = lax.axis_size("seq")
    peers = lax.axis_size("chan")
    seq_rank = lax.axis_index("seq").astype(jnp.int32)
    chan_rank = lax.axis_index("chan").astype(jnp.int32)
    chans = wide // seqs
    rows = micros * seqs
    own = micros * width // peers
    parts = width // own
    both = ("chan", "seq")
    lane = 2 * modes
    spans = int(math.log2(seqs))
    levels = int(math.log2(width)) - 3
    rank = seq_rank.reshape(1)
    lens = lengths.reshape(micros)
    place = jnp.stack([seq_rank, chan_rank])
    bias_rows = (bias_value.reshape(1, wide), bias_gate.reshape(1, wide))

    def exchange(x, axis):
        return lax.all_to_all(x, axis, 0, 0, tiled=True)

    def cross(x, by):
        return lax.ppermute(x, "chan", [(i, i ^ by) for i in range(peers)])

    hbm = pl.BlockSpec(memory_space=pltpu.HBM)
    x_send, part_stats = pl.pallas_call(
        functools.partial(pack_kernel, seqs),
        in_specs=[hbm],
        out_specs=[vmem()] * 2,
        out_shape=[
            shape_of((seqs, micros * (chans + 4), width), bf16),
            shape_of((2 * micros, width)),
        ],
        scratch_shapes=[
            pltpu.VMEM(tokens.shape, bf16),
            pltpu.SemaphoreType.DMA((micros,)),
        ],
        compiler_params=pltpu.CompilerParams(vmem_limit_bytes=8 * 1024 * 1024),
        cost_estimate=cost(1),
        name="pack",
    )(in_hbm(tokens))
    x_mine = exchange(x_send, "seq")
    stats = [part_stats] + [cross(part_stats, k) for k in range(1, peers)]

    cot, wv, wg, _ = lax.optimization_barrier((out_cotangent, w_value, w_gate, part_stats))
    cot_own = cot.reshape(micros, wide, parts, own).transpose(0, 2, 1, 3).reshape(peers, wide, own)
    weights = pl.pallas_call(
        gather_kernel,
        in_specs=[smem()] + [vmem()] * 2 + [hbm] * 3,
        out_specs=[vmem()] * peers,
        out_shape=[shape_of((wide + 2 * full + 16, own), bf16)] * peers,
        scratch_shapes=[pltpu.SemaphoreType.DMA((3 * peers,))],
        compiler_params=pltpu.CompilerParams(vmem_limit_bytes=8 * 1024 * 1024),
        cost_estimate=cost(1),
        name="weights",
    )(chan_rank.reshape(1), *bias_rows, in_hbm(cot_own), in_hbm(wv), in_hbm(wg))

    turned = [jnp.transpose(z, (0, 2, 1)) for z in (b_coef, e_coef, c_coef)]
    const, power, taps, live = pl.pallas_call(
        functools.partial(table_kernel, chans, seqs, width),
        in_specs=[smem()] * 5 + [hbm] * 5,
        out_specs=[vmem()] * 4,
        out_shape=[
            shape_of((12 + 2 * spans, chans, lane)),
            pltpu.HBM((chans, 2 * width, lane), bf16),
            shape_of((chans, 16, width)),
            shape_of((rows, width)),
        ],
        scratch_shapes=[pltpu.VMEM(turned[0].shape, f32)] * 3
        + [pltpu.VMEM((modes, wide), f32)] * 2
        + [
            pltpu.VMEM((wide, lane), f32),
            pltpu.VMEM((8 * chans, lane), f32),
            pltpu.VMEM((16 * chans, lane), f32),
            pltpu.VMEM((2 * levels, chans, lane), f32),
            pltpu.SemaphoreType.DMA((5,)),
        ],
        compiler_params=pltpu.CompilerParams(vmem_limit_bytes=8 * 1024 * 1024),
        cost_estimate=cost(2),
        name="tables",
    )(rank, lens, skip_gain, ln_gain, ln_bias, *[in_hbm(z) for z in (*turned, decay_rate.T, rotation.T)])

    x_mine, const, weights = lax.optimization_barrier((x_mine, const, weights))
    x_stats = x_mine[:, micros * chans :]
    x_stats = [cross(x_stats, k) for k in range(1, peers)]
    weights = [weights[0]] + [cross(weights[k], k) for k in range(1, peers)]
    arrays = (x_mine, const, taps, live, *x_stats, in_hbm(power))
    act, norm_mine, y_mine, kept = pl.pallas_call(
        functools.partial(forward_kernel, micros, seqs, chans, peers),
        in_specs=[vmem()] * (len(arrays) - 1) + [hbm],
        out_specs=[vmem()] * 3 + [hbm],
        out_shape=[
            shape_of((rows * chans, width), bf16),
            shape_of((2 * rows, width)),
            shape_of((chans, rows, width)),
            pltpu.HBM((chans, 3 * rows, lane), f32),
        ],
        scratch_shapes=forward_scratch(micros, seqs, chans, peers, width, lane),
        compiler_params=pltpu.CompilerParams(vmem_limit_bytes=16 * 1024 * 1024),
        cost_estimate=cost(5),
        name="mixer_forward",
    )(*arrays)

    act = (
        act.reshape(micros, seqs, chans, parts, own)
        .transpose(0, 3, 1, 2, 4)
        .reshape(peers * seqs, chans, own)
    )
    act = exchange(act, both).reshape(full, own)
    (d_act,) = kernel_call(
        functools.partial(project_kernel, width),
        "project",
        (place, lens),
        (act, *weights),
        [shape_of((full, own), bf16)],
        2,
        limit=12,
        scratch_shapes=[pltpu.VMEM((own, 2 * full), bf16)],
    )

    act, d_act = lax.optimization_barrier((act, d_act))
    acts = [act] + [cross(act, k) for k in range(1, peers)]
    if parts == 1:
        order = chan_rank ^ jnp.arange(peers, dtype=jnp.int32)
    else:
        stacked = jnp.stack(acts)[chan_rank ^ jnp.arange(peers, dtype=jnp.int32)]
        stacked = stacked.reshape(micros, parts, full, own).transpose(0, 2, 1, 3)
        stacked = stacked.reshape(micros, full, width)
        acts = [stacked[m] for m in range(micros)]
        order = jnp.arange(micros, dtype=jnp.int32)

    d_act = exchange(d_act.reshape(peers * seqs, chans, own), both)
    d_act = (
        d_act.reshape(micros, parts, seqs, chans, own)
        .transpose(0, 2, 3, 1, 4)
        .reshape(rows * chans, width)
    )
    count = full // seqs
    stride = -(-(micros + 3) * chans // 16) * 16
    head = shape_of((seqs, stride, width), bf16)
    arrays = (x_mine, d_act, norm_mine, const, taps, live, y_mine, in_hbm(power), in_hbm(kept))
    head, sums = pl.pallas_call(
        functools.partial(backward_kernel, micros, seqs, chans),
        in_specs=[vmem()] * (len(arrays) - 2) + [hbm] * 2,
        out_specs=[vmem()] * 2,
        out_shape=[head, shape_of((8, width))],
        scratch_shapes=backward_scratch(micros, seqs, chans, stride, width, lane),
        compiler_params=pltpu.CompilerParams(vmem_limit_bytes=20 * 1024 * 1024),
        cost_estimate=cost(5),
        name="mixer_backward",
    )(*arrays)
    arrays = (tokens, out_cotangent, w_value, w_gate) + bias_rows + tuple(acts) + (sums, head)
    send_shape = (seqs, stride + 16 + 2 * count, width)
    out, d_hat = pl.pallas_call(
        functools.partial(output_kernel, seqs),
        in_specs=[smem()] * 3 + [vmem()] * len(arrays),
        out_specs=[vmem(), hbm],
        out_shape=[shape_of(tokens.shape, bf16), pltpu.HBM(send_shape, bf16)],
        scratch_shapes=[
            pltpu.VMEM((micros * width, 2 * wide), bf16),
            pltpu.VMEM((seqs, 16 + 2 * count, width), bf16),
            pltpu.SemaphoreType.DMA((2,)),
        ],
        compiler_params=pltpu.CompilerParams(vmem_limit_bytes=12 * 1024 * 1024),
        cost_estimate=cost(2),
        name="output",
    )(rank, lens, order, *arrays)
    stride += 16
    got = exchange(d_hat, "seq")
    own_sums, head, norm = kernel_call(
        sums_kernel,
        "sums",
        (),
        (got, tokens, *stats),
        [
            shape_of((2 * micros, width)),
            shape_of((seqs, stride, width)),
            shape_of((2 * micros, width)),
        ],
        1,
    )
    hat_sums = [own_sums] + [cross(own_sums, k) for k in range(1, peers)]
    mode_grad = shape_of((2, modes, wide))
    d_input, d_b, d_e, d_c, d_skip, d_gain, d_bias, d_wv, d_wg, d_bv, d_bg = kernel_call(
        final_kernel,
        "final",
        (rank, lens),
        (got, head, tokens, out_cotangent, norm, *hat_sums),
        [shape_of(tokens.shape)]
        + [mode_grad] * 3
        + [shape_of((1, wide))] * 3
        + [shape_of((count, wide))] * 2
        + [shape_of((1, wide))] * 2,
        2,
    )
    d_b, d_e, d_c = [jnp.transpose(z, (0, 2, 1)) for z in (d_b, d_e, d_c)]
    d_skip, d_gain, d_bias, d_bv, d_bg = [
        z.reshape(wide) for z in (d_skip, d_gain, d_bias, d_bv, d_bg)
    ]
    return (out, d_input, d_gain, d_bias, d_b, d_e, d_c, d_skip, d_wv, d_wg, d_bv, d_bg)


def solution(mesh):
    chan = P("chan")
    modes = P(None, "chan", None)
    table = P("chan", None)
    weight = P(None, "chan")
    rows = P(None, "chan", "seq")
    spread = P("seq", "chan")
    return jax.shard_map(
        shards,
        mesh=mesh,
        in_specs=(
            rows,
            P(),
            chan,
            chan,
            modes,
            modes,
            modes,
            chan,
            table,
            table,
            weight,
            weight,
            chan,
            chan,
            rows,
        ),
        out_specs=(
            rows,
            rows,
            chan,
            chan,
            modes,
            modes,
            modes,
            chan,
            spread,
            spread,
            chan,
            chan,
        ),
        check_vma=False,
    )
```

```python
import functools
import math

import jax
import jax.numpy as jnp
from jax import lax
from jax.experimental import pallas as pl
from jax.experimental.pallas import tpu as pltpu
from jax.sharding import PartitionSpec as P

f32 = jnp.float32
bf16 = jnp.bfloat16
epsilon = 1e-05
NN = (((1,), (0,)), ((), ()))
NT = (((1,), (1,)), ((), ()))
TN = (((0,), (0,)), ((), ()))


def mm(left, right, dims=NN):
    return lax.dot_general(left, right, dims, preferred_element_type=f32)


def split(x):
    high = x.astype(bf16)
    return high, (x - high.astype(f32)).astype(bf16)


def swap(x, half):
    return pltpu.roll(x, half, axis=x.ndim - 1)


def lanes(shape):
    return lax.broadcasted_iota(jnp.int32, shape, len(shape) - 1)


def pair(z, half):
    low = lanes(z.shape) < half
    turned = swap(z, half)
    return jnp.where(low, z, turned), jnp.where(low, -turned, z)


def cmul(x, z, half):
    return x * z[0] + swap(x, half) * z[1]


def normal_cdf(y):
    return 0.5 * (1.0 + lax.erf(y * (1.0 / math.sqrt(2.0))))


def mirror(width):
    shape = (width, width)
    at = lanes(shape) + lax.broadcasted_iota(jnp.int32, shape, 0)
    return (at == width - 1).astype(f32).astype(bf16)


def live_rows(lens_ref, micros, chunks, width):
    shape = (chunks, width)
    at = lax.broadcasted_iota(jnp.int32, shape, 0) * width + (width - 1 - lanes(shape))
    rows = [(at < lens_ref[m]).astype(f32) for m in range(micros)]
    return jnp.concatenate(rows, axis=0)


def merge(means, squares, count):
    parts = len(means)
    mean = sum(means[1:], means[0]) * (1.0 / parts)
    square = sum(squares[1:], squares[0])
    for part in means:
        square = square + count * jnp.square(part - mean)
    return mean, lax.rsqrt(square * (1.0 / (parts * count)) + epsilon)


def fetch(copies):
    for copy in copies:
        copy.start()


def shift_chunks(x, by, micros, chunks):
    cube = x.reshape(micros, chunks, x.shape[-1])
    place = lax.broadcasted_iota(jnp.int32, cube.shape, 1)
    if by > 0:
        moved = jnp.where(place >= by, pltpu.roll(cube, by, axis=1), 0.0)
    else:
        moved = jnp.where(place < chunks + by, pltpu.roll(cube, chunks + by, axis=1), 0.0)
    return moved.reshape(x.shape)


def previous(u, micros, chunks):
    width = u.shape[1]
    turned = pltpu.roll(u, width - 1, axis=1)
    return jnp.where(
        lanes(u.shape) == width - 1, shift_chunks(turned, 1, micros, chunks), turned
    )


def following(u, micros, chunks):
    turned = pltpu.roll(u, 1, axis=1)
    return jnp.where(lanes(u.shape) == 0, shift_chunks(turned, -1, micros, chunks), turned)


def hankel(first, width):
    blocks = []
    for k in range(width // 8):
        by = width - 8 - 8 * k
        blocks.append(pltpu.roll(first, by, axis=1) if by else first)
    table = jnp.concatenate(blocks, axis=0)
    at = lanes(table.shape) + lax.broadcasted_iota(jnp.int32, table.shape, 0)
    return split(jnp.where(at >= width - 1, table, 0.0))


def gather_kernel(rank_ref, bv_ref, bg_ref, cot_hbm, wv_hbm, wg_hbm, *refs):
    outs, sems = refs[:-1], refs[-1]
    peers, wide, _ = cot_hbm.shape
    full = wv_hbm.shape[0]
    copies = []
    for k, out in enumerate(outs):
        for source, start, count in (
            (cot_hbm.at[rank_ref[0] ^ k], 0, wide),
            (wv_hbm, wide, full),
            (wg_hbm, wide + full, full),
        ):
            copies.append(
                pltpu.make_async_copy(
                    source, out.at[pl.ds(start, count), :], sems.at[len(copies)]
                )
            )
    fetch(copies)
    pieces = []
    for value in (bv_ref[...], bg_ref[...]):
        for _ in range(3):
            high = value.astype(bf16).astype(f32)
            pieces.append(high)
            value = value - high
    pieces.append(jnp.zeros((10, wide), f32))
    biases = jnp.concatenate(pieces, axis=0).astype(bf16)
    for out in outs:
        out[pl.ds(wide + 2 * full, 16), :] = biases
    for copy in copies:
        copy.wait()


def pack_kernel(seqs, tokens_hbm, send_ref, stats_ref, tokens, sems):
    micros, wide, width = tokens.shape
    chans = wide // seqs
    copies = [
        pltpu.make_async_copy(tokens_hbm.at[m], tokens.at[m], sems.at[m]) for m in range(micros)
    ]
    fetch(copies)
    turn = mirror(width)
    means, squares = [], []
    for m in range(micros):
        copies[m].wait()
        x = tokens[m].astype(f32)
        mean = jnp.sum(x, axis=0, keepdims=True) * (1.0 / wide)
        means.append(mean)
        squares.append(jnp.sum(jnp.square(x - mean), axis=0, keepdims=True))
        turned = mm(tokens[m], turn).astype(bf16)
        send_ref[:, pl.ds(m * chans, chans), :] = turned.reshape(seqs, chans, width)
    stats = jnp.concatenate(means + squares, axis=0)
    stats_ref[...] = stats
    high = stats.astype(bf16).astype(f32)
    tail = jnp.concatenate([high, stats - high], axis=0).astype(bf16)
    tail = mm(tail, turn).astype(bf16)
    for k in range(seqs):
        send_ref[k, pl.ds(micros * chans, 4 * micros), :] = tail


def table_kernel(
    chans,
    seqs,
    width,
    rank_ref,
    lens_ref,
    skip_ref,
    gain_ref,
    bias_ref,
    b_hbm,
    e_hbm,
    c_hbm,
    decay_hbm,
    turn_hbm,
    const_ref,
    power_ref,
    taps_ref,
    live_ref,
    b_ref,
    e_ref,
    c_ref,
    decay_ref,
    turn_ref,
    turned_keep,
    rise,
    coefs,
    steps,
    sems,
):
    half = decay_ref.shape[0]
    loads = [
        pltpu.make_async_copy(source, target, sems.at[k])
        for k, (source, target) in enumerate(
            (
                (b_hbm, b_ref),
                (e_hbm, e_ref),
                (c_hbm, c_ref),
                (decay_hbm, decay_ref),
                (turn_hbm, turn_ref),
            )
        )
    ]
    fetch(loads)
    for load in loads:
        load.wait()
    base = rank_ref[0] * chans
    levels = int(math.log2(width)) - 3
    spans = int(math.log2(seqs))

    def own(value):
        turned_keep[...] = value.T
        return turned_keep[pl.ds(base, chans), :]

    b = own(b_ref[...].reshape(2 * half, -1))
    e = own(e_ref[...].reshape(2 * half, -1))
    c = own(c_ref[...].reshape(2 * half, -1))
    mixed = own(jnp.concatenate([decay_ref[...], turn_ref[...]], axis=0))
    low = lanes(mixed.shape) < half
    other = swap(mixed, half)
    decay = jnp.where(low, mixed, other)
    turn = jnp.where(low, other, mixed)
    turned = jnp.where(low, jnp.cos(turn), jnp.sin(turn))
    a = jnp.exp(-decay) * turned
    inverse = pair(jnp.exp(decay) * jnp.where(low, turned, -turned), half)
    a_pair = pair(a, half)
    power = jnp.where(low, 1.0, 0.0)
    for k in range(8):
        rise[pl.ds(k * chans, chans), :] = power
        power = cmul(power, a_pair, half) if k else a
    for k in range(levels):
        power_pair = pair(power, half)
        steps[2 * k] = power_pair[0]
        steps[2 * k + 1] = power_pair[1]
        power = cmul(power, power_pair, half)
    kept = [pair(b, half), pair(e, half), pair(cmul(a, pair(c, half), half), half)]
    for k in range(spans):
        kept.append(pair(power, half))
        power = cmul(power, kept[-1], half)
    kept += [pair(c, half), a_pair]
    for k, both in enumerate(kept):
        const_ref[2 * k] = both[0]
        const_ref[2 * k + 1] = both[1]
    sign = jnp.where(low, 1.0, -1.0)
    for j in range(2):
        coef = cmul(c, kept[j], half)
        for k in range(7, -1, -1):
            coefs[pl.ds((8 * j + k) * chans, chans), :] = coef * sign
            coef = cmul(coef, inverse, half)

    live_ref[...] = live_rows(lens_ref, lens_ref.shape[0], seqs, width)
    for channel in range(chans):
        for k, ref in enumerate((gain_ref, bias_ref)):
            const_ref[2 * len(kept) + k, channel : channel + 1, :] = jnp.full(
                (1, 2 * half), ref[base + channel], f32
            )
        up = rise[pl.ds(channel, 8, stride=chans), :]
        for k in range(levels):
            by = (
                steps[2 * k, channel : channel + 1, :],
                steps[2 * k + 1, channel : channel + 1, :],
            )
            up = jnp.concatenate([up, cmul(up, by, half)], axis=0)
        high, low_part = split(up)
        power_ref[channel, pl.ds(0, width), :] = high
        power_ref[channel, pl.ds(width, width), :] = low_part
        coef = coefs[pl.ds(channel, 16, stride=chans), :]
        coef_hi = coef.astype(bf16).astype(f32)
        both = jnp.concatenate([coef_hi, coef - coef_hi], axis=0).astype(bf16)
        taps = mm(both, high, NT) + mm(both, low_part, NT)
        taps = taps[:16] + taps[16:]
        at = lanes(taps.shape) + lax.broadcasted_iota(jnp.int32, taps.shape, 0)
        taps_ref[channel] = taps + jnp.where(at == 7, skip_ref[base + channel], 0.0)


def own_rows(keep, at, stride, micros, chunks):
    return jnp.concatenate(
        [keep[pl.ds(at + m, chunks, stride=stride), :] for m in range(micros)], axis=0
    )


def channel_tokens(keep, channel, stride, micros, chunks, chans):
    return jnp.concatenate(
        [keep[pl.ds(m * chans + channel, chunks, stride=stride), :] for m in range(micros)],
        axis=0,
    )


def forward_kernel(
    micros,
    chunks,
    chans,
    peers,
    got_ref,
    const_ref,
    taps_ref,
    live_ref,
    *refs,
):
    stats_refs, refs = refs[: peers - 1], refs[peers - 1 :]
    power_hbm, refs = refs[0], refs[1:]
    act_ref, norm_ref, y_ref, kept_hbm, act_keep, x_keep, stats_keep = refs[:7]
    parts, wide_parts, sent_parts, kept_ref, power_ref, sem = refs[7:]
    load = pltpu.make_async_copy(power_hbm, power_ref, sem.at[0])
    load.start()
    width = got_ref.shape[2]
    half = const_ref.shape[2] // 2
    spans = int(math.log2(chunks))
    rows = micros * chunks
    stride = got_ref.shape[1]
    flip = jnp.where(lanes((1, 2 * half)) < half, 1.0, -1.0)

    def const(channel, k):
        return (
            const_ref[2 * k, channel : channel + 1, :],
            const_ref[2 * k + 1, channel : channel + 1, :],
        )

    live = live_ref[...]
    gain, bias = 2 * (5 + spans), 2 * (5 + spans) + 1
    for k in range(chunks):
        x_keep[pl.ds(k * stride, stride), :] = got_ref[k].astype(f32)
    means, squares = [], []
    for j in range(peers):
        keep, step, at = x_keep, stride, micros * chans
        if j:
            keep, step, at = stats_keep.at[j - 1], 4 * micros, 0
            for k in range(chunks):
                keep[pl.ds(k * step, step), :] = stats_refs[j - 1][k].astype(f32)
        lines = [own_rows(keep, at + q * micros, step, micros, chunks) for q in range(4)]
        means.append(lines[0] + lines[2])
        squares.append(lines[1] + lines[3])
    mean, inverse = merge(means, squares, chans * chunks)
    norm_ref[pl.ds(0, rows), :] = mean
    norm_ref[pl.ds(rows, rows), :] = inverse

    for channel in range(chans):
        x_hat = channel_tokens(x_keep, channel, stride, micros, chunks, chans) - mean
        line = slice(channel, channel + 1)
        u = live * (x_hat * inverse * const_ref[gain, line] + const_ref[bias, line])
        u_hi, u_lo = split(u)
        v_hi, v_lo = split(u * previous(u, micros, chunks))
        for k, part in enumerate((u_hi, v_hi, u_lo, v_lo)):
            parts[channel, k * rows : (k + 1) * rows] = part
        wide_parts[channel, :rows, :width] = u_hi
        wide_parts[channel, :rows, width:] = v_hi
        wide_parts[channel, rows:, :width] = u_lo
        wide_parts[channel, rows:, width:] = v_lo

    for channel in range(chans):
        tables = [hankel(taps_ref[channel, 8 * k : 8 * k + 8], width) for k in range(2)]
        both = wide_parts[channel]
        y = mm(both, jnp.concatenate([tables[0][0], tables[1][0]], axis=0))
        low_part = mm(both[:rows], jnp.concatenate([tables[0][1], tables[1][1]], axis=0))
        y_ref[channel] = y[:rows] + y[rows:] + low_part

    load.wait()
    for channel in range(chans):
        q = mm(parts[channel], power_ref[channel, :width])
        kept_ref[channel, : 2 * rows] = (
            q[: 2 * rows]
            + q[2 * rows :]
            + mm(parts[channel, : 2 * rows], power_ref[channel, width:])
        )

    for channel in range(chans):
        uq, vq = kept_ref[channel, :rows], kept_ref[channel, rows : 2 * rows]
        state = cmul(uq, const(channel, 0), half) + cmul(vq, const(channel, 1), half)
        for k in range(spans):
            moved = shift_chunks(state, 2**k, micros, chunks)
            state = state + cmul(moved, const(channel, 3 + k), half)
        start = shift_chunks(state, 1, micros, chunks)
        kept_ref[channel, 2 * rows :] = start
        high, low_part = split(cmul(start, const(channel, 2), half) * flip)
        sent_parts[channel, :rows] = high
        sent_parts[channel, rows:] = low_part
    store = pltpu.make_async_copy(kept_ref, kept_hbm, sem.at[1])
    store.start()

    for channel in range(chans):
        both = sent_parts[channel]
        cross = mm(both, power_ref[channel, :width], NT)
        y = y_ref[channel] + cross[:rows] + cross[rows:]
        y = y + mm(both[:rows], power_ref[channel, width:], NT)
        y_ref[channel] = y
        act = y * normal_cdf(y)
        for m in range(micros):
            act_keep[pl.ds(m * chunks * chans + channel, chunks, stride=chans), :] = act[
                m * chunks : (m + 1) * chunks
            ]
    act_ref[...] = act_keep[...].astype(bf16)
    store.wait()


def forward_scratch(micros, chunks, chans, peers, width, lane):
    rows = micros * chunks
    return [
        pltpu.VMEM((rows * chans, width), f32),
        pltpu.VMEM((chunks * micros * (chans + 4), width), f32),
        pltpu.VMEM((peers - 1, 4 * rows, width), f32),
        pltpu.VMEM((chans, 4 * rows, width), bf16),
        pltpu.VMEM((chans, 2 * rows, 2 * width), bf16),
        pltpu.VMEM((chans, 2 * rows, lane), bf16),
        pltpu.VMEM((chans, 3 * rows, lane), f32),
        pltpu.VMEM((chans, 2 * width, lane), bf16),
        pltpu.SemaphoreType.DMA((2,)),
    ]


def backward_kernel(
    micros,
    chunks,
    chans,
    got_ref,
    dact_ref,
    norm_ref,
    const_ref,
    taps_ref,
    live_ref,
    y_ref,
    power_hbm,
    kept_hbm,
    send_ref,
    sums_keep,
    head,
    x_keep,
    dact_keep,
    u_keep,
    prev_keep,
    dy_parts,
    uv_parts,
    yd_keep,
    duv_keep,
    lag_keep,
    adj_keep,
    sent_parts,
    dots,
    power_ref,
    kept_ref,
    sems,
):
    loads = [
        pltpu.make_async_copy(power_hbm, power_ref, sems.at[0]),
        pltpu.make_async_copy(kept_hbm, kept_ref, sems.at[1]),
    ]
    fetch(loads)
    width = got_ref.shape[2]
    half = const_ref.shape[2] // 2
    spans = int(math.log2(chunks))
    rows = micros * chunks
    stride = head.shape[0] // chunks
    got_stride = got_ref.shape[1]
    shape = (width, width)
    passed = lanes(shape) <= lax.broadcasted_iota(jnp.int32, shape, 0)
    low = lanes((1, 2 * half)) < half
    flip = jnp.where(low, 1.0, -1.0)
    live = live_ref[...]
    gain, bias = 2 * (5 + spans), 2 * (5 + spans) + 1
    for k in range(chunks):
        x_keep[pl.ds(k * got_stride, got_stride), :] = got_ref[k].astype(f32)
    dact_keep[...] = dact_ref[...].astype(f32)
    mean, inverse = norm_ref[:rows], norm_ref[rows:]

    def x_hat_of(channel):
        x = channel_tokens(x_keep, channel, got_stride, micros, chunks, chans)
        return (x - mean) * inverse

    def const(channel, k):
        return (
            const_ref[2 * k, channel : channel + 1, :],
            const_ref[2 * k + 1, channel : channel + 1, :],
        )

    def total(x):
        return jnp.sum(x, axis=0, keepdims=True)

    for channel in range(chans):
        line = slice(channel, channel + 1)
        u = live * (x_hat_of(channel) * const_ref[gain, line] + const_ref[bias, line])
        u_prev = previous(u, micros, chunks)
        u_keep[channel] = u
        prev_keep[channel] = u_prev
        u_hi, u_lo = split(u)
        v_hi, v_lo = split(u * u_prev)
        for k, (left, right) in enumerate(((u_hi, v_hi), (u_hi, v_hi), (u_lo, v_lo))):
            uv_parts[channel, k * rows : (k + 1) * rows, :width] = left
            uv_parts[channel, k * rows : (k + 1) * rows, width:] = right
        y = y_ref[channel]
        density = jnp.exp(-0.5 * y * y) * (1.0 / math.sqrt(2.0 * math.pi))
        d_y = dact_keep[pl.ds(channel, rows, stride=chans), :] * (normal_cdf(y) + y * density)
        high, low_part = split(d_y)
        dy_parts[channel, :rows] = high
        dy_parts[channel, rows : 2 * rows] = low_part
        dy_parts[channel, 2 * rows :] = high

    for channel in range(chans):
        tables = [hankel(taps_ref[channel, 8 * k : 8 * k + 8], width) for k in range(2)]
        both = dy_parts[channel, : 2 * rows]
        duv = mm(both, jnp.concatenate([tables[0][0], tables[1][0]], axis=1))
        low_part = mm(both[:rows], jnp.concatenate([tables[0][1], tables[1][1]], axis=1))
        duv_keep[channel] = duv[:rows] + duv[rows:] + low_part

    for channel in range(chans):
        outer = mm(dy_parts[channel], uv_parts[channel], TN)
        for k in range(2):
            rolled = pltpu.roll(
                outer[:, k * width : (k + 1) * width], 1, axis=1, stride=1, stride_axis=0
            )
            line = total(jnp.where(passed, rolled, 0.0))
            high = line.astype(bf16).astype(f32)
            lag_keep[channel, k : k + 1, :] = high
            lag_keep[channel, 2 + k : 3 + k, :] = line - high
            if k == 0:
                sums_keep[channel : channel + 1, :] = jnp.where(
                    lanes(line.shape) == 0, line, 0.0
                )

    for load in loads:
        load.wait()
    for channel in range(chans):
        both = dy_parts[channel, : 2 * rows]
        yd = mm(both, power_ref[channel, :width])
        low_part = mm(both[:rows], power_ref[channel, width:])
        yd_keep[channel] = yd[:rows] + yd[rows:] + low_part

    for channel in range(chans):
        adj = cmul(yd_keep[channel], const(channel, 2), half)
        for k in range(spans):
            moved = shift_chunks(adj, -(2**k), micros, chunks)
            adj = adj + cmul(moved, const(channel, 3 + k), half)
        adj = shift_chunks(adj, -1, micros, chunks)
        adj_keep[channel] = adj
        sent = jnp.concatenate(
            [cmul(adj, const(channel, 0), half), cmul(adj, const(channel, 1), half)], axis=0
        )
        high, low_part = split(sent * flip)
        sent_parts[channel, : 2 * rows] = high
        sent_parts[channel, 2 * rows :] = low_part

    for channel in range(chans):
        both = sent_parts[channel]
        cross = mm(both, power_ref[channel, :width], NT)
        cross = cross[: 2 * rows] + cross[2 * rows :]
        cross = cross + mm(both[: 2 * rows], power_ref[channel, width:], NT)
        d_v = duv_keep[channel, :, width:] + cross[rows:]
        d_u = duv_keep[channel, :, :width] + cross[:rows] + d_v * prev_keep[channel]
        d_u = d_u + following(d_v * u_keep[channel], micros, chunks)
        d_q = live * d_u
        sums_keep[chans + channel : chans + channel + 1, :] = total(d_q * x_hat_of(channel))
        sums_keep[2 * chans + channel : 2 * chans + channel + 1, :] = total(d_q)
        d_h = d_q * const_ref[gain, channel : channel + 1]
        for m in range(micros):
            head[pl.ds(m * chans + channel, chunks, stride=stride), :] = d_h[
                m * chunks : (m + 1) * chunks
            ]

    lag_keep[:, 4:, :] = jnp.zeros((chans, 12, width), f32)
    for channel in range(chans):
        lags = lag_keep[channel].astype(bf16)
        tops = mm(lags, power_ref[channel, :width]) + mm(lags, power_ref[channel, width:])
        dots[6, channel : channel + 1, :] = tops[0:1] + tops[2:3]
        dots[7, channel : channel + 1, :] = tops[1:2] + tops[3:4]
        adj, yd = adj_keep[channel], yd_keep[channel]
        adj_swap = swap(adj, half)
        uq, vq, start = [kept_ref[channel, k * rows : (k + 1) * rows] for k in range(3)]
        pairs = ((uq, adj), (uq, adj_swap), (vq, adj), (vq, adj_swap), (start, yd))
        for k, (left, right) in enumerate(pairs + ((start, swap(yd, half)),)):
            dots[k, channel : channel + 1, :] = total(left * right)

    def whole_const(k):
        return const_ref[2 * k], const_ref[2 * k + 1]

    def dot(k):
        same, other = dots[k], dots[k + 1]
        return jnp.where(low, same - swap(same, half), other + swap(other, half))

    top_u, top_v = dots[6], dots[7]
    c = whole_const(3 + spans)
    modes = jnp.concatenate(
        [
            flip * (cmul(top_u, c, half) + dot(0)),
            flip * (cmul(top_v, c, half) + dot(2)),
            flip
            * (
                cmul(top_u, whole_const(0), half)
                + cmul(top_v, whole_const(1), half)
                + cmul(dot(4), whole_const(4 + spans), half)
            ),
        ],
        axis=0,
    )
    sums = jnp.sum(sums_keep[...].T, axis=0, keepdims=True)
    sums_hi = sums.astype(bf16).astype(f32)
    cut = micros * chans
    for k in range(chunks):
        at = k * stride + cut
        head[pl.ds(at, 3 * chans), :] = modes
        head[pl.ds(at + 3 * chans, 1), pl.ds(0, 3 * chans)] = sums_hi
        head[pl.ds(at + 3 * chans + 1, 1), pl.ds(0, 3 * chans)] = sums - sums_hi
        send_ref[k] = head[pl.ds(k * stride, stride), :].astype(bf16)


def backward_scratch(micros, chunks, chans, stride, width, lane):
    rows = micros * chunks
    return [
        pltpu.VMEM((3 * chans, lane), f32),
        pltpu.VMEM((chunks * stride, width), f32),
        pltpu.VMEM((chunks * micros * (chans + 4), width), f32),
        pltpu.VMEM((rows * chans, width), f32),
        pltpu.VMEM((chans, rows, width), f32),
        pltpu.VMEM((chans, rows, width), f32),
        pltpu.VMEM((chans, 3 * rows, width), bf16),
        pltpu.VMEM((chans, 3 * rows, 2 * width), bf16),
        pltpu.VMEM((chans, rows, lane), f32),
        pltpu.VMEM((chans, rows, 2 * width), f32),
        pltpu.VMEM((chans, 16, width), f32),
        pltpu.VMEM((chans, rows, lane), f32),
        pltpu.VMEM((chans, 4 * rows, lane), bf16),
        pltpu.VMEM((8, chans, lane), f32),
        pltpu.VMEM((chans, 2 * width, lane), bf16),
        pltpu.VMEM((chans, 3 * rows, lane), f32),
        pltpu.SemaphoreType.DMA((2,)),
    ]


def gated(both, bias, g):
    wide = g.shape[1]
    value = both[:, :wide] + bias[:, :wide]
    gate = jax.nn.sigmoid(both[:, wide:] + bias[:, wide:])
    d_value = g * gate
    return value * gate, jnp.concatenate(
        [d_value.astype(bf16), (d_value * value * (1.0 - gate)).astype(bf16)], axis=1
    )


def project_kernel(width, place_ref, lens_ref, act_ref, *refs):
    refs, (dact_ref, d_keep) = refs[:-2], refs[-2:]
    full, rows = act_ref.shape
    peers = len(refs)
    wide = full // peers
    start = place_ref[1] * rows
    at = place_ref[0] * width + lax.rem(start, width)
    at = at + lax.broadcasted_iota(jnp.int32, (rows, wide), 0)
    live = (at < lens_ref[start // width]).astype(f32)
    act = act_ref[...].T

    def weight(ref):
        return jnp.concatenate(
            [ref[wide : wide + full, :], ref[wide + full : wide + 2 * full, :]], axis=1
        )

    for k, ref in enumerate(refs):
        g = live * ref[:wide, :].T.astype(f32)
        bias = ref[wide + 2 * full :, :].astype(f32)
        bias = jnp.concatenate(
            [bias[0:1] + bias[1:2] + bias[2:3], bias[3:4] + bias[4:5] + bias[5:6]], axis=1
        )
        d_both = gated(mm(act, weight(ref)), bias, g)[1]
        d_keep[:, 2 * k * wide : 2 * (k + 1) * wide] = d_both
    weights = jnp.concatenate([weight(ref) for ref in refs], axis=1)
    dact_ref[...] = mm(weights, d_keep[...], NT).astype(bf16)


def output_kernel(
    seqs,
    rank_ref,
    lens_ref,
    order_ref,
    tokens_ref,
    cot_ref,
    wv_ref,
    wg_ref,
    bv_ref,
    bg_ref,
    *refs,
):
    micros, wide, width = tokens_ref.shape
    acts_in, refs = refs[:micros], refs[micros:]
    out_ref, keep_ref, send_ref, d_keep, grad = refs
    full = wv_ref.shape[0]
    at = rank_ref[0] * width + lax.broadcasted_iota(jnp.int32, (width, wide), 0)
    place = rank_ref[0] * width + lanes((1, width))
    weights = jnp.concatenate([wv_ref[...], wg_ref[...]], axis=1)
    bias = jnp.concatenate([bv_ref[...], bg_ref[...]], axis=1)
    for k in range(micros):
        m = order_ref[k]
        g = (at < lens_ref[m]).astype(f32) * cot_ref[m].T.astype(f32)
        added, d_both = gated(mm(acts_in[k][...].T, weights), bias, g)
        live = (place < lens_ref[m]).astype(f32)
        out_ref[m] = (live * (tokens_ref[m].astype(f32) + added.T)).astype(bf16)
        d_keep[k * width : (k + 1) * width] = d_both
    d_both = d_keep[...]
    acts = jnp.concatenate([ref[...] for ref in acts_in], axis=1)
    grad_w = mm(acts, d_both)
    grad_b = mm(jnp.ones((8, micros * width), bf16), d_both)
    row = lax.broadcasted_iota(jnp.int32, (8, wide), 0)
    small = jnp.where(row == 0, grad_b[:, :wide], grad_b[:, wide:])
    count = full // seqs
    for k in range(seqs):
        part = grad_w[k * count : (k + 1) * count]
        grad[k, pl.ds(0, count), :] = part[:, :wide]
        grad[k, pl.ds(count, count), :] = part[:, wide:]
        grad[k, pl.ds(2 * count, 8), :] = small
    bit = rank_ref[0] & 1
    for k in range(seqs // 2):
        keep_ref[k] = grad[2 * k + bit]
        send_ref[k] = grad[2 * k + 1 - bit].astype(bf16)


def halve_kernel(bit_ref, left_ref, right_ref, keep_ref, send_ref, total):
    total[...] = left_ref[...] + right_ref[...].astype(f32)
    for k in range(keep_ref.shape[0]):
        keep_ref[k] = total[2 * k + bit_ref[0]]
        send_ref[k] = total[2 * k + 1 - bit_ref[0]].astype(bf16)


def last_kernel(left_ref, right_ref, wv_ref, wg_ref, bv_ref, bg_ref):
    count = wv_ref.shape[0]
    total = left_ref[0] + right_ref[0].astype(f32)
    wv_ref[...] = total[:count]
    wg_ref[...] = total[count : 2 * count]
    bv_ref[...] = total[2 * count : 2 * count + 1]
    bg_ref[...] = total[2 * count + 1 : 2 * count + 2]


def normal(tokens_ref, norm_ref, m):
    micros = tokens_ref.shape[0]
    return (tokens_ref[m].astype(f32) - norm_ref[m : m + 1]) * norm_ref[
        micros + m : micros + m + 1
    ]


def sums_kernel(got_ref, tokens_ref, *refs):
    stats_refs, (out_ref, head_ref, norm_ref) = refs[:-3], refs[-3:]
    micros, wide, width = tokens_ref.shape
    seqs, stride, _ = head_ref.shape
    chans = wide // seqs
    mean, inverse = merge(
        [ref[pl.ds(0, micros), :] for ref in stats_refs],
        [ref[pl.ds(micros, micros), :] for ref in stats_refs],
        wide,
    )
    norm_ref[pl.ds(0, micros), :] = mean
    norm_ref[pl.ds(micros, micros), :] = inverse
    cut = micros * chans
    turned = got_ref[:, pl.ds(0, cut), :].reshape(seqs * cut, width)
    head_ref[:, pl.ds(0, cut), :] = mm(turned, mirror(width)).reshape(seqs, cut, width)
    head_ref[:, pl.ds(cut, stride - cut), :] = got_ref[:, pl.ds(cut, stride - cut), :].astype(f32)
    for m in range(micros):
        d_hat = head_ref[:, pl.ds(m * chans, chans), :].reshape(wide, width)
        x_hat = normal(tokens_ref, norm_ref, m)
        out_ref[pl.ds(m, 1), :] = jnp.sum(d_hat, axis=0, keepdims=True)
        out_ref[pl.ds(micros + m, 1), :] = jnp.sum(d_hat * x_hat, axis=0, keepdims=True)


def final_kernel(
    rank_ref,
    lens_ref,
    head_ref,
    tokens_ref,
    cot_ref,
    norm_ref,
    *refs,
):
    hat_refs, refs = refs[:-7], refs[-7:]
    d_in_ref, b_ref, e_ref, c_ref, skip_ref, gain_ref, norm_bias_ref = refs
    micros, wide, width = tokens_ref.shape
    seqs, stride, _ = head_ref.shape
    peers = len(hat_refs)
    chans = wide // seqs
    hats = [ref[...] for ref in hat_refs]
    hat = sum(hats[1:], hats[0]) * (1.0 / (peers * wide))
    at = rank_ref[0] * width + lanes((1, width))
    for m in range(micros):
        live = (at < lens_ref[m]).astype(f32)
        d_hat = head_ref[:, pl.ds(m * chans, chans), :].reshape(wide, width)
        x_hat = normal(tokens_ref, norm_ref, m)
        inside = d_hat - hat[m : m + 1] - x_hat * hat[micros + m : micros + m + 1]
        d_in_ref[m] = (
            live * cot_ref[m].astype(f32) + norm_ref[micros + m : micros + m + 1] * inside
        )
    cut = micros * chans
    for k, ref in enumerate((b_ref, e_ref, c_ref)):
        modes = head_ref[:, pl.ds(cut + k * chans, chans), :]
        ref[...] = modes.reshape(wide, -1).T.reshape(ref.shape)
    place = lanes((1, wide)) // chans
    last = cut + 3 * chans
    for k, ref in enumerate((skip_ref, gain_ref, norm_bias_ref)):
        line = jnp.zeros((1, wide), f32)
        for s in range(seqs):
            own = head_ref[s, pl.ds(last, 1), :] + head_ref[s, pl.ds(last + 1, 1), :]
            own = pltpu.roll(own, (s - k) * chans % own.shape[1], axis=1)[:, :wide]
            line = jnp.where(place == s, own, line)
        ref[...] = line


def smem():
    return pl.BlockSpec(memory_space=pltpu.SMEM)


def vmem():
    return pl.BlockSpec(memory_space=pltpu.VMEM)


def in_hbm(x):
    return pltpu.with_memory_space_constraint(x, pltpu.HBM)


def shape_of(shape, kind=f32):
    return jax.ShapeDtypeStruct(shape, kind)


def kernel_call(kernel, name, scalars, arrays, outs, micros_of_time, limit=8, **more):
    ins = [smem()] * len(scalars) + [vmem()] * len(arrays)
    return pl.pallas_call(
        kernel,
        in_specs=ins,
        out_specs=[vmem()] * len(outs),
        out_shape=outs,
        compiler_params=pltpu.CompilerParams(vmem_limit_bytes=limit * 1024 * 1024),
        cost_estimate=cost(micros_of_time),
        name=name,
        **more,
    )(*scalars, *arrays)


def cost(micros_of_time):
    return pl.CostEstimate(
        flops=int(micros_of_time * 1e9), bytes_accessed=int(micros_of_time * 3e6), transcendentals=0
    )


def shards(
    tokens,
    lengths,
    ln_gain,
    ln_bias,
    b_coef,
    e_coef,
    c_coef,
    skip_gain,
    decay_rate,
    rotation,
    w_value,
    w_gate,
    bias_value,
    bias_gate,
    out_cotangent,
):
    micros, wide, width = tokens.shape
    modes = decay_rate.shape[1]
    full = w_value.shape[0]
    seqs = lax.axis_size("seq")
    peers = lax.axis_size("chan")
    seq_rank = lax.axis_index("seq").astype(jnp.int32)
    chan_rank = lax.axis_index("chan").astype(jnp.int32)
    chans = wide // seqs
    rows = micros * seqs
    own = micros * width // peers
    parts = width // own
    both = ("chan", "seq")
    lane = 2 * modes
    spans = int(math.log2(seqs))
    levels = int(math.log2(width)) - 3
    rank = seq_rank.reshape(1)
    lens = lengths.reshape(micros)
    place = jnp.stack([seq_rank, chan_rank])
    bias_rows = (bias_value.reshape(1, wide), bias_gate.reshape(1, wide))

    def exchange(x, axis):
        return lax.all_to_all(x, axis, 0, 0, tiled=True)

    def cross(x, by):
        return lax.ppermute(x, "chan", [(i, i ^ by) for i in range(peers)])

    hbm = pl.BlockSpec(memory_space=pltpu.HBM)
    x_send, part_stats = pl.pallas_call(
        functools.partial(pack_kernel, seqs),
        in_specs=[hbm],
        out_specs=[vmem()] * 2,
        out_shape=[
            shape_of((seqs, micros * (chans + 4), width), bf16),
            shape_of((2 * micros, width)),
        ],
        scratch_shapes=[
            pltpu.VMEM(tokens.shape, bf16),
            pltpu.SemaphoreType.DMA((micros,)),
        ],
        compiler_params=pltpu.CompilerParams(vmem_limit_bytes=8 * 1024 * 1024),
        cost_estimate=cost(1),
        name="pack",
    )(in_hbm(tokens))
    x_mine = exchange(x_send, "seq")
    stats = [part_stats] + [cross(part_stats, k) for k in range(1, peers)]

    cot, wv, wg, _ = lax.optimization_barrier((out_cotangent, w_value, w_gate, part_stats))
    cot_own = cot.reshape(micros, wide, parts, own).transpose(0, 2, 1, 3).reshape(peers, wide, own)
    weights = pl.pallas_call(
        gather_kernel,
        in_specs=[smem()] + [vmem()] * 2 + [hbm] * 3,
        out_specs=[vmem()] * peers,
        out_shape=[shape_of((wide + 2 * full + 16, own), bf16)] * peers,
        scratch_shapes=[pltpu.SemaphoreType.DMA((3 * peers,))],
        compiler_params=pltpu.CompilerParams(vmem_limit_bytes=8 * 1024 * 1024),
        cost_estimate=cost(1),
        name="weights",
    )(chan_rank.reshape(1), *bias_rows, in_hbm(cot_own), in_hbm(wv), in_hbm(wg))

    turned = [jnp.transpose(z, (0, 2, 1)) for z in (b_coef, e_coef, c_coef)]
    const, power, taps, live = pl.pallas_call(
        functools.partial(table_kernel, chans, seqs, width),
        in_specs=[smem()] * 5 + [hbm] * 5,
        out_specs=[vmem()] * 4,
        out_shape=[
            shape_of((12 + 2 * spans, chans, lane)),
            pltpu.HBM((chans, 2 * width, lane), bf16),
            shape_of((chans, 16, width)),
            shape_of((rows, width)),
        ],
        scratch_shapes=[pltpu.VMEM(turned[0].shape, f32)] * 3
        + [pltpu.VMEM((modes, wide), f32)] * 2
        + [
            pltpu.VMEM((wide, lane), f32),
            pltpu.VMEM((8 * chans, lane), f32),
            pltpu.VMEM((16 * chans, lane), f32),
            pltpu.VMEM((2 * levels, chans, lane), f32),
            pltpu.SemaphoreType.DMA((5,)),
        ],
        compiler_params=pltpu.CompilerParams(vmem_limit_bytes=8 * 1024 * 1024),
        cost_estimate=cost(2),
        name="tables",
    )(rank, lens, skip_gain, ln_gain, ln_bias, *[in_hbm(z) for z in (*turned, decay_rate.T, rotation.T)])

    x_mine, const, weights = lax.optimization_barrier((x_mine, const, weights))
    x_stats = x_mine[:, micros * chans :]
    x_stats = [cross(x_stats, k) for k in range(1, peers)]
    weights = [weights[0]] + [cross(weights[k], k) for k in range(1, peers)]
    arrays = (x_mine, const, taps, live, *x_stats, in_hbm(power))
    act, norm_mine, y_mine, kept = pl.pallas_call(
        functools.partial(forward_kernel, micros, seqs, chans, peers),
        in_specs=[vmem()] * (len(arrays) - 1) + [hbm],
        out_specs=[vmem()] * 3 + [hbm],
        out_shape=[
            shape_of((rows * chans, width), bf16),
            shape_of((2 * rows, width)),
            shape_of((chans, rows, width)),
            pltpu.HBM((chans, 3 * rows, lane), f32),
        ],
        scratch_shapes=forward_scratch(micros, seqs, chans, peers, width, lane),
        compiler_params=pltpu.CompilerParams(vmem_limit_bytes=16 * 1024 * 1024),
        cost_estimate=cost(5),
        name="mixer_forward",
    )(*arrays)

    act = (
        act.reshape(micros, seqs, chans, parts, own)
        .transpose(0, 3, 1, 2, 4)
        .reshape(peers * seqs, chans, own)
    )
    act = exchange(act, both).reshape(full, own)
    (d_act,) = kernel_call(
        functools.partial(project_kernel, width),
        "project",
        (place, lens),
        (act, *weights),
        [shape_of((full, own), bf16)],
        2,
        limit=12,
        scratch_shapes=[pltpu.VMEM((own, 2 * full), bf16)],
    )

    acts = [act] + [cross(act, k) for k in range(1, peers)]
    if parts == 1:
        order = chan_rank ^ jnp.arange(peers, dtype=jnp.int32)
    else:
        stacked = jnp.stack(acts)[chan_rank ^ jnp.arange(peers, dtype=jnp.int32)]
        stacked = stacked.reshape(micros, parts, full, own).transpose(0, 2, 1, 3)
        stacked = stacked.reshape(micros, full, width)
        acts = [stacked[m] for m in range(micros)]
        order = jnp.arange(micros, dtype=jnp.int32)

    d_act = exchange(d_act.reshape(peers * seqs, chans, own), both)
    d_act = (
        d_act.reshape(micros, parts, seqs, chans, own)
        .transpose(0, 2, 3, 1, 4)
        .reshape(rows * chans, width)
    )
    count = full // seqs
    part = (seqs // 2, 2 * count + 8, wide)
    out, keep, send = kernel_call(
        functools.partial(output_kernel, seqs),
        "output",
        (rank, lens, order),
        (tokens, out_cotangent, w_value, w_gate) + bias_rows + tuple(acts),
        [shape_of(tokens.shape, bf16), shape_of(part), shape_of(part, bf16)],
        2,
        limit=12,
        scratch_shapes=[
            pltpu.VMEM((micros * width, 2 * wide), bf16),
            pltpu.VMEM((seqs,) + part[1:], f32),
        ],
    )
    got = lax.ppermute(send, "seq", [(i, i ^ 1) for i in range(seqs)])
    d_act, keep = lax.optimization_barrier((d_act, keep))
    stride = -(-((micros + 3) * chans + 2) // 16) * 16
    arrays = (x_mine, d_act, norm_mine, const, taps, live, y_mine, in_hbm(power), in_hbm(kept))
    d_hat = pl.pallas_call(
        functools.partial(backward_kernel, micros, seqs, chans),
        in_specs=[vmem()] * (len(arrays) - 2) + [hbm] * 2,
        out_specs=vmem(),
        out_shape=shape_of((seqs, stride, width), bf16),
        scratch_shapes=backward_scratch(micros, seqs, chans, stride, width, lane),
        compiler_params=pltpu.CompilerParams(vmem_limit_bytes=20 * 1024 * 1024),
        cost_estimate=cost(5),
        name="mixer_backward",
    )(*arrays)
    d_hat, got = lax.optimization_barrier((d_hat, got))
    for level in range(spans):
        by = 1 << level
        if level:
            got = lax.ppermute(send, "seq", [(i, i ^ by) for i in range(seqs)])
        if level == spans - 1:
            break
        half_part = (seqs >> (level + 2),) + part[1:]
        keep, send = kernel_call(
            halve_kernel,
            "halve",
            ((seq_rank.reshape(1) >> (level + 1)) & 1,),
            (keep, got),
            [shape_of(half_part), shape_of(half_part, bf16)],
            1,
            scratch_shapes=[pltpu.VMEM(keep.shape, f32)],
        )
    d_wv, d_wg, d_bv, d_bg = kernel_call(
        last_kernel,
        "last",
        (),
        (keep, got),
        [shape_of((count, wide))] * 2 + [shape_of((1, wide))] * 2,
        1,
    )
    got = exchange(d_hat, "seq")
    own_sums, head, norm = kernel_call(
        sums_kernel,
        "sums",
        (),
        (got, tokens, *stats),
        [
            shape_of((2 * micros, width)),
            shape_of((seqs, stride, width)),
            shape_of((2 * micros, width)),
        ],
        1,
    )
    hat_sums = [own_sums] + [cross(own_sums, k) for k in range(1, peers)]
    mode_grad = shape_of((2, modes, wide))
    d_input, d_b, d_e, d_c, d_skip, d_gain, d_bias = kernel_call(
        final_kernel,
        "final",
        (rank, lens),
        (head, tokens, out_cotangent, norm, *hat_sums),
        [shape_of(tokens.shape)]
        + [mode_grad] * 3
        + [shape_of((1, wide))] * 3,
        2,
    )
    d_b, d_e, d_c = [jnp.transpose(z, (0, 2, 1)) for z in (d_b, d_e, d_c)]
    d_skip, d_gain, d_bias, d_bv, d_bg = [
        z.reshape(wide) for z in (d_skip, d_gain, d_bias, d_bv, d_bg)
    ]
    return (out, d_input, d_gain, d_bias, d_b, d_e, d_c, d_skip, d_wv, d_wg, d_bv, d_bg)


def solution(mesh):
    chan = P("chan")
    modes = P(None, "chan", None)
    table = P("chan", None)
    weight = P(None, "chan")
    rows = P(None, "chan", "seq")
    spread = P("seq", "chan")
    return jax.shard_map(
        shards,
        mesh=mesh,
        in_specs=(
            rows,
            P(),
            chan,
            chan,
            modes,
            modes,
            modes,
            chan,
            table,
            table,
            weight,
            weight,
            chan,
            chan,
            rows,
        ),
        out_specs=(
            rows,
            rows,
            chan,
            chan,
            modes,
            modes,
            modes,
            chan,
            spread,
            spread,
            chan,
            chan,
        ),
        check_vma=False,
    )
```

```python
import functools
import math

import jax
import jax.numpy as jnp
from jax import lax
from jax.experimental import pallas as pl
from jax.experimental.pallas import tpu as pltpu
from jax.sharding import PartitionSpec as P

f32 = jnp.float32
bf16 = jnp.bfloat16
epsilon = 1e-05
NN = (((1,), (0,)), ((), ()))
NT = (((1,), (1,)), ((), ()))
TN = (((0,), (0,)), ((), ()))


def mm(left, right, dims=NN):
    return lax.dot_general(left, right, dims, preferred_element_type=f32)


def split(x):
    high = x.astype(bf16)
    return high, (x - high.astype(f32)).astype(bf16)


def swap(x, half):
    return pltpu.roll(x, half, axis=x.ndim - 1)


def lanes(shape):
    return lax.broadcasted_iota(jnp.int32, shape, len(shape) - 1)


def pair(z, half):
    low = lanes(z.shape) < half
    turned = swap(z, half)
    return jnp.where(low, z, turned), jnp.where(low, -turned, z)


def cmul(x, z, half):
    return x * z[0] + swap(x, half) * z[1]


def normal_cdf(y):
    return 0.5 * (1.0 + lax.erf(y * (1.0 / math.sqrt(2.0))))


def mirror(width):
    shape = (width, width)
    at = lanes(shape) + lax.broadcasted_iota(jnp.int32, shape, 0)
    return (at == width - 1).astype(f32).astype(bf16)


def live_rows(lens_ref, micros, chunks, width):
    shape = (chunks, width)
    at = lax.broadcasted_iota(jnp.int32, shape, 0) * width + (width - 1 - lanes(shape))
    rows = [(at < lens_ref[m]).astype(f32) for m in range(micros)]
    return jnp.concatenate(rows, axis=0)


def merge(means, squares, count):
    parts = len(means)
    mean = sum(means[1:], means[0]) * (1.0 / parts)
    square = sum(squares[1:], squares[0])
    for part in means:
        square = square + count * jnp.square(part - mean)
    return mean, lax.rsqrt(square * (1.0 / (parts * count)) + epsilon)


def fetch(copies):
    for copy in copies:
        copy.start()


def shift_chunks(x, by, micros, chunks):
    cube = x.reshape(micros, chunks, x.shape[-1])
    place = lax.broadcasted_iota(jnp.int32, cube.shape, 1)
    if by > 0:
        moved = jnp.where(place >= by, pltpu.roll(cube, by, axis=1), 0.0)
    else:
        moved = jnp.where(place < chunks + by, pltpu.roll(cube, chunks + by, axis=1), 0.0)
    return moved.reshape(x.shape)


def previous(u, micros, chunks):
    width = u.shape[1]
    turned = pltpu.roll(u, width - 1, axis=1)
    return jnp.where(
        lanes(u.shape) == width - 1, shift_chunks(turned, 1, micros, chunks), turned
    )


def following(u, micros, chunks):
    turned = pltpu.roll(u, 1, axis=1)
    return jnp.where(lanes(u.shape) == 0, shift_chunks(turned, -1, micros, chunks), turned)


def hankel(first, width):
    blocks = []
    for k in range(width // 8):
        by = width - 8 - 8 * k
        blocks.append(pltpu.roll(first, by, axis=1) if by else first)
    table = jnp.concatenate(blocks, axis=0)
    at = lanes(table.shape) + lax.broadcasted_iota(jnp.int32, table.shape, 0)
    return split(jnp.where(at >= width - 1, table, 0.0))


def gather_kernel(rank_ref, bv_ref, bg_ref, cot_hbm, wv_hbm, wg_hbm, *refs):
    outs, sems = refs[:-1], refs[-1]
    peers, wide, _ = cot_hbm.shape
    full = wv_hbm.shape[0]
    copies = []
    for k, out in enumerate(outs):
        for source, start, count in (
            (cot_hbm.at[rank_ref[0] ^ k], 0, wide),
            (wv_hbm, wide, full),
            (wg_hbm, wide + full, full),
        ):
            copies.append(
                pltpu.make_async_copy(
                    source, out.at[pl.ds(start, count), :], sems.at[len(copies)]
                )
            )
    fetch(copies)
    pieces = []
    for value in (bv_ref[...], bg_ref[...]):
        for _ in range(3):
            high = value.astype(bf16).astype(f32)
            pieces.append(high)
            value = value - high
    pieces.append(jnp.zeros((10, wide), f32))
    biases = jnp.concatenate(pieces, axis=0).astype(bf16)
    for out in outs:
        out[pl.ds(wide + 2 * full, 16), :] = biases
    for copy in copies:
        copy.wait()


def pack_kernel(seqs, tokens_hbm, send_ref, stats_ref, tokens, sems):
    micros, wide, width = tokens.shape
    chans = wide // seqs
    copies = [
        pltpu.make_async_copy(tokens_hbm.at[m], tokens.at[m], sems.at[m]) for m in range(micros)
    ]
    fetch(copies)
    turn = mirror(width)
    means, squares = [], []
    for m in range(micros):
        copies[m].wait()
        x = tokens[m].astype(f32)
        mean = jnp.sum(x, axis=0, keepdims=True) * (1.0 / wide)
        means.append(mean)
        squares.append(jnp.sum(jnp.square(x - mean), axis=0, keepdims=True))
        turned = mm(tokens[m], turn).astype(bf16)
        send_ref[:, pl.ds(m * chans, chans), :] = turned.reshape(seqs, chans, width)
    stats = jnp.concatenate(means + squares, axis=0)
    stats_ref[...] = stats
    high = stats.astype(bf16).astype(f32)
    tail = jnp.concatenate([high, stats - high], axis=0).astype(bf16)
    tail = mm(tail, turn).astype(bf16)
    for k in range(seqs):
        send_ref[k, pl.ds(micros * chans, 4 * micros), :] = tail


def table_kernel(
    chans,
    seqs,
    width,
    rank_ref,
    lens_ref,
    skip_ref,
    gain_ref,
    bias_ref,
    b_hbm,
    e_hbm,
    c_hbm,
    decay_hbm,
    turn_hbm,
    const_ref,
    rise,
    taps_ref,
    live_ref,
    b_ref,
    e_ref,
    c_ref,
    decay_ref,
    turn_ref,
    turned_keep,
    coefs,
    sems,
):
    half = decay_ref.shape[0]
    loads = [
        pltpu.make_async_copy(source, target, sems.at[k])
        for k, (source, target) in enumerate(
            (
                (b_hbm, b_ref),
                (e_hbm, e_ref),
                (c_hbm, c_ref),
                (decay_hbm, decay_ref),
                (turn_hbm, turn_ref),
            )
        )
    ]
    fetch(loads)
    for load in loads:
        load.wait()
    base = rank_ref[0] * chans
    levels = int(math.log2(width)) - 3
    spans = int(math.log2(seqs))

    def own(value):
        turned_keep[...] = value.T
        return turned_keep[pl.ds(base, chans), :]

    b = own(b_ref[...].reshape(2 * half, -1))
    e = own(e_ref[...].reshape(2 * half, -1))
    c = own(c_ref[...].reshape(2 * half, -1))
    mixed = own(jnp.concatenate([decay_ref[...], turn_ref[...]], axis=0))
    low = lanes(mixed.shape) < half
    other = swap(mixed, half)
    decay = jnp.where(low, mixed, other)
    turn = jnp.where(low, other, mixed)
    turned = jnp.where(low, jnp.cos(turn), jnp.sin(turn))
    a = jnp.exp(-decay) * turned
    inverse = pair(jnp.exp(decay) * jnp.where(low, turned, -turned), half)
    a_pair = pair(a, half)
    power = jnp.where(low, 1.0, 0.0)
    for k in range(8):
        rise[pl.ds(k * chans, chans), :] = power
        power = cmul(power, a_pair, half) if k else a
    for k in range(levels):
        power_pair = pair(power, half)
        rise[pl.ds((8 + 2 * k) * chans, chans), :] = power_pair[0]
        rise[pl.ds((9 + 2 * k) * chans, chans), :] = power_pair[1]
        power = cmul(power, power_pair, half)
    kept = [pair(b, half), pair(e, half), pair(cmul(a, pair(c, half), half), half)]
    for k in range(spans):
        kept.append(pair(power, half))
        power = cmul(power, kept[-1], half)
    kept += [pair(c, half), a_pair]
    for k, both in enumerate(kept):
        const_ref[2 * k] = both[0]
        const_ref[2 * k + 1] = both[1]
    sign = jnp.where(low, 1.0, -1.0)
    for j in range(2):
        coef = cmul(c, kept[j], half)
        for k in range(7, -1, -1):
            coefs[pl.ds((8 * j + k) * chans, chans), :] = coef * sign
            coef = cmul(coef, inverse, half)

    live_ref[...] = live_rows(lens_ref, lens_ref.shape[0], seqs, width)
    for channel in range(chans):
        for k, ref in enumerate((gain_ref, bias_ref)):
            const_ref[2 * len(kept) + k, channel : channel + 1, :] = jnp.full(
                (1, 2 * half), ref[base + channel], f32
            )
        high, low_part = mode_powers(rise, channel, chans, levels, half)
        coef = coefs[pl.ds(channel, 16, stride=chans), :]
        coef_hi = coef.astype(bf16).astype(f32)
        both = jnp.concatenate([coef_hi, coef - coef_hi], axis=0).astype(bf16)
        taps = mm(both, high, NT) + mm(both, low_part, NT)
        taps = taps[:16] + taps[16:]
        at = lanes(taps.shape) + lax.broadcasted_iota(jnp.int32, taps.shape, 0)
        taps_ref[channel] = taps + jnp.where(at == 7, skip_ref[base + channel], 0.0)


def mode_powers(rise_ref, channel, chans, levels, half):
    up = rise_ref[pl.ds(channel, 8, stride=chans), :]
    for k in range(levels):
        at = (8 + 2 * k) * chans + channel
        by = (rise_ref[at : at + 1, :], rise_ref[at + chans : at + chans + 1, :])
        up = jnp.concatenate([up, cmul(up, by, half)], axis=0)
    return split(up)


def own_rows(keep, at, stride, micros, chunks):
    return jnp.concatenate(
        [keep[pl.ds(at + m, chunks, stride=stride), :] for m in range(micros)], axis=0
    )


def channel_tokens(keep, channel, stride, micros, chunks, chans):
    return jnp.concatenate(
        [keep[pl.ds(m * chans + channel, chunks, stride=stride), :] for m in range(micros)],
        axis=0,
    )


def forward_kernel(
    micros,
    chunks,
    chans,
    peers,
    got_ref,
    const_ref,
    rise_ref,
    taps_ref,
    live_ref,
    *refs,
):
    stats_refs, refs = refs[: peers - 1], refs[peers - 1 :]
    act_ref, norm_ref, y_ref, kept_hbm, act_keep, x_keep, stats_keep = refs[:7]
    parts, wide_parts, sent_parts, kept_ref, power_ref, sem = refs[7:]
    width = got_ref.shape[2]
    half = const_ref.shape[2] // 2
    spans = int(math.log2(chunks))
    rows = micros * chunks
    stride = got_ref.shape[1]
    flip = jnp.where(lanes((1, 2 * half)) < half, 1.0, -1.0)

    def const(channel, k):
        return (
            const_ref[2 * k, channel : channel + 1, :],
            const_ref[2 * k + 1, channel : channel + 1, :],
        )

    live = live_ref[...]
    gain, bias = 2 * (5 + spans), 2 * (5 + spans) + 1
    for k in range(chunks):
        x_keep[pl.ds(k * stride, stride), :] = got_ref[k].astype(f32)
    means, squares = [], []
    for j in range(peers):
        keep, step, at = x_keep, stride, micros * chans
        if j:
            keep, step, at = stats_keep.at[j - 1], 4 * micros, 0
            for k in range(chunks):
                keep[pl.ds(k * step, step), :] = stats_refs[j - 1][k].astype(f32)
        lines = [own_rows(keep, at + q * micros, step, micros, chunks) for q in range(4)]
        means.append(lines[0] + lines[2])
        squares.append(lines[1] + lines[3])
    mean, inverse = merge(means, squares, chans * chunks)
    norm_ref[pl.ds(0, rows), :] = mean
    norm_ref[pl.ds(rows, rows), :] = inverse

    for channel in range(chans):
        x_hat = channel_tokens(x_keep, channel, stride, micros, chunks, chans) - mean
        line = slice(channel, channel + 1)
        u = live * (x_hat * inverse * const_ref[gain, line] + const_ref[bias, line])
        u_hi, u_lo = split(u)
        v_hi, v_lo = split(u * previous(u, micros, chunks))
        for k, part in enumerate((u_hi, v_hi, u_lo, v_lo)):
            parts[channel, k * rows : (k + 1) * rows] = part
        wide_parts[channel, :rows, :width] = u_hi
        wide_parts[channel, :rows, width:] = v_hi
        wide_parts[channel, rows:, :width] = u_lo
        wide_parts[channel, rows:, width:] = v_lo

    levels = int(math.log2(width)) - 3
    for channel in range(chans):
        high, low_part = mode_powers(rise_ref, channel, chans, levels, half)
        power_ref[channel, :width] = high
        power_ref[channel, width:] = low_part

    for channel in range(chans):
        q = mm(parts[channel], power_ref[channel, :width])
        kept_ref[channel, : 2 * rows] = (
            q[: 2 * rows]
            + q[2 * rows :]
            + mm(parts[channel, : 2 * rows], power_ref[channel, width:])
        )

    for channel in range(chans):
        uq, vq = kept_ref[channel, :rows], kept_ref[channel, rows : 2 * rows]
        state = cmul(uq, const(channel, 0), half) + cmul(vq, const(channel, 1), half)
        for k in range(spans):
            moved = shift_chunks(state, 2**k, micros, chunks)
            state = state + cmul(moved, const(channel, 3 + k), half)
        start = shift_chunks(state, 1, micros, chunks)
        kept_ref[channel, 2 * rows :] = start
        high, low_part = split(cmul(start, const(channel, 2), half) * flip)
        sent_parts[channel, :rows] = high
        sent_parts[channel, rows:] = low_part
    store = pltpu.make_async_copy(kept_ref, kept_hbm, sem)
    store.start()

    for channel in range(chans):
        tables = [hankel(taps_ref[channel, 8 * k : 8 * k + 8], width) for k in range(2)]
        both = wide_parts[channel]
        y = mm(both, jnp.concatenate([tables[0][0], tables[1][0]], axis=0))
        low_part = mm(both[:rows], jnp.concatenate([tables[0][1], tables[1][1]], axis=0))
        y_ref[channel] = y[:rows] + y[rows:] + low_part

    for channel in range(chans):
        both = sent_parts[channel]
        cross = mm(both, power_ref[channel, :width], NT)
        y = y_ref[channel] + cross[:rows] + cross[rows:]
        y = y + mm(both[:rows], power_ref[channel, width:], NT)
        y_ref[channel] = y
        act = y * normal_cdf(y)
        for m in range(micros):
            act_keep[pl.ds(m * chunks * chans + channel, chunks, stride=chans), :] = act[
                m * chunks : (m + 1) * chunks
            ]
    act_ref[...] = act_keep[...].astype(bf16)
    store.wait()


def forward_scratch(micros, chunks, chans, peers, width, lane):
    rows = micros * chunks
    return [
        pltpu.VMEM((rows * chans, width), f32),
        pltpu.VMEM((chunks * micros * (chans + 4), width), f32),
        pltpu.VMEM((peers - 1, 4 * rows, width), f32),
        pltpu.VMEM((chans, 4 * rows, width), bf16),
        pltpu.VMEM((chans, 2 * rows, 2 * width), bf16),
        pltpu.VMEM((chans, 2 * rows, lane), bf16),
        pltpu.VMEM((chans, 3 * rows, lane), f32),
        pltpu.VMEM((chans, 2 * width, lane), bf16),
        pltpu.SemaphoreType.DMA(()),
    ]


def backward_kernel(
    micros,
    chunks,
    chans,
    got_ref,
    dact_ref,
    norm_ref,
    const_ref,
    rise_ref,
    taps_ref,
    live_ref,
    y_ref,
    kept_hbm,
    send_ref,
    sums_keep,
    head,
    x_keep,
    dact_keep,
    u_keep,
    prev_keep,
    dy_parts,
    uv_parts,
    yd_keep,
    duv_keep,
    lag_keep,
    adj_keep,
    sent_parts,
    dots,
    power_ref,
    kept_ref,
    sem,
):
    load = pltpu.make_async_copy(kept_hbm, kept_ref, sem)
    load.start()
    width = got_ref.shape[2]
    half = const_ref.shape[2] // 2
    spans = int(math.log2(chunks))
    rows = micros * chunks
    stride = head.shape[0] // chunks
    got_stride = got_ref.shape[1]
    shape = (width, width)
    passed = lanes(shape) <= lax.broadcasted_iota(jnp.int32, shape, 0)
    low = lanes((1, 2 * half)) < half
    flip = jnp.where(low, 1.0, -1.0)
    live = live_ref[...]
    gain, bias = 2 * (5 + spans), 2 * (5 + spans) + 1
    for k in range(chunks):
        x_keep[pl.ds(k * got_stride, got_stride), :] = got_ref[k].astype(f32)
    dact_keep[...] = dact_ref[...].astype(f32)
    mean, inverse = norm_ref[:rows], norm_ref[rows:]

    def x_hat_of(channel):
        x = channel_tokens(x_keep, channel, got_stride, micros, chunks, chans)
        return (x - mean) * inverse

    def const(channel, k):
        return (
            const_ref[2 * k, channel : channel + 1, :],
            const_ref[2 * k + 1, channel : channel + 1, :],
        )

    def total(x):
        return jnp.sum(x, axis=0, keepdims=True)

    for channel in range(chans):
        line = slice(channel, channel + 1)
        u = live * (x_hat_of(channel) * const_ref[gain, line] + const_ref[bias, line])
        u_prev = previous(u, micros, chunks)
        u_keep[channel] = u
        prev_keep[channel] = u_prev
        u_hi, u_lo = split(u)
        v_hi, v_lo = split(u * u_prev)
        for k, (left, right) in enumerate(((u_hi, v_hi), (u_hi, v_hi), (u_lo, v_lo))):
            uv_parts[channel, k * rows : (k + 1) * rows, :width] = left
            uv_parts[channel, k * rows : (k + 1) * rows, width:] = right
        y = y_ref[channel]
        density = jnp.exp(-0.5 * y * y) * (1.0 / math.sqrt(2.0 * math.pi))
        d_y = dact_keep[pl.ds(channel, rows, stride=chans), :] * (normal_cdf(y) + y * density)
        high, low_part = split(d_y)
        dy_parts[channel, :rows] = high
        dy_parts[channel, rows : 2 * rows] = low_part
        dy_parts[channel, 2 * rows :] = high

    for channel in range(chans):
        tables = [hankel(taps_ref[channel, 8 * k : 8 * k + 8], width) for k in range(2)]
        both = dy_parts[channel, : 2 * rows]
        duv = mm(both, jnp.concatenate([tables[0][0], tables[1][0]], axis=1))
        low_part = mm(both[:rows], jnp.concatenate([tables[0][1], tables[1][1]], axis=1))
        duv_keep[channel] = duv[:rows] + duv[rows:] + low_part

    for channel in range(chans):
        outer = mm(dy_parts[channel], uv_parts[channel], TN)
        for k in range(2):
            rolled = pltpu.roll(
                outer[:, k * width : (k + 1) * width], 1, axis=1, stride=1, stride_axis=0
            )
            line = total(jnp.where(passed, rolled, 0.0))
            high = line.astype(bf16).astype(f32)
            lag_keep[channel, k : k + 1, :] = high
            lag_keep[channel, 2 + k : 3 + k, :] = line - high
            if k == 0:
                sums_keep[channel : channel + 1, :] = jnp.where(
                    lanes(line.shape) == 0, line, 0.0
                )

    levels = int(math.log2(width)) - 3
    for channel in range(chans):
        high, low_part = mode_powers(rise_ref, channel, chans, levels, half)
        power_ref[channel, :width] = high
        power_ref[channel, width:] = low_part

    for channel in range(chans):
        both = dy_parts[channel, : 2 * rows]
        yd = mm(both, power_ref[channel, :width])
        low_part = mm(both[:rows], power_ref[channel, width:])
        yd_keep[channel] = yd[:rows] + yd[rows:] + low_part

    for channel in range(chans):
        adj = cmul(yd_keep[channel], const(channel, 2), half)
        for k in range(spans):
            moved = shift_chunks(adj, -(2**k), micros, chunks)
            adj = adj + cmul(moved, const(channel, 3 + k), half)
        adj = shift_chunks(adj, -1, micros, chunks)
        adj_keep[channel] = adj
        sent = jnp.concatenate(
            [cmul(adj, const(channel, 0), half), cmul(adj, const(channel, 1), half)], axis=0
        )
        high, low_part = split(sent * flip)
        sent_parts[channel, : 2 * rows] = high
        sent_parts[channel, 2 * rows :] = low_part

    for channel in range(chans):
        both = sent_parts[channel]
        cross = mm(both, power_ref[channel, :width], NT)
        cross = cross[: 2 * rows] + cross[2 * rows :]
        cross = cross + mm(both[: 2 * rows], power_ref[channel, width:], NT)
        d_v = duv_keep[channel, :, width:] + cross[rows:]
        d_u = duv_keep[channel, :, :width] + cross[:rows] + d_v * prev_keep[channel]
        d_u = d_u + following(d_v * u_keep[channel], micros, chunks)
        d_q = live * d_u
        sums_keep[chans + channel : chans + channel + 1, :] = total(d_q * x_hat_of(channel))
        sums_keep[2 * chans + channel : 2 * chans + channel + 1, :] = total(d_q)
        d_h = d_q * const_ref[gain, channel : channel + 1]
        for m in range(micros):
            head[pl.ds(m * chans + channel, chunks, stride=stride), :] = d_h[
                m * chunks : (m + 1) * chunks
            ]

    load.wait()
    lag_keep[:, 4:, :] = jnp.zeros((chans, 12, width), f32)
    for channel in range(chans):
        lags = lag_keep[channel].astype(bf16)
        tops = mm(lags, power_ref[channel, :width]) + mm(lags, power_ref[channel, width:])
        dots[6, channel : channel + 1, :] = tops[0:1] + tops[2:3]
        dots[7, channel : channel + 1, :] = tops[1:2] + tops[3:4]
        adj, yd = adj_keep[channel], yd_keep[channel]
        adj_swap = swap(adj, half)
        uq, vq, start = [kept_ref[channel, k * rows : (k + 1) * rows] for k in range(3)]
        pairs = ((uq, adj), (uq, adj_swap), (vq, adj), (vq, adj_swap), (start, yd))
        for k, (left, right) in enumerate(pairs + ((start, swap(yd, half)),)):
            dots[k, channel : channel + 1, :] = total(left * right)

    def whole_const(k):
        return const_ref[2 * k], const_ref[2 * k + 1]

    def dot(k):
        same, other = dots[k], dots[k + 1]
        return jnp.where(low, same - swap(same, half), other + swap(other, half))

    top_u, top_v = dots[6], dots[7]
    c = whole_const(3 + spans)
    modes = jnp.concatenate(
        [
            flip * (cmul(top_u, c, half) + dot(0)),
            flip * (cmul(top_v, c, half) + dot(2)),
            flip
            * (
                cmul(top_u, whole_const(0), half)
                + cmul(top_v, whole_const(1), half)
                + cmul(dot(4), whole_const(4 + spans), half)
            ),
        ],
        axis=0,
    )
    sums = jnp.sum(sums_keep[...].T, axis=0, keepdims=True)
    sums_hi = sums.astype(bf16).astype(f32)
    cut = micros * chans
    for k in range(chunks):
        at = k * stride + cut
        head[pl.ds(at, 3 * chans), :] = modes
        head[pl.ds(at + 3 * chans, 1), pl.ds(0, 3 * chans)] = sums_hi
        head[pl.ds(at + 3 * chans + 1, 1), pl.ds(0, 3 * chans)] = sums - sums_hi
        send_ref[k] = head[pl.ds(k * stride, stride), :].astype(bf16)


def backward_scratch(micros, chunks, chans, stride, width, lane):
    rows = micros * chunks
    return [
        pltpu.VMEM((3 * chans, lane), f32),
        pltpu.VMEM((chunks * stride, width), f32),
        pltpu.VMEM((chunks * micros * (chans + 4), width), f32),
        pltpu.VMEM((rows * chans, width), f32),
        pltpu.VMEM((chans, rows, width), f32),
        pltpu.VMEM((chans, rows, width), f32),
        pltpu.VMEM((chans, 3 * rows, width), bf16),
        pltpu.VMEM((chans, 3 * rows, 2 * width), bf16),
        pltpu.VMEM((chans, rows, lane), f32),
        pltpu.VMEM((chans, rows, 2 * width), f32),
        pltpu.VMEM((chans, 16, width), f32),
        pltpu.VMEM((chans, rows, lane), f32),
        pltpu.VMEM((chans, 4 * rows, lane), bf16),
        pltpu.VMEM((8, chans, lane), f32),
        pltpu.VMEM((chans, 2 * width, lane), bf16),
        pltpu.VMEM((chans, 3 * rows, lane), f32),
        pltpu.SemaphoreType.DMA(()),
    ]


def gated(both, bias, g):
    wide = g.shape[1]
    value = both[:, :wide] + bias[:, :wide]
    gate = jax.nn.sigmoid(both[:, wide:] + bias[:, wide:])
    d_value = g * gate
    return value * gate, jnp.concatenate(
        [d_value.astype(bf16), (d_value * value * (1.0 - gate)).astype(bf16)], axis=1
    )


def project_kernel(width, place_ref, lens_ref, act_ref, *refs):
    refs, (dact_ref, d_keep) = refs[:-2], refs[-2:]
    full, rows = act_ref.shape
    peers = len(refs)
    wide = full // peers
    start = place_ref[1] * rows
    at = place_ref[0] * width + lax.rem(start, width)
    at = at + lax.broadcasted_iota(jnp.int32, (rows, wide), 0)
    live = (at < lens_ref[start // width]).astype(f32)
    act = act_ref[...].T

    def weight(ref):
        return jnp.concatenate(
            [ref[wide : wide + full, :], ref[wide + full : wide + 2 * full, :]], axis=1
        )

    for k, ref in enumerate(refs):
        g = live * ref[:wide, :].T.astype(f32)
        bias = ref[wide + 2 * full :, :].astype(f32)
        bias = jnp.concatenate(
            [bias[0:1] + bias[1:2] + bias[2:3], bias[3:4] + bias[4:5] + bias[5:6]], axis=1
        )
        d_both = gated(mm(act, weight(ref)), bias, g)[1]
        d_keep[:, 2 * k * wide : 2 * (k + 1) * wide] = d_both
    weights = jnp.concatenate([weight(ref) for ref in refs], axis=1)
    dact_ref[...] = mm(weights, d_keep[...], NT).astype(bf16)


def output_kernel(
    seqs,
    rank_ref,
    lens_ref,
    order_ref,
    tokens_ref,
    cot_ref,
    wv_ref,
    wg_ref,
    bv_ref,
    bg_ref,
    *refs,
):
    micros, wide, width = tokens_ref.shape
    acts_in, refs = refs[:micros], refs[micros:]
    out_ref, keep_ref, send_ref, d_keep, grad = refs
    full = wv_ref.shape[0]
    at = rank_ref[0] * width + lax.broadcasted_iota(jnp.int32, (width, wide), 0)
    place = rank_ref[0] * width + lanes((1, width))
    weights = jnp.concatenate([wv_ref[...], wg_ref[...]], axis=1)
    bias = jnp.concatenate([bv_ref[...], bg_ref[...]], axis=1)
    for k in range(micros):
        m = order_ref[k]
        g = (at < lens_ref[m]).astype(f32) * cot_ref[m].T.astype(f32)
        added, d_both = gated(mm(acts_in[k][...].T, weights), bias, g)
        live = (place < lens_ref[m]).astype(f32)
        out_ref[m] = (live * (tokens_ref[m].astype(f32) + added.T)).astype(bf16)
        d_keep[k * width : (k + 1) * width] = d_both
    d_both = d_keep[...]
    acts = jnp.concatenate([ref[...] for ref in acts_in], axis=1)
    grad_w = mm(acts, d_both)
    grad_b = mm(jnp.ones((8, micros * width), bf16), d_both)
    row = lax.broadcasted_iota(jnp.int32, (8, wide), 0)
    small = jnp.where(row == 0, grad_b[:, :wide], grad_b[:, wide:])
    count = full // seqs
    for k in range(seqs):
        part = grad_w[k * count : (k + 1) * count]
        grad[k, pl.ds(0, count), :] = part[:, :wide]
        grad[k, pl.ds(count, count), :] = part[:, wide:]
        grad[k, pl.ds(2 * count, 8), :] = small
    bit = rank_ref[0] & 1
    for k in range(seqs // 2):
        keep_ref[k] = grad[2 * k + bit]
        send_ref[k] = grad[2 * k + 1 - bit].astype(bf16)


def halve_kernel(bit_ref, left_ref, right_ref, keep_ref, send_ref, total):
    total[...] = left_ref[...] + right_ref[...].astype(f32)
    for k in range(keep_ref.shape[0]):
        keep_ref[k] = total[2 * k + bit_ref[0]]
        send_ref[k] = total[2 * k + 1 - bit_ref[0]].astype(bf16)


def last_kernel(left_ref, right_ref, wv_ref, wg_ref, bv_ref, bg_ref):
    count = wv_ref.shape[0]
    total = left_ref[0] + right_ref[0].astype(f32)
    wv_ref[...] = total[:count]
    wg_ref[...] = total[count : 2 * count]
    bv_ref[...] = total[2 * count : 2 * count + 1]
    bg_ref[...] = total[2 * count + 1 : 2 * count + 2]


def normal(tokens_ref, norm_ref, m):
    micros = tokens_ref.shape[0]
    return (tokens_ref[m].astype(f32) - norm_ref[m : m + 1]) * norm_ref[
        micros + m : micros + m + 1
    ]


def sums_kernel(got_ref, tokens_ref, *refs):
    stats_refs, (out_ref, head_ref, norm_ref) = refs[:-3], refs[-3:]
    micros, wide, width = tokens_ref.shape
    seqs, stride, _ = head_ref.shape
    chans = wide // seqs
    mean, inverse = merge(
        [ref[pl.ds(0, micros), :] for ref in stats_refs],
        [ref[pl.ds(micros, micros), :] for ref in stats_refs],
        wide,
    )
    norm_ref[pl.ds(0, micros), :] = mean
    norm_ref[pl.ds(micros, micros), :] = inverse
    cut = micros * chans
    turned = got_ref[:, pl.ds(0, cut), :].reshape(seqs * cut, width)
    head_ref[:, pl.ds(0, cut), :] = mm(turned, mirror(width)).reshape(seqs, cut, width)
    head_ref[:, pl.ds(cut, stride - cut), :] = got_ref[:, pl.ds(cut, stride - cut), :].astype(f32)
    for m in range(micros):
        d_hat = head_ref[:, pl.ds(m * chans, chans), :].reshape(wide, width)
        x_hat = normal(tokens_ref, norm_ref, m)
        out_ref[pl.ds(m, 1), :] = jnp.sum(d_hat, axis=0, keepdims=True)
        out_ref[pl.ds(micros + m, 1), :] = jnp.sum(d_hat * x_hat, axis=0, keepdims=True)


def final_kernel(
    rank_ref,
    lens_ref,
    head_ref,
    tokens_ref,
    cot_ref,
    norm_ref,
    *refs,
):
    hat_refs, refs = refs[:-7], refs[-7:]
    d_in_ref, b_ref, e_ref, c_ref, skip_ref, gain_ref, norm_bias_ref = refs
    micros, wide, width = tokens_ref.shape
    seqs, stride, _ = head_ref.shape
    peers = len(hat_refs)
    chans = wide // seqs
    hats = [ref[...] for ref in hat_refs]
    hat = sum(hats[1:], hats[0]) * (1.0 / (peers * wide))
    at = rank_ref[0] * width + lanes((1, width))
    for m in range(micros):
        live = (at < lens_ref[m]).astype(f32)
        d_hat = head_ref[:, pl.ds(m * chans, chans), :].reshape(wide, width)
        x_hat = normal(tokens_ref, norm_ref, m)
        inside = d_hat - hat[m : m + 1] - x_hat * hat[micros + m : micros + m + 1]
        d_in_ref[m] = (
            live * cot_ref[m].astype(f32) + norm_ref[micros + m : micros + m + 1] * inside
        )
    cut = micros * chans
    for k, ref in enumerate((b_ref, e_ref, c_ref)):
        modes = head_ref[:, pl.ds(cut + k * chans, chans), :]
        ref[...] = modes.reshape(wide, -1).T.reshape(ref.shape)
    place = lanes((1, wide)) // chans
    last = cut + 3 * chans
    for k, ref in enumerate((skip_ref, gain_ref, norm_bias_ref)):
        line = jnp.zeros((1, wide), f32)
        for s in range(seqs):
            own = head_ref[s, pl.ds(last, 1), :] + head_ref[s, pl.ds(last + 1, 1), :]
            own = pltpu.roll(own, (s - k) * chans % own.shape[1], axis=1)[:, :wide]
            line = jnp.where(place == s, own, line)
        ref[...] = line


def smem():
    return pl.BlockSpec(memory_space=pltpu.SMEM)


def vmem():
    return pl.BlockSpec(memory_space=pltpu.VMEM)


def in_hbm(x):
    return pltpu.with_memory_space_constraint(x, pltpu.HBM)


def shape_of(shape, kind=f32):
    return jax.ShapeDtypeStruct(shape, kind)


def kernel_call(kernel, name, scalars, arrays, outs, micros_of_time, limit=8, **more):
    ins = [smem()] * len(scalars) + [vmem()] * len(arrays)
    return pl.pallas_call(
        kernel,
        in_specs=ins,
        out_specs=[vmem()] * len(outs),
        out_shape=outs,
        compiler_params=pltpu.CompilerParams(vmem_limit_bytes=limit * 1024 * 1024),
        cost_estimate=cost(micros_of_time),
        name=name,
        **more,
    )(*scalars, *arrays)


def cost(micros_of_time):
    return pl.CostEstimate(
        flops=int(micros_of_time * 1e9), bytes_accessed=int(micros_of_time * 3e6), transcendentals=0
    )


def shards(
    tokens,
    lengths,
    ln_gain,
    ln_bias,
    b_coef,
    e_coef,
    c_coef,
    skip_gain,
    decay_rate,
    rotation,
    w_value,
    w_gate,
    bias_value,
    bias_gate,
    out_cotangent,
):
    micros, wide, width = tokens.shape
    modes = decay_rate.shape[1]
    full = w_value.shape[0]
    seqs = lax.axis_size("seq")
    peers = lax.axis_size("chan")
    seq_rank = lax.axis_index("seq").astype(jnp.int32)
    chan_rank = lax.axis_index("chan").astype(jnp.int32)
    chans = wide // seqs
    rows = micros * seqs
    own = micros * width // peers
    parts = width // own
    both = ("chan", "seq")
    lane = 2 * modes
    spans = int(math.log2(seqs))
    levels = int(math.log2(width)) - 3
    rank = seq_rank.reshape(1)
    lens = lengths.reshape(micros)
    place = jnp.stack([seq_rank, chan_rank])
    bias_rows = (bias_value.reshape(1, wide), bias_gate.reshape(1, wide))

    def exchange(x, axis):
        return lax.all_to_all(x, axis, 0, 0, tiled=True)

    def cross(x, by):
        return lax.ppermute(x, "chan", [(i, i ^ by) for i in range(peers)])

    hbm = pl.BlockSpec(memory_space=pltpu.HBM)
    x_send, part_stats = pl.pallas_call(
        functools.partial(pack_kernel, seqs),
        in_specs=[hbm],
        out_specs=[vmem()] * 2,
        out_shape=[
            shape_of((seqs, micros * (chans + 4), width), bf16),
            shape_of((2 * micros, width)),
        ],
        scratch_shapes=[
            pltpu.VMEM(tokens.shape, bf16),
            pltpu.SemaphoreType.DMA((micros,)),
        ],
        compiler_params=pltpu.CompilerParams(vmem_limit_bytes=8 * 1024 * 1024),
        cost_estimate=cost(1),
        name="pack",
    )(in_hbm(tokens))
    x_mine = exchange(x_send, "seq")
    stats = [part_stats] + [cross(part_stats, k) for k in range(1, peers)]

    cot, wv, wg, _ = lax.optimization_barrier((out_cotangent, w_value, w_gate, part_stats))
    cot_own = cot.reshape(micros, wide, parts, own).transpose(0, 2, 1, 3).reshape(peers, wide, own)
    weights = pl.pallas_call(
        gather_kernel,
        in_specs=[smem()] + [vmem()] * 2 + [hbm] * 3,
        out_specs=[vmem()] * peers,
        out_shape=[shape_of((wide + 2 * full + 16, own), bf16)] * peers,
        scratch_shapes=[pltpu.SemaphoreType.DMA((3 * peers,))],
        compiler_params=pltpu.CompilerParams(vmem_limit_bytes=8 * 1024 * 1024),
        cost_estimate=cost(1),
        name="weights",
    )(chan_rank.reshape(1), *bias_rows, in_hbm(cot_own), in_hbm(wv), in_hbm(wg))

    turned = [jnp.transpose(z, (0, 2, 1)) for z in (b_coef, e_coef, c_coef)]
    const, rise, taps, live = pl.pallas_call(
        functools.partial(table_kernel, chans, seqs, width),
        in_specs=[smem()] * 5 + [hbm] * 5,
        out_specs=[vmem()] * 4,
        out_shape=[
            shape_of((12 + 2 * spans, chans, lane)),
            shape_of(((8 + 2 * levels) * chans, lane)),
            shape_of((chans, 16, width)),
            shape_of((rows, width)),
        ],
        scratch_shapes=[pltpu.VMEM(turned[0].shape, f32)] * 3
        + [pltpu.VMEM((modes, wide), f32)] * 2
        + [
            pltpu.VMEM((wide, lane), f32),
            pltpu.VMEM((16 * chans, lane), f32),
            pltpu.SemaphoreType.DMA((5,)),
        ],
        compiler_params=pltpu.CompilerParams(vmem_limit_bytes=8 * 1024 * 1024),
        cost_estimate=cost(2),
        name="tables",
    )(rank, lens, skip_gain, ln_gain, ln_bias, *[in_hbm(z) for z in (*turned, decay_rate.T, rotation.T)])

    x_mine, const, weights = lax.optimization_barrier((x_mine, const, weights))
    x_stats = x_mine[:, micros * chans :]
    x_stats = [cross(x_stats, k) for k in range(1, peers)]
    weights = [weights[0]] + [cross(weights[k], k) for k in range(1, peers)]
    arrays = (x_mine, const, rise, taps, live, *x_stats)
    act, norm_mine, y_mine, kept = pl.pallas_call(
        functools.partial(forward_kernel, micros, seqs, chans, peers),
        in_specs=[vmem()] * len(arrays),
        out_specs=[vmem()] * 3 + [hbm],
        out_shape=[
            shape_of((rows * chans, width), bf16),
            shape_of((2 * rows, width)),
            shape_of((chans, rows, width)),
            pltpu.HBM((chans, 3 * rows, lane), f32),
        ],
        scratch_shapes=forward_scratch(micros, seqs, chans, peers, width, lane),
        compiler_params=pltpu.CompilerParams(vmem_limit_bytes=16 * 1024 * 1024),
        cost_estimate=cost(5),
        name="mixer_forward",
    )(*arrays)

    act = (
        act.reshape(micros, seqs, chans, parts, own)
        .transpose(0, 3, 1, 2, 4)
        .reshape(peers * seqs, chans, own)
    )
    act = exchange(act, both).reshape(full, own)
    (d_act,) = kernel_call(
        functools.partial(project_kernel, width),
        "project",
        (place, lens),
        (act, *weights),
        [shape_of((full, own), bf16)],
        2,
        limit=12,
        scratch_shapes=[pltpu.VMEM((own, 2 * full), bf16)],
    )

    acts = [act] + [cross(act, k) for k in range(1, peers)]
    if parts == 1:
        order = chan_rank ^ jnp.arange(peers, dtype=jnp.int32)
    else:
        stacked = jnp.stack(acts)[chan_rank ^ jnp.arange(peers, dtype=jnp.int32)]
        stacked = stacked.reshape(micros, parts, full, own).transpose(0, 2, 1, 3)
        stacked = stacked.reshape(micros, full, width)
        acts = [stacked[m] for m in range(micros)]
        order = jnp.arange(micros, dtype=jnp.int32)

    d_act = exchange(d_act.reshape(peers * seqs, chans, own), both)
    d_act = (
        d_act.reshape(micros, parts, seqs, chans, own)
        .transpose(0, 2, 3, 1, 4)
        .reshape(rows * chans, width)
    )
    count = full // seqs
    part = (seqs // 2, 2 * count + 8, wide)
    out, keep, send = kernel_call(
        functools.partial(output_kernel, seqs),
        "output",
        (rank, lens, order),
        (tokens, out_cotangent, w_value, w_gate) + bias_rows + tuple(acts),
        [shape_of(tokens.shape, bf16), shape_of(part), shape_of(part, bf16)],
        2,
        limit=12,
        scratch_shapes=[
            pltpu.VMEM((micros * width, 2 * wide), bf16),
            pltpu.VMEM((seqs,) + part[1:], f32),
        ],
    )
    got = lax.ppermute(send, "seq", [(i, i ^ 1) for i in range(seqs)])
    d_act, keep, *stats = lax.optimization_barrier((d_act, keep, *stats))
    stride = -(-((micros + 3) * chans + 2) // 16) * 16
    arrays = (x_mine, d_act, norm_mine, const, rise, taps, live, y_mine, in_hbm(kept))
    d_hat = pl.pallas_call(
        functools.partial(backward_kernel, micros, seqs, chans),
        in_specs=[vmem()] * (len(arrays) - 1) + [hbm],
        out_specs=vmem(),
        out_shape=shape_of((seqs, stride, width), bf16),
        scratch_shapes=backward_scratch(micros, seqs, chans, stride, width, lane),
        compiler_params=pltpu.CompilerParams(vmem_limit_bytes=20 * 1024 * 1024),
        cost_estimate=cost(5),
        name="mixer_backward",
    )(*arrays)
    d_hat, got = lax.optimization_barrier((d_hat, got))
    for level in range(spans):
        by = 1 << level
        if level:
            got = lax.ppermute(send, "seq", [(i, i ^ by) for i in range(seqs)])
        if level == spans - 1:
            break
        half_part = (seqs >> (level + 2),) + part[1:]
        keep, send = kernel_call(
            halve_kernel,
            "halve",
            ((seq_rank.reshape(1) >> (level + 1)) & 1,),
            (keep, got),
            [shape_of(half_part), shape_of(half_part, bf16)],
            1,
            scratch_shapes=[pltpu.VMEM(keep.shape, f32)],
        )
    d_wv, d_wg, d_bv, d_bg = kernel_call(
        last_kernel,
        "last",
        (),
        (keep, got),
        [shape_of((count, wide))] * 2 + [shape_of((1, wide))] * 2,
        1,
    )
    got = exchange(d_hat, "seq")
    own_sums, head, norm = kernel_call(
        sums_kernel,
        "sums",
        (),
        (got, tokens, *stats),
        [
            shape_of((2 * micros, width)),
            shape_of((seqs, stride, width)),
            shape_of((2 * micros, width)),
        ],
        1,
    )
    hat_sums = [own_sums] + [cross(own_sums, k) for k in range(1, peers)]
    mode_grad = shape_of((2, modes, wide))
    d_input, d_b, d_e, d_c, d_skip, d_gain, d_bias = kernel_call(
        final_kernel,
        "final",
        (rank, lens),
        (head, tokens, out_cotangent, norm, *hat_sums),
        [shape_of(tokens.shape)]
        + [mode_grad] * 3
        + [shape_of((1, wide))] * 3,
        2,
    )
    d_b, d_e, d_c = [jnp.transpose(z, (0, 2, 1)) for z in (d_b, d_e, d_c)]
    d_skip, d_gain, d_bias, d_bv, d_bg = [
        z.reshape(wide) for z in (d_skip, d_gain, d_bias, d_bv, d_bg)
    ]
    return (out, d_input, d_gain, d_bias, d_b, d_e, d_c, d_skip, d_wv, d_wg, d_bv, d_bg)


def solution(mesh):
    chan = P("chan")
    modes = P(None, "chan", None)
    table = P("chan", None)
    weight = P(None, "chan")
    rows = P(None, "chan", "seq")
    spread = P("seq", "chan")
    return jax.shard_map(
        shards,
        mesh=mesh,
        in_specs=(
            rows,
            P(),
            chan,
            chan,
            modes,
            modes,
            modes,
            chan,
            table,
            table,
            weight,
            weight,
            chan,
            chan,
            rows,
        ),
        out_specs=(
            rows,
            rows,
            chan,
            chan,
            modes,
            modes,
            modes,
            chan,
            spread,
            spread,
            chan,
            chan,
        ),
        check_vma=False,
    )
```

```python
import functools
import math

import jax
import jax.numpy as jnp
from jax import lax
from jax.experimental import pallas as pl
from jax.experimental.pallas import tpu as pltpu
from jax.sharding import PartitionSpec as P

f32 = jnp.float32
bf16 = jnp.bfloat16
epsilon = 1e-05
NN = (((1,), (0,)), ((), ()))
NT = (((1,), (1,)), ((), ()))
TN = (((0,), (0,)), ((), ()))


def mm(left, right, dims=NN):
    return lax.dot_general(left, right, dims, preferred_element_type=f32)


def split(x):
    high = x.astype(bf16)
    return high, (x - high.astype(f32)).astype(bf16)


def swap(x, half):
    return pltpu.roll(x, half, axis=x.ndim - 1)


def lanes(shape):
    return lax.broadcasted_iota(jnp.int32, shape, len(shape) - 1)


def pair(z, half):
    low = lanes(z.shape) < half
    turned = swap(z, half)
    return jnp.where(low, z, turned), jnp.where(low, -turned, z)


def cmul(x, z, half):
    return x * z[0] + swap(x, half) * z[1]


def normal_cdf(y):
    return 0.5 * (1.0 + lax.erf(y * (1.0 / math.sqrt(2.0))))


def mirror(width):
    shape = (width, width)
    at = lanes(shape) + lax.broadcasted_iota(jnp.int32, shape, 0)
    return (at == width - 1).astype(f32).astype(bf16)


def live_rows(lens_ref, micros, chunks, width):
    shape = (chunks, width)
    at = lax.broadcasted_iota(jnp.int32, shape, 0) * width + (width - 1 - lanes(shape))
    rows = [(at < lens_ref[m]).astype(f32) for m in range(micros)]
    return jnp.concatenate(rows, axis=0)


def merge(means, squares, count):
    parts = len(means)
    mean = sum(means[1:], means[0]) * (1.0 / parts)
    square = sum(squares[1:], squares[0])
    for part in means:
        square = square + count * jnp.square(part - mean)
    return mean, lax.rsqrt(square * (1.0 / (parts * count)) + epsilon)


def fetch(copies):
    for copy in copies:
        copy.start()


def shift_chunks(x, by, micros, chunks):
    cube = x.reshape(micros, chunks, x.shape[-1])
    place = lax.broadcasted_iota(jnp.int32, cube.shape, 1)
    if by > 0:
        moved = jnp.where(place >= by, pltpu.roll(cube, by, axis=1), 0.0)
    else:
        moved = jnp.where(place < chunks + by, pltpu.roll(cube, chunks + by, axis=1), 0.0)
    return moved.reshape(x.shape)


def previous(u, micros, chunks):
    width = u.shape[1]
    turned = pltpu.roll(u, width - 1, axis=1)
    return jnp.where(
        lanes(u.shape) == width - 1, shift_chunks(turned, 1, micros, chunks), turned
    )


def following(u, micros, chunks):
    turned = pltpu.roll(u, 1, axis=1)
    return jnp.where(lanes(u.shape) == 0, shift_chunks(turned, -1, micros, chunks), turned)


def hankel(first, width):
    blocks = []
    for k in range(width // 8):
        by = width - 8 - 8 * k
        blocks.append(pltpu.roll(first, by, axis=1) if by else first)
    table = jnp.concatenate(blocks, axis=0)
    at = lanes(table.shape) + lax.broadcasted_iota(jnp.int32, table.shape, 0)
    return split(jnp.where(at >= width - 1, table, 0.0))


def gather_kernel(rank_ref, bv_ref, bg_ref, cot_hbm, wv_hbm, wg_hbm, *refs):
    outs, sems = refs[:-1], refs[-1]
    peers, wide, _ = cot_hbm.shape
    full = wv_hbm.shape[0]
    copies = []
    for k, out in enumerate(outs):
        for source, start, count in (
            (cot_hbm.at[rank_ref[0] ^ k], 0, wide),
            (wv_hbm, wide, full),
            (wg_hbm, wide + full, full),
        ):
            copies.append(
                pltpu.make_async_copy(
                    source, out.at[pl.ds(start, count), :], sems.at[len(copies)]
                )
            )
    fetch(copies)
    pieces = []
    for value in (bv_ref[...], bg_ref[...]):
        for _ in range(3):
            high = value.astype(bf16).astype(f32)
            pieces.append(high)
            value = value - high
    pieces.append(jnp.zeros((10, wide), f32))
    biases = jnp.concatenate(pieces, axis=0).astype(bf16)
    for out in outs:
        out[pl.ds(wide + 2 * full, 16), :] = biases
    for copy in copies:
        copy.wait()


def pack_kernel(seqs, tokens_hbm, send_ref, stats_ref, tokens, sems):
    micros, wide, width = tokens.shape
    chans = wide // seqs
    copies = [
        pltpu.make_async_copy(tokens_hbm.at[m], tokens.at[m], sems.at[m]) for m in range(micros)
    ]
    fetch(copies)
    turn = mirror(width)
    means, squares = [], []
    for m in range(micros):
        copies[m].wait()
        x = tokens[m].astype(f32)
        mean = jnp.sum(x, axis=0, keepdims=True) * (1.0 / wide)
        means.append(mean)
        squares.append(jnp.sum(jnp.square(x - mean), axis=0, keepdims=True))
        turned = mm(tokens[m], turn).astype(bf16)
        send_ref[:, pl.ds(m * chans, chans), :] = turned.reshape(seqs, chans, width)
    stats = jnp.concatenate(means + squares, axis=0)
    stats_ref[...] = stats
    high = stats.astype(bf16).astype(f32)
    tail = jnp.concatenate([high, stats - high], axis=0).astype(bf16)
    tail = mm(tail, turn).astype(bf16)
    for k in range(seqs):
        send_ref[k, pl.ds(micros * chans, 4 * micros), :] = tail


def table_kernel(
    chans,
    seqs,
    width,
    rank_ref,
    lens_ref,
    skip_ref,
    gain_ref,
    bias_ref,
    b_hbm,
    e_hbm,
    c_hbm,
    decay_hbm,
    turn_hbm,
    const_ref,
    rise,
    taps_ref,
    live_ref,
    b_ref,
    e_ref,
    c_ref,
    decay_ref,
    turn_ref,
    turned_keep,
    coefs,
    sems,
):
    half = decay_ref.shape[0]
    loads = [
        pltpu.make_async_copy(source, target, sems.at[k])
        for k, (source, target) in enumerate(
            (
                (b_hbm, b_ref),
                (e_hbm, e_ref),
                (c_hbm, c_ref),
                (decay_hbm, decay_ref),
                (turn_hbm, turn_ref),
            )
        )
    ]
    fetch(loads)
    for load in loads:
        load.wait()
    base = rank_ref[0] * chans
    levels = int(math.log2(width)) - 3
    spans = int(math.log2(seqs))

    def own(value):
        turned_keep[...] = value.T
        return turned_keep[pl.ds(base, chans), :]

    b = own(b_ref[...].reshape(2 * half, -1))
    e = own(e_ref[...].reshape(2 * half, -1))
    c = own(c_ref[...].reshape(2 * half, -1))
    mixed = own(jnp.concatenate([decay_ref[...], turn_ref[...]], axis=0))
    low = lanes(mixed.shape) < half
    other = swap(mixed, half)
    decay = jnp.where(low, mixed, other)
    turn = jnp.where(low, other, mixed)
    turned = jnp.where(low, jnp.cos(turn), jnp.sin(turn))
    a = jnp.exp(-decay) * turned
    inverse = pair(jnp.exp(decay) * jnp.where(low, turned, -turned), half)
    a_pair = pair(a, half)
    power = jnp.where(low, 1.0, 0.0)
    for k in range(8):
        rise[pl.ds(k * chans, chans), :] = power
        power = cmul(power, a_pair, half) if k else a
    for k in range(levels):
        power_pair = pair(power, half)
        rise[pl.ds((8 + 2 * k) * chans, chans), :] = power_pair[0]
        rise[pl.ds((9 + 2 * k) * chans, chans), :] = power_pair[1]
        power = cmul(power, power_pair, half)
    kept = [pair(b, half), pair(e, half), pair(cmul(a, pair(c, half), half), half)]
    for k in range(spans):
        kept.append(pair(power, half))
        power = cmul(power, kept[-1], half)
    kept += [pair(c, half), a_pair]
    for k, both in enumerate(kept):
        const_ref[2 * k] = both[0]
        const_ref[2 * k + 1] = both[1]
    sign = jnp.where(low, 1.0, -1.0)
    for j in range(2):
        coef = cmul(c, kept[j], half)
        for k in range(7, -1, -1):
            coefs[pl.ds((8 * j + k) * chans, chans), :] = coef * sign
            coef = cmul(coef, inverse, half)

    live_ref[...] = live_rows(lens_ref, lens_ref.shape[0], seqs, width)
    for channel in range(chans):
        for k, ref in enumerate((gain_ref, bias_ref)):
            const_ref[2 * len(kept) + k, channel : channel + 1, :] = jnp.full(
                (1, 2 * half), ref[base + channel], f32
            )
        high, low_part = mode_powers(rise, channel, chans, levels, half)
        coef = coefs[pl.ds(channel, 16, stride=chans), :]
        coef_hi = coef.astype(bf16).astype(f32)
        both = jnp.concatenate([coef_hi, coef - coef_hi], axis=0).astype(bf16)
        taps = mm(both, high, NT) + mm(both, low_part, NT)
        taps = taps[:16] + taps[16:]
        at = lanes(taps.shape) + lax.broadcasted_iota(jnp.int32, taps.shape, 0)
        taps_ref[channel] = taps + jnp.where(at == 7, skip_ref[base + channel], 0.0)


def mode_powers(rise_ref, channel, chans, levels, half):
    up = rise_ref[pl.ds(channel, 8, stride=chans), :]
    for k in range(levels):
        at = (8 + 2 * k) * chans + channel
        by = (rise_ref[at : at + 1, :], rise_ref[at + chans : at + chans + 1, :])
        up = jnp.concatenate([up, cmul(up, by, half)], axis=0)
    return split(up)


def own_rows(keep, at, stride, micros, chunks):
    return jnp.concatenate(
        [keep[pl.ds(at + m, chunks, stride=stride), :] for m in range(micros)], axis=0
    )


def channel_tokens(keep, channel, stride, micros, chunks, chans):
    return jnp.concatenate(
        [keep[pl.ds(m * chans + channel, chunks, stride=stride), :] for m in range(micros)],
        axis=0,
    )


def forward_kernel(
    micros,
    chunks,
    chans,
    peers,
    got_ref,
    const_ref,
    rise_ref,
    taps_ref,
    live_ref,
    *refs,
):
    stats_refs, refs = refs[: peers - 1], refs[peers - 1 :]
    act_ref, norm_ref, y_ref, kept_hbm, act_keep, x_keep, stats_keep = refs[:7]
    parts, wide_parts, sent_parts, kept_ref, power_ref, sem = refs[7:]
    width = got_ref.shape[2]
    half = const_ref.shape[2] // 2
    spans = int(math.log2(chunks))
    rows = micros * chunks
    stride = got_ref.shape[1]
    flip = jnp.where(lanes((1, 2 * half)) < half, 1.0, -1.0)

    def const(channel, k):
        return (
            const_ref[2 * k, channel : channel + 1, :],
            const_ref[2 * k + 1, channel : channel + 1, :],
        )

    live = live_ref[...]
    gain, bias = 2 * (5 + spans), 2 * (5 + spans) + 1
    for k in range(chunks):
        x_keep[pl.ds(k * stride, stride), :] = got_ref[k].astype(f32)
    means, squares = [], []
    for j in range(peers):
        keep, step, at = x_keep, stride, micros * chans
        if j:
            keep, step, at = stats_keep.at[j - 1], 4 * micros, 0
            for k in range(chunks):
                keep[pl.ds(k * step, step), :] = stats_refs[j - 1][k].astype(f32)
        lines = [own_rows(keep, at + q * micros, step, micros, chunks) for q in range(4)]
        means.append(lines[0] + lines[2])
        squares.append(lines[1] + lines[3])
    mean, inverse = merge(means, squares, chans * chunks)
    norm_ref[pl.ds(0, rows), :] = mean
    norm_ref[pl.ds(rows, rows), :] = inverse

    for channel in range(chans):
        x_hat = channel_tokens(x_keep, channel, stride, micros, chunks, chans) - mean
        line = slice(channel, channel + 1)
        u = live * (x_hat * inverse * const_ref[gain, line] + const_ref[bias, line])
        u_hi, u_lo = split(u)
        v_hi, v_lo = split(u * previous(u, micros, chunks))
        for k, part in enumerate((u_hi, v_hi, u_lo, v_lo)):
            parts[channel, k * rows : (k + 1) * rows] = part
        wide_parts[channel, :rows, :width] = u_hi
        wide_parts[channel, :rows, width:] = v_hi
        wide_parts[channel, rows:, :width] = u_lo
        wide_parts[channel, rows:, width:] = v_lo

    levels = int(math.log2(width)) - 3
    for channel in range(chans):
        high, low_part = mode_powers(rise_ref, channel, chans, levels, half)
        power_ref[channel, :width] = high
        power_ref[channel, width:] = low_part

    for channel in range(chans):
        q = mm(parts[channel], power_ref[channel, :width])
        kept_ref[channel, : 2 * rows] = (
            q[: 2 * rows]
            + q[2 * rows :]
            + mm(parts[channel, : 2 * rows], power_ref[channel, width:])
        )

    for channel in range(chans):
        uq, vq = kept_ref[channel, :rows], kept_ref[channel, rows : 2 * rows]
        state = cmul(uq, const(channel, 0), half) + cmul(vq, const(channel, 1), half)
        for k in range(spans):
            moved = shift_chunks(state, 2**k, micros, chunks)
            state = state + cmul(moved, const(channel, 3 + k), half)
        start = shift_chunks(state, 1, micros, chunks)
        kept_ref[channel, 2 * rows :] = start
        high, low_part = split(cmul(start, const(channel, 2), half) * flip)
        sent_parts[channel, :rows] = high
        sent_parts[channel, rows:] = low_part
    store = pltpu.make_async_copy(kept_ref, kept_hbm, sem)
    store.start()

    for channel in range(chans):
        tables = [hankel(taps_ref[channel, 8 * k : 8 * k + 8], width) for k in range(2)]
        both = wide_parts[channel]
        y = mm(both, jnp.concatenate([tables[0][0], tables[1][0]], axis=0))
        low_part = mm(both[:rows], jnp.concatenate([tables[0][1], tables[1][1]], axis=0))
        y_ref[channel] = y[:rows] + y[rows:] + low_part

    for channel in range(chans):
        both = sent_parts[channel]
        cross = mm(both, power_ref[channel, :width], NT)
        y = y_ref[channel] + cross[:rows] + cross[rows:]
        y = y + mm(both[:rows], power_ref[channel, width:], NT)
        y_ref[channel] = y
        act = y * normal_cdf(y)
        for m in range(micros):
            act_keep[pl.ds(m * chunks * chans + channel, chunks, stride=chans), :] = act[
                m * chunks : (m + 1) * chunks
            ]
    act_ref[...] = act_keep[...].astype(bf16)
    store.wait()


def forward_scratch(micros, chunks, chans, peers, width, lane):
    rows = micros * chunks
    return [
        pltpu.VMEM((rows * chans, width), f32),
        pltpu.VMEM((chunks * micros * (chans + 4), width), f32),
        pltpu.VMEM((peers - 1, 4 * rows, width), f32),
        pltpu.VMEM((chans, 4 * rows, width), bf16),
        pltpu.VMEM((chans, 2 * rows, 2 * width), bf16),
        pltpu.VMEM((chans, 2 * rows, lane), bf16),
        pltpu.VMEM((chans, 3 * rows, lane), f32),
        pltpu.VMEM((chans, 2 * width, lane), bf16),
        pltpu.SemaphoreType.DMA(()),
    ]


def backward_kernel(
    micros,
    chunks,
    chans,
    got_ref,
    dact_ref,
    norm_ref,
    const_ref,
    rise_ref,
    taps_ref,
    live_ref,
    y_ref,
    kept_hbm,
    send_ref,
    sums_keep,
    head,
    x_keep,
    dact_keep,
    u_keep,
    prev_keep,
    dy_parts,
    uv_parts,
    yd_keep,
    duv_keep,
    lag_keep,
    adj_keep,
    sent_parts,
    dots,
    power_ref,
    kept_ref,
    sem,
):
    load = pltpu.make_async_copy(kept_hbm, kept_ref, sem)
    load.start()
    width = got_ref.shape[2]
    half = const_ref.shape[2] // 2
    spans = int(math.log2(chunks))
    rows = micros * chunks
    stride = head.shape[0] // chunks
    got_stride = got_ref.shape[1]
    shape = (width, width)
    passed = lanes(shape) <= lax.broadcasted_iota(jnp.int32, shape, 0)
    low = lanes((1, 2 * half)) < half
    flip = jnp.where(low, 1.0, -1.0)
    live = live_ref[...]
    gain, bias = 2 * (5 + spans), 2 * (5 + spans) + 1
    for k in range(chunks):
        x_keep[pl.ds(k * got_stride, got_stride), :] = got_ref[k].astype(f32)
    dact_keep[...] = dact_ref[...].astype(f32)
    mean, inverse = norm_ref[:rows], norm_ref[rows:]

    def x_hat_of(channel):
        x = channel_tokens(x_keep, channel, got_stride, micros, chunks, chans)
        return (x - mean) * inverse

    def const(channel, k):
        return (
            const_ref[2 * k, channel : channel + 1, :],
            const_ref[2 * k + 1, channel : channel + 1, :],
        )

    def total(x):
        return jnp.sum(x, axis=0, keepdims=True)

    for channel in range(chans):
        line = slice(channel, channel + 1)
        u = live * (x_hat_of(channel) * const_ref[gain, line] + const_ref[bias, line])
        u_prev = previous(u, micros, chunks)
        u_keep[channel] = u
        prev_keep[channel] = u_prev
        u_hi, u_lo = split(u)
        v_hi, v_lo = split(u * u_prev)
        for k, (left, right) in enumerate(((u_hi, v_hi), (u_hi, v_hi), (u_lo, v_lo))):
            uv_parts[channel, k * rows : (k + 1) * rows, :width] = left
            uv_parts[channel, k * rows : (k + 1) * rows, width:] = right
        y = y_ref[channel]
        density = jnp.exp(-0.5 * y * y) * (1.0 / math.sqrt(2.0 * math.pi))
        d_y = dact_keep[pl.ds(channel, rows, stride=chans), :] * (normal_cdf(y) + y * density)
        high, low_part = split(d_y)
        dy_parts[channel, :rows] = high
        dy_parts[channel, rows : 2 * rows] = low_part
        dy_parts[channel, 2 * rows :] = high

    for channel in range(chans):
        tables = [hankel(taps_ref[channel, 8 * k : 8 * k + 8], width) for k in range(2)]
        both = dy_parts[channel, : 2 * rows]
        duv = mm(both, jnp.concatenate([tables[0][0], tables[1][0]], axis=1))
        low_part = mm(both[:rows], jnp.concatenate([tables[0][1], tables[1][1]], axis=1))
        duv_keep[channel] = duv[:rows] + duv[rows:] + low_part

    for channel in range(chans):
        outer = mm(dy_parts[channel], uv_parts[channel], TN)
        for k in range(2):
            rolled = pltpu.roll(
                outer[:, k * width : (k + 1) * width], 1, axis=1, stride=1, stride_axis=0
            )
            line = total(jnp.where(passed, rolled, 0.0))
            high = line.astype(bf16).astype(f32)
            lag_keep[channel, k : k + 1, :] = high
            lag_keep[channel, 2 + k : 3 + k, :] = line - high
            if k == 0:
                sums_keep[channel : channel + 1, :] = jnp.where(
                    lanes(line.shape) == 0, line, 0.0
                )

    levels = int(math.log2(width)) - 3
    for channel in range(chans):
        high, low_part = mode_powers(rise_ref, channel, chans, levels, half)
        power_ref[channel, :width] = high
        power_ref[channel, width:] = low_part

    for channel in range(chans):
        both = dy_parts[channel, : 2 * rows]
        yd = mm(both, power_ref[channel, :width])
        low_part = mm(both[:rows], power_ref[channel, width:])
        yd_keep[channel] = yd[:rows] + yd[rows:] + low_part

    for channel in range(chans):
        adj = cmul(yd_keep[channel], const(channel, 2), half)
        for k in range(spans):
            moved = shift_chunks(adj, -(2**k), micros, chunks)
            adj = adj + cmul(moved, const(channel, 3 + k), half)
        adj = shift_chunks(adj, -1, micros, chunks)
        adj_keep[channel] = adj
        sent = jnp.concatenate(
            [cmul(adj, const(channel, 0), half), cmul(adj, const(channel, 1), half)], axis=0
        )
        high, low_part = split(sent * flip)
        sent_parts[channel, : 2 * rows] = high
        sent_parts[channel, 2 * rows :] = low_part

    for channel in range(chans):
        both = sent_parts[channel]
        cross = mm(both, power_ref[channel, :width], NT)
        cross = cross[: 2 * rows] + cross[2 * rows :]
        cross = cross + mm(both[: 2 * rows], power_ref[channel, width:], NT)
        d_v = duv_keep[channel, :, width:] + cross[rows:]
        d_u = duv_keep[channel, :, :width] + cross[:rows] + d_v * prev_keep[channel]
        d_u = d_u + following(d_v * u_keep[channel], micros, chunks)
        d_q = live * d_u
        sums_keep[chans + channel : chans + channel + 1, :] = total(d_q * x_hat_of(channel))
        sums_keep[2 * chans + channel : 2 * chans + channel + 1, :] = total(d_q)
        d_h = d_q * const_ref[gain, channel : channel + 1]
        for m in range(micros):
            head[pl.ds(m * chans + channel, chunks, stride=stride), :] = d_h[
                m * chunks : (m + 1) * chunks
            ]

    load.wait()
    lag_keep[:, 4:, :] = jnp.zeros((chans, 12, width), f32)
    for channel in range(chans):
        lags = lag_keep[channel].astype(bf16)
        tops = mm(lags, power_ref[channel, :width]) + mm(lags, power_ref[channel, width:])
        dots[6, channel : channel + 1, :] = tops[0:1] + tops[2:3]
        dots[7, channel : channel + 1, :] = tops[1:2] + tops[3:4]
        adj, yd = adj_keep[channel], yd_keep[channel]
        adj_swap = swap(adj, half)
        uq, vq, start = [kept_ref[channel, k * rows : (k + 1) * rows] for k in range(3)]
        pairs = ((uq, adj), (uq, adj_swap), (vq, adj), (vq, adj_swap), (start, yd))
        for k, (left, right) in enumerate(pairs + ((start, swap(yd, half)),)):
            dots[k, channel : channel + 1, :] = total(left * right)

    def whole_const(k):
        return const_ref[2 * k], const_ref[2 * k + 1]

    def dot(k):
        same, other = dots[k], dots[k + 1]
        return jnp.where(low, same - swap(same, half), other + swap(other, half))

    top_u, top_v = dots[6], dots[7]
    c = whole_const(3 + spans)
    modes = jnp.concatenate(
        [
            flip * (cmul(top_u, c, half) + dot(0)),
            flip * (cmul(top_v, c, half) + dot(2)),
            flip
            * (
                cmul(top_u, whole_const(0), half)
                + cmul(top_v, whole_const(1), half)
                + cmul(dot(4), whole_const(4 + spans), half)
            ),
        ],
        axis=0,
    )
    sums = jnp.sum(sums_keep[...].T, axis=0, keepdims=True)
    sums_hi = sums.astype(bf16).astype(f32)
    cut = micros * chans
    for k in range(chunks):
        at = k * stride + cut
        head[pl.ds(at, 3 * chans), :] = modes
        head[pl.ds(at + 3 * chans, 1), pl.ds(0, 3 * chans)] = sums_hi
        head[pl.ds(at + 3 * chans + 1, 1), pl.ds(0, 3 * chans)] = sums - sums_hi
        send_ref[k] = head[pl.ds(k * stride, stride), :].astype(bf16)


def backward_scratch(micros, chunks, chans, stride, width, lane):
    rows = micros * chunks
    return [
        pltpu.VMEM((3 * chans, lane), f32),
        pltpu.VMEM((chunks * stride, width), f32),
        pltpu.VMEM((chunks * micros * (chans + 4), width), f32),
        pltpu.VMEM((rows * chans, width), f32),
        pltpu.VMEM((chans, rows, width), f32),
        pltpu.VMEM((chans, rows, width), f32),
        pltpu.VMEM((chans, 3 * rows, width), bf16),
        pltpu.VMEM((chans, 3 * rows, 2 * width), bf16),
        pltpu.VMEM((chans, rows, lane), f32),
        pltpu.VMEM((chans, rows, 2 * width), f32),
        pltpu.VMEM((chans, 16, width), f32),
        pltpu.VMEM((chans, rows, lane), f32),
        pltpu.VMEM((chans, 4 * rows, lane), bf16),
        pltpu.VMEM((8, chans, lane), f32),
        pltpu.VMEM((chans, 2 * width, lane), bf16),
        pltpu.VMEM((chans, 3 * rows, lane), f32),
        pltpu.SemaphoreType.DMA(()),
    ]


def gated(both, bias, g):
    wide = g.shape[1]
    value = both[:, :wide] + bias[:, :wide]
    gate = jax.nn.sigmoid(both[:, wide:] + bias[:, wide:])
    d_value = g * gate
    return value * gate, jnp.concatenate(
        [d_value.astype(bf16), (d_value * value * (1.0 - gate)).astype(bf16)], axis=1
    )


def project_kernel(width, place_ref, lens_ref, act_ref, *refs):
    refs, (dact_ref, d_keep) = refs[:-2], refs[-2:]
    full, rows = act_ref.shape
    peers = len(refs)
    wide = full // peers
    start = place_ref[1] * rows
    at = place_ref[0] * width + lax.rem(start, width)
    at = at + lax.broadcasted_iota(jnp.int32, (rows, wide), 0)
    live = (at < lens_ref[start // width]).astype(f32)
    act = act_ref[...].T

    def weight(ref):
        return jnp.concatenate(
            [ref[wide : wide + full, :], ref[wide + full : wide + 2 * full, :]], axis=1
        )

    for k, ref in enumerate(refs):
        g = live * ref[:wide, :].T.astype(f32)
        bias = ref[wide + 2 * full :, :].astype(f32)
        bias = jnp.concatenate(
            [bias[0:1] + bias[1:2] + bias[2:3], bias[3:4] + bias[4:5] + bias[5:6]], axis=1
        )
        d_both = gated(mm(act, weight(ref)), bias, g)[1]
        d_keep[:, 2 * k * wide : 2 * (k + 1) * wide] = d_both
    weights = jnp.concatenate([weight(ref) for ref in refs], axis=1)
    dact_ref[...] = mm(weights, d_keep[...], NT).astype(bf16)


def output_kernel(
    seqs,
    rank_ref,
    lens_ref,
    order_ref,
    tokens_ref,
    cot_ref,
    wv_ref,
    wg_ref,
    bv_ref,
    bg_ref,
    *refs,
):
    micros, wide, width = tokens_ref.shape
    acts_in, refs = refs[:micros], refs[micros:]
    out_ref, keep_ref, send_refs = refs[0], refs[1], refs[2:-2]
    d_keep, grad = refs[-2:]
    full = wv_ref.shape[0]
    at = rank_ref[0] * width + lax.broadcasted_iota(jnp.int32, (width, wide), 0)
    place = rank_ref[0] * width + lanes((1, width))
    weights = jnp.concatenate([wv_ref[...], wg_ref[...]], axis=1)
    bias = jnp.concatenate([bv_ref[...], bg_ref[...]], axis=1)
    for k in range(micros):
        m = order_ref[k]
        g = (at < lens_ref[m]).astype(f32) * cot_ref[m].T.astype(f32)
        added, d_both = gated(mm(acts_in[k][...].T, weights), bias, g)
        live = (place < lens_ref[m]).astype(f32)
        out_ref[m] = (live * (tokens_ref[m].astype(f32) + added.T)).astype(bf16)
        d_keep[k * width : (k + 1) * width] = d_both
    d_both = d_keep[...]
    acts = jnp.concatenate([ref[...] for ref in acts_in], axis=1)
    grad_w = mm(acts, d_both)
    grad_b = mm(jnp.ones((8, micros * width), bf16), d_both)
    row = lax.broadcasted_iota(jnp.int32, (8, wide), 0)
    small = jnp.where(row == 0, grad_b[:, :wide], grad_b[:, wide:])
    count = full // seqs
    for k in range(seqs):
        part = grad_w[k * count : (k + 1) * count]
        grad[k, pl.ds(0, count), :] = part[:, :wide]
        grad[k, pl.ds(count, count), :] = part[:, wide:]
        grad[k, pl.ds(2 * count, 8), :] = small
    place = rank_ref[0] >> 1
    for j in range(2):
        keep_ref[j] = grad[2 * place + j]
        for k, ref in enumerate(send_refs):
            ref[j] = grad[2 * (place ^ (k + 1)) + j].astype(bf16)


def parts_kernel(bit_ref, keep_in_ref, *refs):
    got_refs, (keep_ref, send_ref, total) = refs[:-3], refs[-3:]
    value = keep_in_ref[...]
    for ref in got_refs:
        value = value + ref[...].astype(f32)
    total[...] = value
    keep_ref[...] = total[bit_ref[0]]
    send_ref[...] = total[1 - bit_ref[0]].astype(bf16)


def last_kernel(left_ref, right_ref, wv_ref, wg_ref, bv_ref, bg_ref):
    count = wv_ref.shape[0]
    total = left_ref[...] + right_ref[...].astype(f32)
    wv_ref[...] = total[:count]
    wg_ref[...] = total[count : 2 * count]
    bv_ref[...] = total[2 * count : 2 * count + 1]
    bg_ref[...] = total[2 * count + 1 : 2 * count + 2]


def normal(tokens_ref, norm_ref, m):
    micros = tokens_ref.shape[0]
    return (tokens_ref[m].astype(f32) - norm_ref[m : m + 1]) * norm_ref[
        micros + m : micros + m + 1
    ]


def sums_kernel(got_ref, tokens_ref, *refs):
    stats_refs, (out_ref, head_ref, norm_ref) = refs[:-3], refs[-3:]
    micros, wide, width = tokens_ref.shape
    seqs, stride, _ = head_ref.shape
    chans = wide // seqs
    mean, inverse = merge(
        [ref[pl.ds(0, micros), :] for ref in stats_refs],
        [ref[pl.ds(micros, micros), :] for ref in stats_refs],
        wide,
    )
    norm_ref[pl.ds(0, micros), :] = mean
    norm_ref[pl.ds(micros, micros), :] = inverse
    cut = micros * chans
    turned = got_ref[:, pl.ds(0, cut), :].reshape(seqs * cut, width)
    head_ref[:, pl.ds(0, cut), :] = mm(turned, mirror(width)).reshape(seqs, cut, width)
    head_ref[:, pl.ds(cut, stride - cut), :] = got_ref[:, pl.ds(cut, stride - cut), :].astype(f32)
    for m in range(micros):
        d_hat = head_ref[:, pl.ds(m * chans, chans), :].reshape(wide, width)
        x_hat = normal(tokens_ref, norm_ref, m)
        out_ref[pl.ds(m, 1), :] = jnp.sum(d_hat, axis=0, keepdims=True)
        out_ref[pl.ds(micros + m, 1), :] = jnp.sum(d_hat * x_hat, axis=0, keepdims=True)


def final_kernel(
    rank_ref,
    lens_ref,
    head_ref,
    tokens_ref,
    cot_ref,
    norm_ref,
    *refs,
):
    hat_refs, refs = refs[:-7], refs[-7:]
    d_in_ref, b_ref, e_ref, c_ref, skip_ref, gain_ref, norm_bias_ref = refs
    micros, wide, width = tokens_ref.shape
    seqs, stride, _ = head_ref.shape
    peers = len(hat_refs)
    chans = wide // seqs
    hats = [ref[...] for ref in hat_refs]
    hat = sum(hats[1:], hats[0]) * (1.0 / (peers * wide))
    at = rank_ref[0] * width + lanes((1, width))
    for m in range(micros):
        live = (at < lens_ref[m]).astype(f32)
        d_hat = head_ref[:, pl.ds(m * chans, chans), :].reshape(wide, width)
        x_hat = normal(tokens_ref, norm_ref, m)
        inside = d_hat - hat[m : m + 1] - x_hat * hat[micros + m : micros + m + 1]
        d_in_ref[m] = (
            live * cot_ref[m].astype(f32) + norm_ref[micros + m : micros + m + 1] * inside
        )
    cut = micros * chans
    for k, ref in enumerate((b_ref, e_ref, c_ref)):
        modes = head_ref[:, pl.ds(cut + k * chans, chans), :]
        ref[...] = modes.reshape(wide, -1).T.reshape(ref.shape)
    place = lanes((1, wide)) // chans
    last = cut + 3 * chans
    for k, ref in enumerate((skip_ref, gain_ref, norm_bias_ref)):
        line = jnp.zeros((1, wide), f32)
        for s in range(seqs):
            own = head_ref[s, pl.ds(last, 1), :] + head_ref[s, pl.ds(last + 1, 1), :]
            own = pltpu.roll(own, (s - k) * chans % own.shape[1], axis=1)[:, :wide]
            line = jnp.where(place == s, own, line)
        ref[...] = line


def smem():
    return pl.BlockSpec(memory_space=pltpu.SMEM)


def vmem():
    return pl.BlockSpec(memory_space=pltpu.VMEM)


def in_hbm(x):
    return pltpu.with_memory_space_constraint(x, pltpu.HBM)


def shape_of(shape, kind=f32):
    return jax.ShapeDtypeStruct(shape, kind)


def kernel_call(kernel, name, scalars, arrays, outs, micros_of_time, limit=8, **more):
    ins = [smem()] * len(scalars) + [vmem()] * len(arrays)
    return pl.pallas_call(
        kernel,
        in_specs=ins,
        out_specs=[vmem()] * len(outs),
        out_shape=outs,
        compiler_params=pltpu.CompilerParams(vmem_limit_bytes=limit * 1024 * 1024),
        cost_estimate=cost(micros_of_time),
        name=name,
        **more,
    )(*scalars, *arrays)


def cost(micros_of_time):
    return pl.CostEstimate(
        flops=int(micros_of_time * 1e9), bytes_accessed=int(micros_of_time * 3e6), transcendentals=0
    )


def shards(
    tokens,
    lengths,
    ln_gain,
    ln_bias,
    b_coef,
    e_coef,
    c_coef,
    skip_gain,
    decay_rate,
    rotation,
    w_value,
    w_gate,
    bias_value,
    bias_gate,
    out_cotangent,
):
    micros, wide, width = tokens.shape
    modes = decay_rate.shape[1]
    full = w_value.shape[0]
    seqs = lax.axis_size("seq")
    peers = lax.axis_size("chan")
    seq_rank = lax.axis_index("seq").astype(jnp.int32)
    chan_rank = lax.axis_index("chan").astype(jnp.int32)
    chans = wide // seqs
    rows = micros * seqs
    own = micros * width // peers
    parts = width // own
    both = ("chan", "seq")
    lane = 2 * modes
    spans = int(math.log2(seqs))
    levels = int(math.log2(width)) - 3
    rank = seq_rank.reshape(1)
    lens = lengths.reshape(micros)
    place = jnp.stack([seq_rank, chan_rank])
    bias_rows = (bias_value.reshape(1, wide), bias_gate.reshape(1, wide))

    def exchange(x, axis):
        return lax.all_to_all(x, axis, 0, 0, tiled=True)

    def cross(x, by):
        return lax.ppermute(x, "chan", [(i, i ^ by) for i in range(peers)])

    hbm = pl.BlockSpec(memory_space=pltpu.HBM)
    x_send, part_stats = pl.pallas_call(
        functools.partial(pack_kernel, seqs),
        in_specs=[hbm],
        out_specs=[vmem()] * 2,
        out_shape=[
            shape_of((seqs, micros * (chans + 4), width), bf16),
            shape_of((2 * micros, width)),
        ],
        scratch_shapes=[
            pltpu.VMEM(tokens.shape, bf16),
            pltpu.SemaphoreType.DMA((micros,)),
        ],
        compiler_params=pltpu.CompilerParams(vmem_limit_bytes=8 * 1024 * 1024),
        cost_estimate=cost(1),
        name="pack",
    )(in_hbm(tokens))
    x_mine = exchange(x_send, "seq")
    stats = [part_stats] + [cross(part_stats, k) for k in range(1, peers)]

    cot, wv, wg, _ = lax.optimization_barrier((out_cotangent, w_value, w_gate, part_stats))
    cot_own = cot.reshape(micros, wide, parts, own).transpose(0, 2, 1, 3).reshape(peers, wide, own)
    weights = pl.pallas_call(
        gather_kernel,
        in_specs=[smem()] + [vmem()] * 2 + [hbm] * 3,
        out_specs=[vmem()] * peers,
        out_shape=[shape_of((wide + 2 * full + 16, own), bf16)] * peers,
        scratch_shapes=[pltpu.SemaphoreType.DMA((3 * peers,))],
        compiler_params=pltpu.CompilerParams(vmem_limit_bytes=8 * 1024 * 1024),
        cost_estimate=cost(1),
        name="weights",
    )(chan_rank.reshape(1), *bias_rows, in_hbm(cot_own), in_hbm(wv), in_hbm(wg))

    turned = [jnp.transpose(z, (0, 2, 1)) for z in (b_coef, e_coef, c_coef)]
    const, rise, taps, live = pl.pallas_call(
        functools.partial(table_kernel, chans, seqs, width),
        in_specs=[smem()] * 5 + [hbm] * 5,
        out_specs=[vmem()] * 4,
        out_shape=[
            shape_of((12 + 2 * spans, chans, lane)),
            shape_of(((8 + 2 * levels) * chans, lane)),
            shape_of((chans, 16, width)),
            shape_of((rows, width)),
        ],
        scratch_shapes=[pltpu.VMEM(turned[0].shape, f32)] * 3
        + [pltpu.VMEM((modes, wide), f32)] * 2
        + [
            pltpu.VMEM((wide, lane), f32),
            pltpu.VMEM((16 * chans, lane), f32),
            pltpu.SemaphoreType.DMA((5,)),
        ],
        compiler_params=pltpu.CompilerParams(vmem_limit_bytes=8 * 1024 * 1024),
        cost_estimate=cost(2),
        name="tables",
    )(rank, lens, skip_gain, ln_gain, ln_bias, *[in_hbm(z) for z in (*turned, decay_rate.T, rotation.T)])

    x_mine, const, weights = lax.optimization_barrier((x_mine, const, weights))
    x_stats = x_mine[:, micros * chans :]
    x_stats = [cross(x_stats, k) for k in range(1, peers)]
    weights = [weights[0]] + [cross(weights[k], k) for k in range(1, peers)]
    arrays = (x_mine, const, rise, taps, live, *x_stats)
    act, norm_mine, y_mine, kept = pl.pallas_call(
        functools.partial(forward_kernel, micros, seqs, chans, peers),
        in_specs=[vmem()] * len(arrays),
        out_specs=[vmem()] * 3 + [hbm],
        out_shape=[
            shape_of((rows * chans, width), bf16),
            shape_of((2 * rows, width)),
            shape_of((chans, rows, width)),
            pltpu.HBM((chans, 3 * rows, lane), f32),
        ],
        scratch_shapes=forward_scratch(micros, seqs, chans, peers, width, lane),
        compiler_params=pltpu.CompilerParams(vmem_limit_bytes=16 * 1024 * 1024),
        cost_estimate=cost(5),
        name="mixer_forward",
    )(*arrays)

    act = (
        act.reshape(micros, seqs, chans, parts, own)
        .transpose(0, 3, 1, 2, 4)
        .reshape(peers * seqs, chans, own)
    )
    act = exchange(act, both).reshape(full, own)
    (d_act,) = kernel_call(
        functools.partial(project_kernel, width),
        "project",
        (place, lens),
        (act, *weights),
        [shape_of((full, own), bf16)],
        2,
        limit=12,
        scratch_shapes=[pltpu.VMEM((own, 2 * full), bf16)],
    )

    acts = [act] + [cross(act, k) for k in range(1, peers)]
    if parts == 1:
        order = chan_rank ^ jnp.arange(peers, dtype=jnp.int32)
    else:
        stacked = jnp.stack(acts)[chan_rank ^ jnp.arange(peers, dtype=jnp.int32)]
        stacked = stacked.reshape(micros, parts, full, own).transpose(0, 2, 1, 3)
        stacked = stacked.reshape(micros, full, width)
        acts = [stacked[m] for m in range(micros)]
        order = jnp.arange(micros, dtype=jnp.int32)

    d_act = exchange(d_act.reshape(peers * seqs, chans, own), both)
    d_act = (
        d_act.reshape(micros, parts, seqs, chans, own)
        .transpose(0, 2, 3, 1, 4)
        .reshape(rows * chans, width)
    )
    count = full // seqs
    part = (2, 2 * count + 8, wide)
    out, keep, *blocks = kernel_call(
        functools.partial(output_kernel, seqs),
        "output",
        (rank, lens, order),
        (tokens, out_cotangent, w_value, w_gate) + bias_rows + tuple(acts),
        [shape_of(tokens.shape, bf16), shape_of(part)] + [shape_of(part, bf16)] * (seqs // 2 - 1),
        2,
        limit=12,
        scratch_shapes=[
            pltpu.VMEM((micros * width, 2 * wide), bf16),
            pltpu.VMEM((seqs,) + part[1:], f32),
        ],
    )
    blocks = [
        lax.ppermute(block, "seq", [(i, i ^ ((k + 1) << 1)) for i in range(seqs)])
        for k, block in enumerate(blocks)
    ]
    d_act, keep, *stats = lax.optimization_barrier((d_act, keep, *stats))
    stride = -(-((micros + 3) * chans + 2) // 16) * 16
    arrays = (x_mine, d_act, norm_mine, const, rise, taps, live, y_mine, in_hbm(kept))
    d_hat = pl.pallas_call(
        functools.partial(backward_kernel, micros, seqs, chans),
        in_specs=[vmem()] * (len(arrays) - 1) + [hbm],
        out_specs=vmem(),
        out_shape=shape_of((seqs, stride, width), bf16),
        scratch_shapes=backward_scratch(micros, seqs, chans, stride, width, lane),
        compiler_params=pltpu.CompilerParams(vmem_limit_bytes=20 * 1024 * 1024),
        cost_estimate=cost(5),
        name="mixer_backward",
    )(*arrays)
    d_hat, *blocks = lax.optimization_barrier((d_hat, *blocks))
    keep, send = kernel_call(
        parts_kernel,
        "parts",
        (seq_rank.reshape(1) & 1,),
        (keep, *blocks),
        [shape_of(part[1:]), shape_of(part[1:], bf16)],
        1,
        scratch_shapes=[pltpu.VMEM(part, f32)],
    )
    got = lax.ppermute(send, "seq", [(i, i ^ 1) for i in range(seqs)])
    d_wv, d_wg, d_bv, d_bg = kernel_call(
        last_kernel,
        "last",
        (),
        (keep, got),
        [shape_of((count, wide))] * 2 + [shape_of((1, wide))] * 2,
        1,
    )
    got = exchange(d_hat, "seq")
    own_sums, head, norm = kernel_call(
        sums_kernel,
        "sums",
        (),
        (got, tokens, *stats),
        [
            shape_of((2 * micros, width)),
            shape_of((seqs, stride, width)),
            shape_of((2 * micros, width)),
        ],
        1,
    )
    hat_sums = [own_sums] + [cross(own_sums, k) for k in range(1, peers)]
    mode_grad = shape_of((2, modes, wide))
    d_input, d_b, d_e, d_c, d_skip, d_gain, d_bias = kernel_call(
        final_kernel,
        "final",
        (rank, lens),
        (head, tokens, out_cotangent, norm, *hat_sums),
        [shape_of(tokens.shape)]
        + [mode_grad] * 3
        + [shape_of((1, wide))] * 3,
        2,
    )
    d_b, d_e, d_c = [jnp.transpose(z, (0, 2, 1)) for z in (d_b, d_e, d_c)]
    d_skip, d_gain, d_bias, d_bv, d_bg = [
        z.reshape(wide) for z in (d_skip, d_gain, d_bias, d_bv, d_bg)
    ]
    return (out, d_input, d_gain, d_bias, d_b, d_e, d_c, d_skip, d_wv, d_wg, d_bv, d_bg)


def solution(mesh):
    chan = P("chan")
    modes = P(None, "chan", None)
    table = P("chan", None)
    weight = P(None, "chan")
    rows = P(None, "chan", "seq")
    spread = P("seq", "chan")
    return jax.shard_map(
        shards,
        mesh=mesh,
        in_specs=(
            rows,
            P(),
            chan,
            chan,
            modes,
            modes,
            modes,
            chan,
            table,
            table,
            weight,
            weight,
            chan,
            chan,
            rows,
        ),
        out_specs=(
            rows,
            rows,
            chan,
            chan,
            modes,
            modes,
            modes,
            chan,
            spread,
            spread,
            chan,
            chan,
        ),
        check_vma=False,
    )
```

```python
import functools
import math

import jax
import jax.numpy as jnp
from jax import lax
from jax.experimental import pallas as pl
from jax.experimental.pallas import tpu as pltpu
from jax.sharding import PartitionSpec as P

f32 = jnp.float32
bf16 = jnp.bfloat16
epsilon = 1e-05
NN = (((1,), (0,)), ((), ()))
NT = (((1,), (1,)), ((), ()))
TN = (((0,), (0,)), ((), ()))


def mm(left, right, dims=NN):
    return lax.dot_general(left, right, dims, preferred_element_type=f32)


def split(x):
    high = x.astype(bf16)
    return high, (x - high.astype(f32)).astype(bf16)


def swap(x, half):
    return pltpu.roll(x, half, axis=x.ndim - 1)


def lanes(shape):
    return lax.broadcasted_iota(jnp.int32, shape, len(shape) - 1)


def pair(z, half):
    low = lanes(z.shape) < half
    turned = swap(z, half)
    return jnp.where(low, z, turned), jnp.where(low, -turned, z)


def cmul(x, z, half):
    return x * z[0] + swap(x, half) * z[1]


def normal_cdf(y):
    return 0.5 * (1.0 + lax.erf(y * (1.0 / math.sqrt(2.0))))


def mirror(width):
    shape = (width, width)
    at = lanes(shape) + lax.broadcasted_iota(jnp.int32, shape, 0)
    return (at == width - 1).astype(f32).astype(bf16)


def live_rows(lens_ref, micros, chunks, width):
    shape = (chunks, width)
    at = lax.broadcasted_iota(jnp.int32, shape, 0) * width + (width - 1 - lanes(shape))
    rows = [(at < lens_ref[m]).astype(f32) for m in range(micros)]
    return jnp.concatenate(rows, axis=0)


def merge(means, squares, count):
    parts = len(means)
    mean = sum(means[1:], means[0]) * (1.0 / parts)
    square = sum(squares[1:], squares[0])
    for part in means:
        square = square + count * jnp.square(part - mean)
    return mean, lax.rsqrt(square * (1.0 / (parts * count)) + epsilon)


def fetch(copies):
    for copy in copies:
        copy.start()


def shift_chunks(x, by, micros, chunks):
    cube = x.reshape(micros, chunks, x.shape[-1])
    place = lax.broadcasted_iota(jnp.int32, cube.shape, 1)
    if by > 0:
        moved = jnp.where(place >= by, pltpu.roll(cube, by, axis=1), 0.0)
    else:
        moved = jnp.where(place < chunks + by, pltpu.roll(cube, chunks + by, axis=1), 0.0)
    return moved.reshape(x.shape)


def previous(u, micros, chunks):
    width = u.shape[1]
    turned = pltpu.roll(u, width - 1, axis=1)
    return jnp.where(
        lanes(u.shape) == width - 1, shift_chunks(turned, 1, micros, chunks), turned
    )


def following(u, micros, chunks):
    turned = pltpu.roll(u, 1, axis=1)
    return jnp.where(lanes(u.shape) == 0, shift_chunks(turned, -1, micros, chunks), turned)


def hankel(first, width):
    blocks = []
    for k in range(width // 8):
        by = width - 8 - 8 * k
        blocks.append(pltpu.roll(first, by, axis=1) if by else first)
    table = jnp.concatenate(blocks, axis=0)
    at = lanes(table.shape) + lax.broadcasted_iota(jnp.int32, table.shape, 0)
    return split(jnp.where(at >= width - 1, table, 0.0))


def gather_kernel(rank_ref, bv_ref, bg_ref, cot_hbm, wv_hbm, wg_hbm, *refs):
    outs, sems = refs[:-1], refs[-1]
    peers, wide, _ = cot_hbm.shape
    full = wv_hbm.shape[0]
    copies = []
    for k, out in enumerate(outs):
        for source, start, count in (
            (cot_hbm.at[rank_ref[0] ^ k], 0, wide),
            (wv_hbm, wide, full),
            (wg_hbm, wide + full, full),
        ):
            copies.append(
                pltpu.make_async_copy(
                    source, out.at[pl.ds(start, count), :], sems.at[len(copies)]
                )
            )
    fetch(copies)
    pieces = []
    for value in (bv_ref[...], bg_ref[...]):
        for _ in range(3):
            high = value.astype(bf16).astype(f32)
            pieces.append(high)
            value = value - high
    pieces.append(jnp.zeros((10, wide), f32))
    biases = jnp.concatenate(pieces, axis=0).astype(bf16)
    for out in outs:
        out[pl.ds(wide + 2 * full, 16), :] = biases
    for copy in copies:
        copy.wait()


def pack_kernel(seqs, tokens_hbm, send_ref, stats_ref, tokens, sems):
    micros, wide, width = tokens.shape
    chans = wide // seqs
    copies = [
        pltpu.make_async_copy(tokens_hbm.at[m], tokens.at[m], sems.at[m]) for m in range(micros)
    ]
    fetch(copies)
    turn = mirror(width)
    means, squares = [], []
    for copy in copies:
        copy.wait()
    for m in range(micros):
        x = tokens[m].astype(f32)
        mean = jnp.sum(x, axis=0, keepdims=True) * (1.0 / wide)
        means.append(mean)
        squares.append(jnp.sum(jnp.square(x - mean), axis=0, keepdims=True))
        turned = mm(tokens[m], turn).astype(bf16)
        send_ref[:, pl.ds(m * chans, chans), :] = turned.reshape(seqs, chans, width)
    stats = jnp.concatenate(means + squares, axis=0)
    stats_ref[...] = stats
    high = stats.astype(bf16).astype(f32)
    tail = jnp.concatenate([high, stats - high], axis=0).astype(bf16)
    tail = mm(tail, turn).astype(bf16)
    for k in range(seqs):
        send_ref[k, pl.ds(micros * chans, 4 * micros), :] = tail


def table_kernel(
    chans,
    seqs,
    width,
    rank_ref,
    lens_ref,
    skip_ref,
    gain_ref,
    bias_ref,
    b_hbm,
    e_hbm,
    c_hbm,
    decay_hbm,
    turn_hbm,
    const_ref,
    rise,
    taps_ref,
    live_ref,
    b_ref,
    e_ref,
    c_ref,
    decay_ref,
    turn_ref,
    turned_keep,
    coefs,
    sems,
):
    half = decay_ref.shape[0]
    loads = [
        pltpu.make_async_copy(source, target, sems.at[k])
        for k, (source, target) in enumerate(
            (
                (b_hbm, b_ref),
                (e_hbm, e_ref),
                (c_hbm, c_ref),
                (decay_hbm, decay_ref),
                (turn_hbm, turn_ref),
            )
        )
    ]
    fetch(loads)
    for load in loads:
        load.wait()
    base = rank_ref[0] * chans
    levels = int(math.log2(width)) - 3
    spans = int(math.log2(seqs))

    def own(value):
        turned_keep[...] = value.T
        return turned_keep[pl.ds(base, chans), :]

    b = own(b_ref[...].reshape(2 * half, -1))
    e = own(e_ref[...].reshape(2 * half, -1))
    c = own(c_ref[...].reshape(2 * half, -1))
    mixed = own(jnp.concatenate([decay_ref[...], turn_ref[...]], axis=0))
    low = lanes(mixed.shape) < half
    other = swap(mixed, half)
    decay = jnp.where(low, mixed, other)
    turn = jnp.where(low, other, mixed)
    turned = jnp.where(low, jnp.cos(turn), jnp.sin(turn))
    a = jnp.exp(-decay) * turned
    inverse = pair(jnp.exp(decay) * jnp.where(low, turned, -turned), half)
    a_pair = pair(a, half)
    power = jnp.where(low, 1.0, 0.0)
    for k in range(8):
        rise[pl.ds(k * chans, chans), :] = power
        power = cmul(power, a_pair, half) if k else a
    for k in range(levels):
        power_pair = pair(power, half)
        rise[pl.ds((8 + 2 * k) * chans, chans), :] = power_pair[0]
        rise[pl.ds((9 + 2 * k) * chans, chans), :] = power_pair[1]
        power = cmul(power, power_pair, half)
    kept = [pair(b, half), pair(e, half), pair(cmul(a, pair(c, half), half), half)]
    for k in range(spans):
        kept.append(pair(power, half))
        power = cmul(power, kept[-1], half)
    kept += [pair(c, half), a_pair]
    for k, both in enumerate(kept):
        const_ref[2 * k] = both[0]
        const_ref[2 * k + 1] = both[1]
    sign = jnp.where(low, 1.0, -1.0)
    for j in range(2):
        coef = cmul(c, kept[j], half)
        for k in range(7, -1, -1):
            coefs[pl.ds((8 * j + k) * chans, chans), :] = coef * sign
            coef = cmul(coef, inverse, half)

    live_ref[...] = live_rows(lens_ref, lens_ref.shape[0], seqs, width)
    for channel in range(chans):
        for k, ref in enumerate((gain_ref, bias_ref)):
            const_ref[2 * len(kept) + k, channel : channel + 1, :] = jnp.full(
                (1, 2 * half), ref[base + channel], f32
            )
        high, low_part = mode_powers(rise, channel, chans, levels, half)
        coef = coefs[pl.ds(channel, 16, stride=chans), :]
        coef_hi = coef.astype(bf16).astype(f32)
        both = jnp.concatenate([coef_hi, coef - coef_hi], axis=0).astype(bf16)
        taps = mm(both, high, NT) + mm(both, low_part, NT)
        taps = taps[:16] + taps[16:]
        at = lanes(taps.shape) + lax.broadcasted_iota(jnp.int32, taps.shape, 0)
        taps_ref[channel] = taps + jnp.where(at == 7, skip_ref[base + channel], 0.0)


def mode_powers(rise_ref, channel, chans, levels, half):
    up = rise_ref[pl.ds(channel, 8, stride=chans), :]
    for k in range(levels):
        at = (8 + 2 * k) * chans + channel
        by = (rise_ref[at : at + 1, :], rise_ref[at + chans : at + chans + 1, :])
        up = jnp.concatenate([up, cmul(up, by, half)], axis=0)
    return split(up)


def own_rows(keep, at, stride, micros, chunks):
    return jnp.concatenate(
        [keep[pl.ds(at + m, chunks, stride=stride), :] for m in range(micros)], axis=0
    )


def channel_tokens(keep, channel, stride, micros, chunks, chans):
    return jnp.concatenate(
        [keep[pl.ds(m * chans + channel, chunks, stride=stride), :] for m in range(micros)],
        axis=0,
    )


def forward_kernel(
    micros,
    chunks,
    chans,
    peers,
    got_ref,
    const_ref,
    rise_ref,
    taps_ref,
    live_ref,
    *refs,
):
    stats_refs, refs = refs[: peers - 1], refs[peers - 1 :]
    act_ref, norm_ref, y_ref, start_ref, act_keep, x_keep, stats_keep = refs[:7]
    parts, wide_parts, sent_parts, kept_ref, power_ref = refs[7:]
    width = got_ref.shape[2]
    half = const_ref.shape[2] // 2
    spans = int(math.log2(chunks))
    rows = micros * chunks
    stride = got_ref.shape[1]
    flip = jnp.where(lanes((1, 2 * half)) < half, 1.0, -1.0)

    def const(channel, k):
        return (
            const_ref[2 * k, channel : channel + 1, :],
            const_ref[2 * k + 1, channel : channel + 1, :],
        )

    live = live_ref[...]
    gain, bias = 2 * (5 + spans), 2 * (5 + spans) + 1
    for k in range(chunks):
        x_keep[pl.ds(k * stride, stride), :] = got_ref[k].astype(f32)
    means, squares = [], []
    for j in range(peers):
        keep, step, at = x_keep, stride, micros * chans
        if j:
            keep, step, at = stats_keep.at[j - 1], 4 * micros, 0
            for k in range(chunks):
                keep[pl.ds(k * step, step), :] = stats_refs[j - 1][k].astype(f32)
        lines = [own_rows(keep, at + q * micros, step, micros, chunks) for q in range(4)]
        means.append(lines[0] + lines[2])
        squares.append(lines[1] + lines[3])
    mean, inverse = merge(means, squares, chans * chunks)
    norm_ref[pl.ds(0, rows), :] = mean
    norm_ref[pl.ds(rows, rows), :] = inverse

    for channel in range(chans):
        x_hat = channel_tokens(x_keep, channel, stride, micros, chunks, chans) - mean
        line = slice(channel, channel + 1)
        u = live * (x_hat * inverse * const_ref[gain, line] + const_ref[bias, line])
        u_hi, u_lo = split(u)
        v_hi, v_lo = split(u * previous(u, micros, chunks))
        for k, part in enumerate((u_hi, v_hi, u_lo, v_lo)):
            parts[channel, k * rows : (k + 1) * rows] = part
        wide_parts[channel, :rows, :width] = u_hi
        wide_parts[channel, :rows, width:] = v_hi
        wide_parts[channel, rows:, :width] = u_lo
        wide_parts[channel, rows:, width:] = v_lo

    levels = int(math.log2(width)) - 3
    for channel in range(chans):
        high, low_part = mode_powers(rise_ref, channel, chans, levels, half)
        power_ref[channel, :width] = high
        power_ref[channel, width:] = low_part

    for channel in range(chans):
        q = mm(parts[channel], power_ref[channel, :width])
        kept_ref[channel, : 2 * rows] = (
            q[: 2 * rows]
            + q[2 * rows :]
            + mm(parts[channel, : 2 * rows], power_ref[channel, width:])
        )

    for channel in range(chans):
        uq, vq = kept_ref[channel, :rows], kept_ref[channel, rows : 2 * rows]
        state = cmul(uq, const(channel, 0), half) + cmul(vq, const(channel, 1), half)
        for k in range(spans):
            moved = shift_chunks(state, 2**k, micros, chunks)
            state = state + cmul(moved, const(channel, 3 + k), half)
        start = shift_chunks(state, 1, micros, chunks)
        start_ref[channel] = start
        high, low_part = split(cmul(start, const(channel, 2), half) * flip)
        sent_parts[channel, :rows] = high
        sent_parts[channel, rows:] = low_part

    for channel in range(chans):
        tables = [hankel(taps_ref[channel, 8 * k : 8 * k + 8], width) for k in range(2)]
        both = wide_parts[channel]
        y = mm(both, jnp.concatenate([tables[0][0], tables[1][0]], axis=0))
        low_part = mm(both[:rows], jnp.concatenate([tables[0][1], tables[1][1]], axis=0))
        y_ref[channel] = y[:rows] + y[rows:] + low_part

    for channel in range(chans):
        both = sent_parts[channel]
        cross = mm(both, power_ref[channel, :width], NT)
        y = y_ref[channel] + cross[:rows] + cross[rows:]
        y = y + mm(both[:rows], power_ref[channel, width:], NT)
        y_ref[channel] = y
        act = y * normal_cdf(y)
        for m in range(micros):
            act_keep[pl.ds(m * chunks * chans + channel, chunks, stride=chans), :] = act[
                m * chunks : (m + 1) * chunks
            ]
    act_ref[...] = act_keep[...].astype(bf16)


def forward_scratch(micros, chunks, chans, peers, width, lane):
    rows = micros * chunks
    return [
        pltpu.VMEM((rows * chans, width), f32),
        pltpu.VMEM((chunks * micros * (chans + 4), width), f32),
        pltpu.VMEM((peers - 1, 4 * rows, width), f32),
        pltpu.VMEM((chans, 4 * rows, width), bf16),
        pltpu.VMEM((chans, 2 * rows, 2 * width), bf16),
        pltpu.VMEM((chans, 2 * rows, lane), bf16),
        pltpu.VMEM((chans, 2 * rows, lane), f32),
        pltpu.VMEM((chans, 2 * width, lane), bf16),
    ]


def backward_kernel(
    micros,
    chunks,
    chans,
    got_ref,
    dact_ref,
    norm_ref,
    const_ref,
    rise_ref,
    taps_ref,
    live_ref,
    y_ref,
    start_ref,
    send_ref,
    sums_keep,
    head,
    x_keep,
    dact_keep,
    u_keep,
    prev_keep,
    dy_parts,
    uv_parts,
    yd_keep,
    duv_keep,
    lag_keep,
    adj_keep,
    sent_parts,
    dots,
    power_ref,
):
    width = got_ref.shape[2]
    half = const_ref.shape[2] // 2
    spans = int(math.log2(chunks))
    rows = micros * chunks
    stride = head.shape[0] // chunks
    got_stride = got_ref.shape[1]
    shape = (width, width)
    passed = lanes(shape) <= lax.broadcasted_iota(jnp.int32, shape, 0)
    low = lanes((1, 2 * half)) < half
    flip = jnp.where(low, 1.0, -1.0)
    live = live_ref[...]
    gain, bias = 2 * (5 + spans), 2 * (5 + spans) + 1
    for k in range(chunks):
        x_keep[pl.ds(k * got_stride, got_stride), :] = got_ref[k].astype(f32)
    dact_keep[...] = dact_ref[...].astype(f32)
    mean, inverse = norm_ref[:rows], norm_ref[rows:]

    def x_hat_of(channel):
        x = channel_tokens(x_keep, channel, got_stride, micros, chunks, chans)
        return (x - mean) * inverse

    def const(channel, k):
        return (
            const_ref[2 * k, channel : channel + 1, :],
            const_ref[2 * k + 1, channel : channel + 1, :],
        )

    def total(x):
        return jnp.sum(x, axis=0, keepdims=True)

    for channel in range(chans):
        line = slice(channel, channel + 1)
        u = live * (x_hat_of(channel) * const_ref[gain, line] + const_ref[bias, line])
        u_prev = previous(u, micros, chunks)
        u_keep[channel] = u
        prev_keep[channel] = u_prev
        u_hi, u_lo = split(u)
        v_hi, v_lo = split(u * u_prev)
        for k, (left, right) in enumerate(((u_hi, v_hi), (u_hi, v_hi), (u_lo, v_lo))):
            uv_parts[channel, k * rows : (k + 1) * rows, :width] = left
            uv_parts[channel, k * rows : (k + 1) * rows, width:] = right
        y = y_ref[channel]
        density = jnp.exp(-0.5 * y * y) * (1.0 / math.sqrt(2.0 * math.pi))
        d_y = dact_keep[pl.ds(channel, rows, stride=chans), :] * (normal_cdf(y) + y * density)
        high, low_part = split(d_y)
        dy_parts[channel, :rows] = high
        dy_parts[channel, rows : 2 * rows] = low_part
        dy_parts[channel, 2 * rows :] = high

    for channel in range(chans):
        tables = [hankel(taps_ref[channel, 8 * k : 8 * k + 8], width) for k in range(2)]
        both = dy_parts[channel, : 2 * rows]
        duv = mm(both, jnp.concatenate([tables[0][0], tables[1][0]], axis=1))
        low_part = mm(both[:rows], jnp.concatenate([tables[0][1], tables[1][1]], axis=1))
        duv_keep[channel] = duv[:rows] + duv[rows:] + low_part

    for channel in range(chans):
        outer = mm(dy_parts[channel], uv_parts[channel], TN)
        for k in range(2):
            rolled = pltpu.roll(
                outer[:, k * width : (k + 1) * width], 1, axis=1, stride=1, stride_axis=0
            )
            line = total(jnp.where(passed, rolled, 0.0))
            high = line.astype(bf16).astype(f32)
            lag_keep[channel, k : k + 1, :] = high
            lag_keep[channel, 2 + k : 3 + k, :] = line - high
            if k == 0:
                sums_keep[channel : channel + 1, :] = jnp.where(
                    lanes(line.shape) == 0, line, 0.0
                )

    levels = int(math.log2(width)) - 3
    for channel in range(chans):
        high, low_part = mode_powers(rise_ref, channel, chans, levels, half)
        power_ref[channel, :width] = high
        power_ref[channel, width:] = low_part

    for channel in range(chans):
        both = dy_parts[channel, : 2 * rows]
        yd = mm(both, power_ref[channel, :width])
        low_part = mm(both[:rows], power_ref[channel, width:])
        yd_keep[channel] = yd[:rows] + yd[rows:] + low_part

    for channel in range(chans):
        adj = cmul(yd_keep[channel], const(channel, 2), half)
        for k in range(spans):
            moved = shift_chunks(adj, -(2**k), micros, chunks)
            adj = adj + cmul(moved, const(channel, 3 + k), half)
        adj = shift_chunks(adj, -1, micros, chunks)
        adj_keep[channel] = adj
        sent = jnp.concatenate(
            [cmul(adj, const(channel, 0), half), cmul(adj, const(channel, 1), half)], axis=0
        )
        high, low_part = split(sent * flip)
        sent_parts[channel, : 2 * rows] = high
        sent_parts[channel, 2 * rows :] = low_part

    for channel in range(chans):
        both = sent_parts[channel]
        cross = mm(both, power_ref[channel, :width], NT)
        cross = cross[: 2 * rows] + cross[2 * rows :]
        cross = cross + mm(both[: 2 * rows], power_ref[channel, width:], NT)
        d_v = duv_keep[channel, :, width:] + cross[rows:]
        d_u = duv_keep[channel, :, :width] + cross[:rows] + d_v * prev_keep[channel]
        d_u = d_u + following(d_v * u_keep[channel], micros, chunks)
        d_q = live * d_u
        sums_keep[chans + channel : chans + channel + 1, :] = total(d_q * x_hat_of(channel))
        sums_keep[2 * chans + channel : 2 * chans + channel + 1, :] = total(d_q)
        d_h = d_q * const_ref[gain, channel : channel + 1]
        for m in range(micros):
            head[pl.ds(m * chans + channel, chunks, stride=stride), :] = d_h[
                m * chunks : (m + 1) * chunks
            ]

    lag_keep[:, 4:, :] = jnp.zeros((chans, 12, width), f32)
    for channel in range(chans):
        lags = lag_keep[channel].astype(bf16)
        tops = mm(lags, power_ref[channel, :width]) + mm(lags, power_ref[channel, width:])
        dots[6, channel : channel + 1, :] = tops[0:1] + tops[2:3]
        dots[7, channel : channel + 1, :] = tops[1:2] + tops[3:4]
        adj, yd = adj_keep[channel], yd_keep[channel]
        adj_swap = swap(adj, half)
        high, low_part = uv_parts[channel, :rows], uv_parts[channel, 2 * rows :]
        parts = jnp.concatenate(
            [high[:, :width], high[:, width:], low_part[:, :width], low_part[:, width:]], axis=0
        )
        q = mm(parts, power_ref[channel, :width])
        q = q[: 2 * rows] + q[2 * rows :] + mm(parts[: 2 * rows], power_ref[channel, width:])
        uq, vq, start = q[:rows], q[rows:], start_ref[channel]
        pairs = ((uq, adj), (uq, adj_swap), (vq, adj), (vq, adj_swap), (start, yd))
        for k, (left, right) in enumerate(pairs + ((start, swap(yd, half)),)):
            dots[k, channel : channel + 1, :] = total(left * right)

    def whole_const(k):
        return const_ref[2 * k], const_ref[2 * k + 1]

    def dot(k):
        same, other = dots[k], dots[k + 1]
        return jnp.where(low, same - swap(same, half), other + swap(other, half))

    top_u, top_v = dots[6], dots[7]
    c = whole_const(3 + spans)
    modes = jnp.concatenate(
        [
            flip * (cmul(top_u, c, half) + dot(0)),
            flip * (cmul(top_v, c, half) + dot(2)),
            flip
            * (
                cmul(top_u, whole_const(0), half)
                + cmul(top_v, whole_const(1), half)
                + cmul(dot(4), whole_const(4 + spans), half)
            ),
        ],
        axis=0,
    )
    sums = jnp.sum(sums_keep[...].T, axis=0, keepdims=True)
    sums_hi = sums.astype(bf16).astype(f32)
    cut = micros * chans
    for k in range(chunks):
        at = k * stride + cut
        head[pl.ds(at, 3 * chans), :] = modes
        head[pl.ds(at + 3 * chans, 1), pl.ds(0, 3 * chans)] = sums_hi
        head[pl.ds(at + 3 * chans + 1, 1), pl.ds(0, 3 * chans)] = sums - sums_hi
        send_ref[k] = head[pl.ds(k * stride, stride), :].astype(bf16)


def backward_scratch(micros, chunks, chans, stride, width, lane):
    rows = micros * chunks
    return [
        pltpu.VMEM((3 * chans, lane), f32),
        pltpu.VMEM((chunks * stride, width), f32),
        pltpu.VMEM((chunks * micros * (chans + 4), width), f32),
        pltpu.VMEM((rows * chans, width), f32),
        pltpu.VMEM((chans, rows, width), f32),
        pltpu.VMEM((chans, rows, width), f32),
        pltpu.VMEM((chans, 3 * rows, width), bf16),
        pltpu.VMEM((chans, 3 * rows, 2 * width), bf16),
        pltpu.VMEM((chans, rows, lane), f32),
        pltpu.VMEM((chans, rows, 2 * width), f32),
        pltpu.VMEM((chans, 16, width), f32),
        pltpu.VMEM((chans, rows, lane), f32),
        pltpu.VMEM((chans, 4 * rows, lane), bf16),
        pltpu.VMEM((8, chans, lane), f32),
        pltpu.VMEM((chans, 2 * width, lane), bf16),
    ]


def gated(both, bias, g):
    wide = g.shape[1]
    value = both[:, :wide] + bias[:, :wide]
    gate = jax.nn.sigmoid(both[:, wide:] + bias[:, wide:])
    d_value = g * gate
    return value * gate, jnp.concatenate(
        [d_value.astype(bf16), (d_value * value * (1.0 - gate)).astype(bf16)], axis=1
    )


def project_kernel(width, place_ref, lens_ref, act_ref, *refs):
    refs, (dact_ref, d_keep) = refs[:-2], refs[-2:]
    full, rows = act_ref.shape
    peers = len(refs)
    wide = full // peers
    start = place_ref[1] * rows
    at = place_ref[0] * width + lax.rem(start, width)
    at = at + lax.broadcasted_iota(jnp.int32, (rows, wide), 0)
    live = (at < lens_ref[start // width]).astype(f32)
    act = act_ref[...].T

    def weight(ref):
        return jnp.concatenate(
            [ref[wide : wide + full, :], ref[wide + full : wide + 2 * full, :]], axis=1
        )

    for k, ref in enumerate(refs):
        g = live * ref[:wide, :].T.astype(f32)
        bias = ref[wide + 2 * full :, :].astype(f32)
        bias = jnp.concatenate(
            [bias[0:1] + bias[1:2] + bias[2:3], bias[3:4] + bias[4:5] + bias[5:6]], axis=1
        )
        d_both = gated(mm(act, weight(ref)), bias, g)[1]
        d_keep[:, 2 * k * wide : 2 * (k + 1) * wide] = d_both
    weights = jnp.concatenate([weight(ref) for ref in refs], axis=1)
    dact_ref[...] = mm(weights, d_keep[...], NT).astype(bf16)


def output_kernel(
    seqs,
    rank_ref,
    lens_ref,
    order_ref,
    tokens_ref,
    cot_ref,
    wv_ref,
    wg_ref,
    bv_ref,
    bg_ref,
    *refs,
):
    micros, wide, width = tokens_ref.shape
    acts_in, refs = refs[:micros], refs[micros:]
    out_ref, keep_ref, send_refs = refs[0], refs[1], refs[2:-2]
    d_keep, grad = refs[-2:]
    full = wv_ref.shape[0]
    at = rank_ref[0] * width + lax.broadcasted_iota(jnp.int32, (width, wide), 0)
    place = rank_ref[0] * width + lanes((1, width))
    weights = jnp.concatenate([wv_ref[...], wg_ref[...]], axis=1)
    bias = jnp.concatenate([bv_ref[...], bg_ref[...]], axis=1)
    for k in range(micros):
        m = order_ref[k]
        g = (at < lens_ref[m]).astype(f32) * cot_ref[m].T.astype(f32)
        added, d_both = gated(mm(acts_in[k][...].T, weights), bias, g)
        live = (place < lens_ref[m]).astype(f32)
        out_ref[m] = (live * (tokens_ref[m].astype(f32) + added.T)).astype(bf16)
        d_keep[k * width : (k + 1) * width] = d_both
    d_both = d_keep[...]
    acts = jnp.concatenate([ref[...] for ref in acts_in], axis=1)
    grad_w = mm(acts, d_both)
    grad_b = mm(jnp.ones((8, micros * width), bf16), d_both)
    row = lax.broadcasted_iota(jnp.int32, (8, wide), 0)
    small = jnp.where(row == 0, grad_b[:, :wide], grad_b[:, wide:])
    count = full // seqs
    for k in range(seqs):
        part = grad_w[k * count : (k + 1) * count]
        grad[k, pl.ds(0, count), :] = part[:, :wide]
        grad[k, pl.ds(count, count), :] = part[:, wide:]
        grad[k, pl.ds(2 * count, 8), :] = small
    place = rank_ref[0] >> 1
    for j in range(2):
        keep_ref[j] = grad[2 * place + j]
        for k, ref in enumerate(send_refs):
            ref[j] = grad[2 * (place ^ (k + 1)) + j].astype(bf16)


def parts_kernel(bit_ref, keep_in_ref, *refs):
    got_refs, (keep_ref, send_ref, total) = refs[:-3], refs[-3:]
    value = keep_in_ref[...]
    for ref in got_refs:
        value = value + ref[...].astype(f32)
    total[...] = value
    keep_ref[...] = total[bit_ref[0]]
    send_ref[...] = total[1 - bit_ref[0]].astype(bf16)


def last_kernel(left_ref, right_ref, wv_ref, wg_ref, bv_ref, bg_ref):
    count = wv_ref.shape[0]
    total = left_ref[...] + right_ref[...].astype(f32)
    wv_ref[...] = total[:count]
    wg_ref[...] = total[count : 2 * count]
    bv_ref[...] = total[2 * count : 2 * count + 1]
    bg_ref[...] = total[2 * count + 1 : 2 * count + 2]


def normal(tokens_ref, norm_ref, m):
    micros = tokens_ref.shape[0]
    return (tokens_ref[m].astype(f32) - norm_ref[m : m + 1]) * norm_ref[
        micros + m : micros + m + 1
    ]


def sums_kernel(got_ref, tokens_ref, *refs):
    stats_refs, (out_ref, head_ref, norm_ref) = refs[:-3], refs[-3:]
    micros, wide, width = tokens_ref.shape
    seqs, stride, _ = head_ref.shape
    chans = wide // seqs
    mean, inverse = merge(
        [ref[pl.ds(0, micros), :] for ref in stats_refs],
        [ref[pl.ds(micros, micros), :] for ref in stats_refs],
        wide,
    )
    norm_ref[pl.ds(0, micros), :] = mean
    norm_ref[pl.ds(micros, micros), :] = inverse
    cut = micros * chans
    turned = got_ref[:, pl.ds(0, cut), :].reshape(seqs * cut, width)
    head_ref[:, pl.ds(0, cut), :] = mm(turned, mirror(width)).reshape(seqs, cut, width)
    head_ref[:, pl.ds(cut, stride - cut), :] = got_ref[:, pl.ds(cut, stride - cut), :].astype(f32)
    for m in range(micros):
        d_hat = head_ref[:, pl.ds(m * chans, chans), :].reshape(wide, width)
        x_hat = normal(tokens_ref, norm_ref, m)
        out_ref[pl.ds(m, 1), :] = jnp.sum(d_hat, axis=0, keepdims=True)
        out_ref[pl.ds(micros + m, 1), :] = jnp.sum(d_hat * x_hat, axis=0, keepdims=True)


def final_kernel(
    rank_ref,
    lens_ref,
    head_ref,
    tokens_ref,
    cot_ref,
    norm_ref,
    *refs,
):
    hat_refs, refs = refs[:-7], refs[-7:]
    d_in_ref, b_ref, e_ref, c_ref, skip_ref, gain_ref, norm_bias_ref = refs
    micros, wide, width = tokens_ref.shape
    seqs, stride, _ = head_ref.shape
    peers = len(hat_refs)
    chans = wide // seqs
    hats = [ref[...] for ref in hat_refs]
    hat = sum(hats[1:], hats[0]) * (1.0 / (peers * wide))
    at = rank_ref[0] * width + lanes((1, width))
    for m in range(micros):
        live = (at < lens_ref[m]).astype(f32)
        d_hat = head_ref[:, pl.ds(m * chans, chans), :].reshape(wide, width)
        x_hat = normal(tokens_ref, norm_ref, m)
        inside = d_hat - hat[m : m + 1] - x_hat * hat[micros + m : micros + m + 1]
        d_in_ref[m] = (
            live * cot_ref[m].astype(f32) + norm_ref[micros + m : micros + m + 1] * inside
        )
    cut = micros * chans
    for k, ref in enumerate((b_ref, e_ref, c_ref)):
        modes = head_ref[:, pl.ds(cut + k * chans, chans), :]
        ref[...] = modes.reshape(wide, -1).T.reshape(ref.shape)
    place = lanes((1, wide)) // chans
    last = cut + 3 * chans
    for k, ref in enumerate((skip_ref, gain_ref, norm_bias_ref)):
        line = jnp.zeros((1, wide), f32)
        for s in range(seqs):
            own = head_ref[s, pl.ds(last, 1), :] + head_ref[s, pl.ds(last + 1, 1), :]
            own = pltpu.roll(own, (s - k) * chans % own.shape[1], axis=1)[:, :wide]
            line = jnp.where(place == s, own, line)
        ref[...] = line


def smem():
    return pl.BlockSpec(memory_space=pltpu.SMEM)


def vmem():
    return pl.BlockSpec(memory_space=pltpu.VMEM)


def in_hbm(x):
    return pltpu.with_memory_space_constraint(x, pltpu.HBM)


def shape_of(shape, kind=f32):
    return jax.ShapeDtypeStruct(shape, kind)


def kernel_call(kernel, name, scalars, arrays, outs, micros_of_time, limit=8, **more):
    ins = [smem()] * len(scalars) + [vmem()] * len(arrays)
    return pl.pallas_call(
        kernel,
        in_specs=ins,
        out_specs=[vmem()] * len(outs),
        out_shape=outs,
        compiler_params=pltpu.CompilerParams(vmem_limit_bytes=limit * 1024 * 1024),
        cost_estimate=cost(micros_of_time),
        name=name,
        **more,
    )(*scalars, *arrays)


def cost(micros_of_time):
    return pl.CostEstimate(
        flops=int(micros_of_time * 1e9), bytes_accessed=int(micros_of_time * 3e6), transcendentals=0
    )


def shards(
    tokens,
    lengths,
    ln_gain,
    ln_bias,
    b_coef,
    e_coef,
    c_coef,
    skip_gain,
    decay_rate,
    rotation,
    w_value,
    w_gate,
    bias_value,
    bias_gate,
    out_cotangent,
):
    micros, wide, width = tokens.shape
    modes = decay_rate.shape[1]
    full = w_value.shape[0]
    seqs = lax.axis_size("seq")
    peers = lax.axis_size("chan")
    seq_rank = lax.axis_index("seq").astype(jnp.int32)
    chan_rank = lax.axis_index("chan").astype(jnp.int32)
    chans = wide // seqs
    rows = micros * seqs
    own = micros * width // peers
    parts = width // own
    both = ("chan", "seq")
    lane = 2 * modes
    spans = int(math.log2(seqs))
    levels = int(math.log2(width)) - 3
    rank = seq_rank.reshape(1)
    lens = lengths.reshape(micros)
    place = jnp.stack([seq_rank, chan_rank])
    bias_rows = (bias_value.reshape(1, wide), bias_gate.reshape(1, wide))

    def exchange(x, axis):
        return lax.all_to_all(x, axis, 0, 0, tiled=True)

    def cross(x, by):
        return lax.ppermute(x, "chan", [(i, i ^ by) for i in range(peers)])

    hbm = pl.BlockSpec(memory_space=pltpu.HBM)
    x_send, part_stats = pl.pallas_call(
        functools.partial(pack_kernel, seqs),
        in_specs=[hbm],
        out_specs=[vmem()] * 2,
        out_shape=[
            shape_of((seqs, micros * (chans + 4), width), bf16),
            shape_of((2 * micros, width)),
        ],
        scratch_shapes=[
            pltpu.VMEM(tokens.shape, bf16),
            pltpu.SemaphoreType.DMA((micros,)),
        ],
        compiler_params=pltpu.CompilerParams(vmem_limit_bytes=8 * 1024 * 1024),
        cost_estimate=cost(1),
        name="pack",
    )(in_hbm(tokens))
    x_mine = exchange(x_send, "seq")
    stats = [part_stats] + [cross(part_stats, k) for k in range(1, peers)]

    cot, wv, wg, _ = lax.optimization_barrier((out_cotangent, w_value, w_gate, part_stats))
    cot_own = cot.reshape(micros, wide, parts, own).transpose(0, 2, 1, 3).reshape(peers, wide, own)
    weights = pl.pallas_call(
        gather_kernel,
        in_specs=[smem()] + [vmem()] * 2 + [hbm] * 3,
        out_specs=[vmem()] * peers,
        out_shape=[shape_of((wide + 2 * full + 16, own), bf16)] * peers,
        scratch_shapes=[pltpu.SemaphoreType.DMA((3 * peers,))],
        compiler_params=pltpu.CompilerParams(vmem_limit_bytes=8 * 1024 * 1024),
        cost_estimate=cost(1),
        name="weights",
    )(chan_rank.reshape(1), *bias_rows, in_hbm(cot_own), in_hbm(wv), in_hbm(wg))

    turned = [jnp.transpose(z, (0, 2, 1)) for z in (b_coef, e_coef, c_coef)]
    const, rise, taps, live = pl.pallas_call(
        functools.partial(table_kernel, chans, seqs, width),
        in_specs=[smem()] * 5 + [hbm] * 5,
        out_specs=[vmem()] * 4,
        out_shape=[
            shape_of((12 + 2 * spans, chans, lane)),
            shape_of(((8 + 2 * levels) * chans, lane)),
            shape_of((chans, 16, width)),
            shape_of((rows, width)),
        ],
        scratch_shapes=[pltpu.VMEM(turned[0].shape, f32)] * 3
        + [pltpu.VMEM((modes, wide), f32)] * 2
        + [
            pltpu.VMEM((wide, lane), f32),
            pltpu.VMEM((16 * chans, lane), f32),
            pltpu.SemaphoreType.DMA((5,)),
        ],
        compiler_params=pltpu.CompilerParams(vmem_limit_bytes=8 * 1024 * 1024),
        cost_estimate=cost(2),
        name="tables",
    )(rank, lens, skip_gain, ln_gain, ln_bias, *[in_hbm(z) for z in (*turned, decay_rate.T, rotation.T)])

    x_mine, const, weights = lax.optimization_barrier((x_mine, const, weights))
    x_stats = x_mine[:, micros * chans :]
    x_stats = [cross(x_stats, k) for k in range(1, peers)]
    weights = [weights[0]] + [cross(weights[k], k) for k in range(1, peers)]
    arrays = (x_mine, const, rise, taps, live, *x_stats)
    act, norm_mine, y_mine, start_mine = pl.pallas_call(
        functools.partial(forward_kernel, micros, seqs, chans, peers),
        in_specs=[vmem()] * len(arrays),
        out_specs=[vmem()] * 4,
        out_shape=[
            shape_of((rows * chans, width), bf16),
            shape_of((2 * rows, width)),
            shape_of((chans, rows, width)),
            shape_of((chans, rows, lane)),
        ],
        scratch_shapes=forward_scratch(micros, seqs, chans, peers, width, lane),
        compiler_params=pltpu.CompilerParams(vmem_limit_bytes=16 * 1024 * 1024),
        cost_estimate=cost(5),
        name="mixer_forward",
    )(*arrays)

    act = (
        act.reshape(micros, seqs, chans, parts, own)
        .transpose(0, 3, 1, 2, 4)
        .reshape(peers * seqs, chans, own)
    )
    act = exchange(act, both).reshape(full, own)
    (d_act,) = kernel_call(
        functools.partial(project_kernel, width),
        "project",
        (place, lens),
        (act, *weights),
        [shape_of((full, own), bf16)],
        2,
        limit=12,
        scratch_shapes=[pltpu.VMEM((own, 2 * full), bf16)],
    )

    acts = [act] + [cross(act, k) for k in range(1, peers)]
    if parts == 1:
        order = chan_rank ^ jnp.arange(peers, dtype=jnp.int32)
    else:
        stacked = jnp.stack(acts)[chan_rank ^ jnp.arange(peers, dtype=jnp.int32)]
        stacked = stacked.reshape(micros, parts, full, own).transpose(0, 2, 1, 3)
        stacked = stacked.reshape(micros, full, width)
        acts = [stacked[m] for m in range(micros)]
        order = jnp.arange(micros, dtype=jnp.int32)

    d_act = exchange(d_act.reshape(peers * seqs, chans, own), both)
    d_act = (
        d_act.reshape(micros, parts, seqs, chans, own)
        .transpose(0, 2, 3, 1, 4)
        .reshape(rows * chans, width)
    )
    count = full // seqs
    part = (2, 2 * count + 8, wide)
    out, keep, *blocks = kernel_call(
        functools.partial(output_kernel, seqs),
        "output",
        (rank, lens, order),
        (tokens, out_cotangent, w_value, w_gate) + bias_rows + tuple(acts),
        [shape_of(tokens.shape, bf16), shape_of(part)] + [shape_of(part, bf16)] * (seqs // 2 - 1),
        2,
        limit=12,
        scratch_shapes=[
            pltpu.VMEM((micros * width, 2 * wide), bf16),
            pltpu.VMEM((seqs,) + part[1:], f32),
        ],
    )
    blocks = [
        lax.ppermute(block, "seq", [(i, i ^ ((k + 1) << 1)) for i in range(seqs)])
        for k, block in enumerate(blocks)
    ]
    d_act, keep, *stats = lax.optimization_barrier((d_act, keep, *stats))
    stride = -(-((micros + 3) * chans + 2) // 16) * 16
    arrays = (x_mine, d_act, norm_mine, const, rise, taps, live, y_mine, start_mine)
    d_hat = pl.pallas_call(
        functools.partial(backward_kernel, micros, seqs, chans),
        in_specs=[vmem()] * len(arrays),
        out_specs=vmem(),
        out_shape=shape_of((seqs, stride, width), bf16),
        scratch_shapes=backward_scratch(micros, seqs, chans, stride, width, lane),
        compiler_params=pltpu.CompilerParams(vmem_limit_bytes=20 * 1024 * 1024),
        cost_estimate=cost(5),
        name="mixer_backward",
    )(*arrays)
    d_hat, *blocks = lax.optimization_barrier((d_hat, *blocks))
    keep, send = kernel_call(
        parts_kernel,
        "parts",
        (seq_rank.reshape(1) & 1,),
        (keep, *blocks),
        [shape_of(part[1:]), shape_of(part[1:], bf16)],
        1,
        scratch_shapes=[pltpu.VMEM(part, f32)],
    )
    got = lax.ppermute(send, "seq", [(i, i ^ 1) for i in range(seqs)])
    d_wv, d_wg, d_bv, d_bg = kernel_call(
        last_kernel,
        "last",
        (),
        (keep, got),
        [shape_of((count, wide))] * 2 + [shape_of((1, wide))] * 2,
        1,
    )
    got = exchange(d_hat, "seq")
    own_sums, head, norm = kernel_call(
        sums_kernel,
        "sums",
        (),
        (got, tokens, *stats),
        [
            shape_of((2 * micros, width)),
            shape_of((seqs, stride, width)),
            shape_of((2 * micros, width)),
        ],
        1,
    )
    hat_sums = [own_sums] + [cross(own_sums, k) for k in range(1, peers)]
    mode_grad = shape_of((2, modes, wide))
    d_input, d_b, d_e, d_c, d_skip, d_gain, d_bias = kernel_call(
        final_kernel,
        "final",
        (rank, lens),
        (head, tokens, out_cotangent, norm, *hat_sums),
        [shape_of(tokens.shape)]
        + [mode_grad] * 3
        + [shape_of((1, wide))] * 3,
        2,
    )
    d_b, d_e, d_c = [jnp.transpose(z, (0, 2, 1)) for z in (d_b, d_e, d_c)]
    d_skip, d_gain, d_bias, d_bv, d_bg = [
        z.reshape(wide) for z in (d_skip, d_gain, d_bias, d_bv, d_bg)
    ]
    return (out, d_input, d_gain, d_bias, d_b, d_e, d_c, d_skip, d_wv, d_wg, d_bv, d_bg)


def solution(mesh):
    chan = P("chan")
    modes = P(None, "chan", None)
    table = P("chan", None)
    weight = P(None, "chan")
    rows = P(None, "chan", "seq")
    spread = P("seq", "chan")
    return jax.shard_map(
        shards,
        mesh=mesh,
        in_specs=(
            rows,
            P(),
            chan,
            chan,
            modes,
            modes,
            modes,
            chan,
            table,
            table,
            weight,
            weight,
            chan,
            chan,
            rows,
        ),
        out_specs=(
            rows,
            rows,
            chan,
            chan,
            modes,
            modes,
            modes,
            chan,
            spread,
            spread,
            chan,
            chan,
        ),
        check_vma=False,
    )
```

```python
import functools
import math

import jax
import jax.numpy as jnp
from jax import lax
from jax.experimental import pallas as pl
from jax.experimental.pallas import tpu as pltpu
from jax.sharding import PartitionSpec as P

f32 = jnp.float32
bf16 = jnp.bfloat16
epsilon = 1e-05
NN = (((1,), (0,)), ((), ()))
NT = (((1,), (1,)), ((), ()))
TN = (((0,), (0,)), ((), ()))


def mm(left, right, dims=NN):
    return lax.dot_general(left, right, dims, preferred_element_type=f32)


def split(x):
    high = x.astype(bf16)
    return high, (x - high.astype(f32)).astype(bf16)


def swap(x, half):
    return pltpu.roll(x, half, axis=x.ndim - 1)


def lanes(shape):
    return lax.broadcasted_iota(jnp.int32, shape, len(shape) - 1)


def pair(z, half):
    low = lanes(z.shape) < half
    turned = swap(z, half)
    return jnp.where(low, z, turned), jnp.where(low, -turned, z)


def cmul(x, z, half):
    return x * z[0] + swap(x, half) * z[1]


def normal_cdf(y):
    return 0.5 * (1.0 + lax.erf(y * (1.0 / math.sqrt(2.0))))


def mirror(width):
    shape = (width, width)
    at = lanes(shape) + lax.broadcasted_iota(jnp.int32, shape, 0)
    return (at == width - 1).astype(f32).astype(bf16)


def live_rows(lens_ref, micros, chunks, width):
    shape = (chunks, width)
    at = lax.broadcasted_iota(jnp.int32, shape, 0) * width + (width - 1 - lanes(shape))
    rows = [(at < lens_ref[m]).astype(f32) for m in range(micros)]
    return jnp.concatenate(rows, axis=0)


def merge(means, squares, count):
    parts = len(means)
    mean = sum(means[1:], means[0]) * (1.0 / parts)
    square = sum(squares[1:], squares[0])
    for part in means:
        square = square + count * jnp.square(part - mean)
    return mean, lax.rsqrt(square * (1.0 / (parts * count)) + epsilon)


def fetch(copies):
    for copy in copies:
        copy.start()


def shift_chunks(x, by, micros, chunks):
    cube = x.reshape(micros, chunks, x.shape[-1])
    place = lax.broadcasted_iota(jnp.int32, cube.shape, 1)
    if by > 0:
        moved = jnp.where(place >= by, pltpu.roll(cube, by, axis=1), 0.0)
    else:
        moved = jnp.where(place < chunks + by, pltpu.roll(cube, chunks + by, axis=1), 0.0)
    return moved.reshape(x.shape)


def previous(u, micros, chunks):
    width = u.shape[1]
    turned = pltpu.roll(u, width - 1, axis=1)
    return jnp.where(
        lanes(u.shape) == width - 1, shift_chunks(turned, 1, micros, chunks), turned
    )


def following(u, micros, chunks):
    turned = pltpu.roll(u, 1, axis=1)
    return jnp.where(lanes(u.shape) == 0, shift_chunks(turned, -1, micros, chunks), turned)


def hankel(first, width):
    blocks = []
    for k in range(width // 8):
        by = width - 8 - 8 * k
        blocks.append(pltpu.roll(first, by, axis=1) if by else first)
    table = jnp.concatenate(blocks, axis=0)
    at = lanes(table.shape) + lax.broadcasted_iota(jnp.int32, table.shape, 0)
    return split(jnp.where(at >= width - 1, table, 0.0))


def gather_kernel(rank_ref, bv_ref, bg_ref, cot_hbm, wv_hbm, wg_hbm, *refs):
    outs, sems = refs[:-1], refs[-1]
    peers, wide, _ = cot_hbm.shape
    full = wv_hbm.shape[0]
    copies = []
    for k, out in enumerate(outs):
        for source, start, count in (
            (cot_hbm.at[rank_ref[0] ^ k], 0, wide),
            (wv_hbm, wide, full),
            (wg_hbm, wide + full, full),
        ):
            copies.append(
                pltpu.make_async_copy(
                    source, out.at[pl.ds(start, count), :], sems.at[len(copies)]
                )
            )
    fetch(copies)
    pieces = []
    for value in (bv_ref[...], bg_ref[...]):
        for _ in range(3):
            high = value.astype(bf16).astype(f32)
            pieces.append(high)
            value = value - high
    pieces.append(jnp.zeros((10, wide), f32))
    biases = jnp.concatenate(pieces, axis=0).astype(bf16)
    for out in outs:
        out[pl.ds(wide + 2 * full, 16), :] = biases
    for copy in copies:
        copy.wait()


def pack_kernel(seqs, tokens_hbm, send_ref, stats_ref, tokens, sems):
    micros, wide, width = tokens.shape
    chans = wide // seqs
    copies = [
        pltpu.make_async_copy(tokens_hbm.at[m], tokens.at[m], sems.at[m]) for m in range(micros)
    ]
    fetch(copies)
    turn = mirror(width)
    means, squares = [], []
    for copy in copies:
        copy.wait()
    for m in range(micros):
        x = tokens[m].astype(f32)
        mean = jnp.sum(x, axis=0, keepdims=True) * (1.0 / wide)
        means.append(mean)
        squares.append(jnp.sum(jnp.square(x - mean), axis=0, keepdims=True))
        turned = mm(tokens[m], turn).astype(bf16)
        send_ref[:, pl.ds(m * chans, chans), :] = turned.reshape(seqs, chans, width)
    stats = jnp.concatenate(means + squares, axis=0)
    stats_ref[...] = stats
    rest, lines = stats, []
    for _ in range(3):
        high = rest.astype(bf16).astype(f32)
        lines.append(high)
        rest = rest - high
    tail = jnp.concatenate(lines, axis=0).astype(bf16)
    tail = mm(tail, turn).astype(bf16)
    for k in range(seqs):
        send_ref[k, pl.ds(micros * chans, 6 * micros), :] = tail


def table_kernel(
    chans,
    seqs,
    width,
    rank_ref,
    lens_ref,
    skip_ref,
    gain_ref,
    bias_ref,
    b_hbm,
    e_hbm,
    c_hbm,
    decay_hbm,
    turn_hbm,
    const_ref,
    rise,
    taps_ref,
    live_ref,
    b_ref,
    e_ref,
    c_ref,
    decay_ref,
    turn_ref,
    turned_keep,
    coefs,
    sems,
):
    half = decay_ref.shape[0]
    loads = [
        pltpu.make_async_copy(source, target, sems.at[k])
        for k, (source, target) in enumerate(
            (
                (b_hbm, b_ref),
                (e_hbm, e_ref),
                (c_hbm, c_ref),
                (decay_hbm, decay_ref),
                (turn_hbm, turn_ref),
            )
        )
    ]
    fetch(loads)
    for load in loads:
        load.wait()
    base = rank_ref[0] * chans
    levels = int(math.log2(width)) - 3
    spans = int(math.log2(seqs))

    def own(value):
        turned_keep[...] = value.T
        return turned_keep[pl.ds(base, chans), :]

    b = own(b_ref[...].reshape(2 * half, -1))
    e = own(e_ref[...].reshape(2 * half, -1))
    c = own(c_ref[...].reshape(2 * half, -1))
    mixed = own(jnp.concatenate([decay_ref[...], turn_ref[...]], axis=0))
    low = lanes(mixed.shape) < half
    other = swap(mixed, half)
    decay = jnp.where(low, mixed, other)
    turn = jnp.where(low, other, mixed)
    turned = jnp.where(low, jnp.cos(turn), jnp.sin(turn))
    a = jnp.exp(-decay) * turned
    inverse = pair(jnp.exp(decay) * jnp.where(low, turned, -turned), half)
    a_pair = pair(a, half)
    power = jnp.where(low, 1.0, 0.0)
    for k in range(8):
        rise[pl.ds(k * chans, chans), :] = power
        power = cmul(power, a_pair, half) if k else a
    for k in range(levels):
        power_pair = pair(power, half)
        rise[pl.ds((8 + 2 * k) * chans, chans), :] = power_pair[0]
        rise[pl.ds((9 + 2 * k) * chans, chans), :] = power_pair[1]
        power = cmul(power, power_pair, half)
    kept = [pair(b, half), pair(e, half), pair(cmul(a, pair(c, half), half), half)]
    for k in range(spans):
        kept.append(pair(power, half))
        power = cmul(power, kept[-1], half)
    kept += [pair(c, half), a_pair]
    for k, both in enumerate(kept):
        const_ref[2 * k] = both[0]
        const_ref[2 * k + 1] = both[1]
    sign = jnp.where(low, 1.0, -1.0)
    for j in range(2):
        coef = cmul(c, kept[j], half)
        for k in range(7, -1, -1):
            coefs[pl.ds((8 * j + k) * chans, chans), :] = coef * sign
            coef = cmul(coef, inverse, half)

    live_ref[...] = live_rows(lens_ref, lens_ref.shape[0], seqs, width)
    for channel in range(chans):
        for k, ref in enumerate((gain_ref, bias_ref)):
            const_ref[2 * len(kept) + k, channel : channel + 1, :] = jnp.full(
                (1, 2 * half), ref[base + channel], f32
            )
        high, low_part = mode_powers(rise, channel, chans, levels, half)
        coef = coefs[pl.ds(channel, 16, stride=chans), :]
        coef_hi = coef.astype(bf16).astype(f32)
        both = jnp.concatenate([coef_hi, coef - coef_hi], axis=0).astype(bf16)
        taps = mm(both, high, NT) + mm(both, low_part, NT)
        taps = taps[:16] + taps[16:]
        at = lanes(taps.shape) + lax.broadcasted_iota(jnp.int32, taps.shape, 0)
        taps_ref[channel] = taps + jnp.where(at == 7, skip_ref[base + channel], 0.0)


def mode_powers(rise_ref, channel, chans, levels, half):
    up = rise_ref[pl.ds(channel, 8, stride=chans), :]
    for k in range(levels):
        at = (8 + 2 * k) * chans + channel
        by = (rise_ref[at : at + 1, :], rise_ref[at + chans : at + chans + 1, :])
        up = jnp.concatenate([up, cmul(up, by, half)], axis=0)
    return split(up)


def own_rows(keep, at, stride, micros, chunks):
    return jnp.concatenate(
        [keep[pl.ds(at + m, chunks, stride=stride), :] for m in range(micros)], axis=0
    )


def channel_tokens(keep, channel, stride, micros, chunks, chans):
    return jnp.concatenate(
        [keep[pl.ds(m * chans + channel, chunks, stride=stride), :] for m in range(micros)],
        axis=0,
    )


def forward_kernel(
    micros,
    chunks,
    chans,
    peers,
    got_ref,
    const_ref,
    rise_ref,
    taps_ref,
    live_ref,
    *refs,
):
    stats_refs, refs = refs[: peers - 1], refs[peers - 1 :]
    act_ref, norm_ref, y_ref, start_ref, act_keep, x_keep, stats_keep = refs[:7]
    parts, wide_parts, sent_parts, kept_ref, power_ref = refs[7:]
    width = got_ref.shape[2]
    half = const_ref.shape[2] // 2
    spans = int(math.log2(chunks))
    rows = micros * chunks
    stride = got_ref.shape[1]
    flip = jnp.where(lanes((1, 2 * half)) < half, 1.0, -1.0)

    def const(channel, k):
        return (
            const_ref[2 * k, channel : channel + 1, :],
            const_ref[2 * k + 1, channel : channel + 1, :],
        )

    live = live_ref[...]
    gain, bias = 2 * (5 + spans), 2 * (5 + spans) + 1
    for k in range(chunks):
        x_keep[pl.ds(k * stride, stride), :] = got_ref[k].astype(f32)
    means, squares = [], []
    for j in range(peers):
        keep, step, at = x_keep, stride, micros * chans
        if j:
            keep, step, at = stats_keep.at[j - 1], 6 * micros, 0
            for k in range(chunks):
                keep[pl.ds(k * step, step), :] = stats_refs[j - 1][k].astype(f32)
        lines = [own_rows(keep, at + q * micros, step, micros, chunks) for q in range(5)]
        means.append(lines[0] + lines[2] + lines[4])
        squares.append(lines[1] + lines[3])
    mean, inverse = merge(means, squares, chans * chunks)
    norm_ref[pl.ds(0, rows), :] = mean
    norm_ref[pl.ds(rows, rows), :] = inverse

    for channel in range(chans):
        x_hat = channel_tokens(x_keep, channel, stride, micros, chunks, chans) - mean
        line = slice(channel, channel + 1)
        u = live * (x_hat * inverse * const_ref[gain, line] + const_ref[bias, line])
        u_hi, u_lo = split(u)
        v_hi, v_lo = split(u * previous(u, micros, chunks))
        for k, part in enumerate((u_hi, v_hi, u_lo, v_lo)):
            parts[channel, k * rows : (k + 1) * rows] = part
        wide_parts[channel, :rows, :width] = u_hi
        wide_parts[channel, :rows, width:] = v_hi
        wide_parts[channel, rows:, :width] = u_lo
        wide_parts[channel, rows:, width:] = v_lo

    levels = int(math.log2(width)) - 3
    for channel in range(chans):
        high, low_part = mode_powers(rise_ref, channel, chans, levels, half)
        power_ref[channel, :width] = high
        power_ref[channel, width:] = low_part

    for channel in range(chans):
        q = mm(parts[channel], power_ref[channel, :width])
        kept_ref[channel, : 2 * rows] = (
            q[: 2 * rows]
            + q[2 * rows :]
            + mm(parts[channel, : 2 * rows], power_ref[channel, width:])
        )

    for channel in range(chans):
        uq, vq = kept_ref[channel, :rows], kept_ref[channel, rows : 2 * rows]
        state = cmul(uq, const(channel, 0), half) + cmul(vq, const(channel, 1), half)
        for k in range(spans):
            moved = shift_chunks(state, 2**k, micros, chunks)
            state = state + cmul(moved, const(channel, 3 + k), half)
        start = shift_chunks(state, 1, micros, chunks)
        start_ref[channel] = start
        high, low_part = split(cmul(start, const(channel, 2), half) * flip)
        sent_parts[channel, :rows] = high
        sent_parts[channel, rows:] = low_part

    for channel in range(chans):
        tables = [hankel(taps_ref[channel, 8 * k : 8 * k + 8], width) for k in range(2)]
        both = wide_parts[channel]
        y = mm(both, jnp.concatenate([tables[0][0], tables[1][0]], axis=0))
        low_part = mm(both[:rows], jnp.concatenate([tables[0][1], tables[1][1]], axis=0))
        y_ref[channel] = y[:rows] + y[rows:] + low_part

    for channel in range(chans):
        both = sent_parts[channel]
        cross = mm(both, power_ref[channel, :width], NT)
        y = y_ref[channel] + cross[:rows] + cross[rows:]
        y = y + mm(both[:rows], power_ref[channel, width:], NT)
        y_ref[channel] = y
        act = y * normal_cdf(y)
        for m in range(micros):
            act_keep[pl.ds(m * chunks * chans + channel, chunks, stride=chans), :] = act[
                m * chunks : (m + 1) * chunks
            ]
    act_ref[...] = act_keep[...].astype(bf16)


def forward_scratch(micros, chunks, chans, peers, width, lane):
    rows = micros * chunks
    return [
        pltpu.VMEM((rows * chans, width), f32),
        pltpu.VMEM((chunks * micros * (chans + 6), width), f32),
        pltpu.VMEM((peers - 1, 6 * rows, width), f32),
        pltpu.VMEM((chans, 4 * rows, width), bf16),
        pltpu.VMEM((chans, 2 * rows, 2 * width), bf16),
        pltpu.VMEM((chans, 2 * rows, lane), bf16),
        pltpu.VMEM((chans, 2 * rows, lane), f32),
        pltpu.VMEM((chans, 2 * width, lane), bf16),
    ]


def backward_kernel(
    micros,
    chunks,
    chans,
    got_ref,
    dact_ref,
    norm_ref,
    const_ref,
    rise_ref,
    taps_ref,
    live_ref,
    y_ref,
    start_ref,
    send_ref,
    sums_keep,
    head,
    x_keep,
    dact_keep,
    u_keep,
    prev_keep,
    dy_parts,
    uv_parts,
    yd_keep,
    duv_keep,
    lag_keep,
    adj_keep,
    sent_parts,
    dots,
    power_ref,
):
    width = got_ref.shape[2]
    half = const_ref.shape[2] // 2
    spans = int(math.log2(chunks))
    rows = micros * chunks
    stride = head.shape[0] // chunks
    got_stride = got_ref.shape[1]
    shape = (width, width)
    passed = lanes(shape) <= lax.broadcasted_iota(jnp.int32, shape, 0)
    low = lanes((1, 2 * half)) < half
    flip = jnp.where(low, 1.0, -1.0)
    live = live_ref[...]
    gain, bias = 2 * (5 + spans), 2 * (5 + spans) + 1
    for k in range(chunks):
        x_keep[pl.ds(k * got_stride, got_stride), :] = got_ref[k].astype(f32)
    dact_keep[...] = dact_ref[...].astype(f32)
    mean, inverse = norm_ref[:rows], norm_ref[rows:]

    def x_hat_of(channel):
        x = channel_tokens(x_keep, channel, got_stride, micros, chunks, chans)
        return (x - mean) * inverse

    def const(channel, k):
        return (
            const_ref[2 * k, channel : channel + 1, :],
            const_ref[2 * k + 1, channel : channel + 1, :],
        )

    def total(x):
        return jnp.sum(x, axis=0, keepdims=True)

    for channel in range(chans):
        line = slice(channel, channel + 1)
        u = live * (x_hat_of(channel) * const_ref[gain, line] + const_ref[bias, line])
        u_prev = previous(u, micros, chunks)
        u_keep[channel] = u
        prev_keep[channel] = u_prev
        u_hi, u_lo = split(u)
        v_hi, v_lo = split(u * u_prev)
        for k, (left, right) in enumerate(((u_hi, v_hi), (u_hi, v_hi), (u_lo, v_lo))):
            uv_parts[channel, k * rows : (k + 1) * rows, :width] = left
            uv_parts[channel, k * rows : (k + 1) * rows, width:] = right
        y = y_ref[channel]
        density = jnp.exp(-0.5 * y * y) * (1.0 / math.sqrt(2.0 * math.pi))
        d_y = dact_keep[pl.ds(channel, rows, stride=chans), :] * (normal_cdf(y) + y * density)
        high, low_part = split(d_y)
        dy_parts[channel, :rows] = high
        dy_parts[channel, rows : 2 * rows] = low_part
        dy_parts[channel, 2 * rows :] = high

    for channel in range(chans):
        tables = [hankel(taps_ref[channel, 8 * k : 8 * k + 8], width) for k in range(2)]
        both = dy_parts[channel, : 2 * rows]
        duv = mm(both, jnp.concatenate([tables[0][0], tables[1][0]], axis=1))
        low_part = mm(both[:rows], jnp.concatenate([tables[0][1], tables[1][1]], axis=1))
        duv_keep[channel] = duv[:rows] + duv[rows:] + low_part

    for channel in range(chans):
        outer = mm(dy_parts[channel], uv_parts[channel], TN)
        for k in range(2):
            rolled = pltpu.roll(
                outer[:, k * width : (k + 1) * width], 1, axis=1, stride=1, stride_axis=0
            )
            line = total(jnp.where(passed, rolled, 0.0))
            high = line.astype(bf16).astype(f32)
            lag_keep[channel, k : k + 1, :] = high
            lag_keep[channel, 2 + k : 3 + k, :] = line - high
            if k == 0:
                sums_keep[channel : channel + 1, :] = jnp.where(
                    lanes(line.shape) == 0, line, 0.0
                )

    levels = int(math.log2(width)) - 3
    for channel in range(chans):
        high, low_part = mode_powers(rise_ref, channel, chans, levels, half)
        power_ref[channel, :width] = high
        power_ref[channel, width:] = low_part

    for channel in range(chans):
        both = dy_parts[channel, : 2 * rows]
        yd = mm(both, power_ref[channel, :width])
        low_part = mm(both[:rows], power_ref[channel, width:])
        yd_keep[channel] = yd[:rows] + yd[rows:] + low_part

    for channel in range(chans):
        adj = cmul(yd_keep[channel], const(channel, 2), half)
        for k in range(spans):
            moved = shift_chunks(adj, -(2**k), micros, chunks)
            adj = adj + cmul(moved, const(channel, 3 + k), half)
        adj = shift_chunks(adj, -1, micros, chunks)
        adj_keep[channel] = adj
        sent = jnp.concatenate(
            [cmul(adj, const(channel, 0), half), cmul(adj, const(channel, 1), half)], axis=0
        )
        high, low_part = split(sent * flip)
        sent_parts[channel, : 2 * rows] = high
        sent_parts[channel, 2 * rows :] = low_part

    for channel in range(chans):
        both = sent_parts[channel]
        cross = mm(both, power_ref[channel, :width], NT)
        cross = cross[: 2 * rows] + cross[2 * rows :]
        cross = cross + mm(both[: 2 * rows], power_ref[channel, width:], NT)
        d_v = duv_keep[channel, :, width:] + cross[rows:]
        d_u = duv_keep[channel, :, :width] + cross[:rows] + d_v * prev_keep[channel]
        d_u = d_u + following(d_v * u_keep[channel], micros, chunks)
        d_q = live * d_u
        sums_keep[chans + channel : chans + channel + 1, :] = total(d_q * x_hat_of(channel))
        sums_keep[2 * chans + channel : 2 * chans + channel + 1, :] = total(d_q)
        d_h = d_q * const_ref[gain, channel : channel + 1]
        for m in range(micros):
            head[pl.ds(m * chans + channel, chunks, stride=stride), :] = d_h[
                m * chunks : (m + 1) * chunks
            ]

    lag_keep[:, 4:, :] = jnp.zeros((chans, 12, width), f32)
    for channel in range(chans):
        lags = lag_keep[channel].astype(bf16)
        tops = mm(lags, power_ref[channel, :width]) + mm(lags, power_ref[channel, width:])
        dots[6, channel : channel + 1, :] = tops[0:1] + tops[2:3]
        dots[7, channel : channel + 1, :] = tops[1:2] + tops[3:4]
        adj, yd = adj_keep[channel], yd_keep[channel]
        adj_swap = swap(adj, half)
        high, low_part = uv_parts[channel, :rows], uv_parts[channel, 2 * rows :]
        parts = jnp.concatenate(
            [high[:, :width], high[:, width:], low_part[:, :width], low_part[:, width:]], axis=0
        )
        q = mm(parts, power_ref[channel, :width])
        q = q[: 2 * rows] + q[2 * rows :] + mm(parts[: 2 * rows], power_ref[channel, width:])
        uq, vq, start = q[:rows], q[rows:], start_ref[channel]
        pairs = ((uq, adj), (uq, adj_swap), (vq, adj), (vq, adj_swap), (start, yd))
        for k, (left, right) in enumerate(pairs + ((start, swap(yd, half)),)):
            dots[k, channel : channel + 1, :] = total(left * right)

    def whole_const(k):
        return const_ref[2 * k], const_ref[2 * k + 1]

    def dot(k):
        same, other = dots[k], dots[k + 1]
        return jnp.where(low, same - swap(same, half), other + swap(other, half))

    top_u, top_v = dots[6], dots[7]
    c = whole_const(3 + spans)
    modes = jnp.concatenate(
        [
            flip * (cmul(top_u, c, half) + dot(0)),
            flip * (cmul(top_v, c, half) + dot(2)),
            flip
            * (
                cmul(top_u, whole_const(0), half)
                + cmul(top_v, whole_const(1), half)
                + cmul(dot(4), whole_const(4 + spans), half)
            ),
        ],
        axis=0,
    )
    sums = jnp.sum(sums_keep[...].T, axis=0, keepdims=True)
    sums_hi = sums.astype(bf16).astype(f32)
    cut = micros * chans
    for k in range(chunks):
        at = k * stride + cut
        head[pl.ds(at, 3 * chans), :] = modes
        head[pl.ds(at + 3 * chans, 1), pl.ds(0, 3 * chans)] = sums_hi
        head[pl.ds(at + 3 * chans + 1, 1), pl.ds(0, 3 * chans)] = sums - sums_hi
        send_ref[k] = head[pl.ds(k * stride, stride), :].astype(bf16)


def backward_scratch(micros, chunks, chans, stride, width, lane):
    rows = micros * chunks
    return [
        pltpu.VMEM((3 * chans, lane), f32),
        pltpu.VMEM((chunks * stride, width), f32),
        pltpu.VMEM((chunks * micros * (chans + 6), width), f32),
        pltpu.VMEM((rows * chans, width), f32),
        pltpu.VMEM((chans, rows, width), f32),
        pltpu.VMEM((chans, rows, width), f32),
        pltpu.VMEM((chans, 3 * rows, width), bf16),
        pltpu.VMEM((chans, 3 * rows, 2 * width), bf16),
        pltpu.VMEM((chans, rows, lane), f32),
        pltpu.VMEM((chans, rows, 2 * width), f32),
        pltpu.VMEM((chans, 16, width), f32),
        pltpu.VMEM((chans, rows, lane), f32),
        pltpu.VMEM((chans, 4 * rows, lane), bf16),
        pltpu.VMEM((8, chans, lane), f32),
        pltpu.VMEM((chans, 2 * width, lane), bf16),
    ]


def gated(both, bias, g):
    wide = g.shape[1]
    value = both[:, :wide] + bias[:, :wide]
    gate = jax.nn.sigmoid(both[:, wide:] + bias[:, wide:])
    d_value = g * gate
    return value * gate, jnp.concatenate(
        [d_value.astype(bf16), (d_value * value * (1.0 - gate)).astype(bf16)], axis=1
    )


def project_kernel(width, place_ref, lens_ref, act_ref, *refs):
    refs, (dact_ref, d_keep) = refs[:-2], refs[-2:]
    full, rows = act_ref.shape
    peers = len(refs)
    wide = full // peers
    start = place_ref[1] * rows
    at = place_ref[0] * width + lax.rem(start, width)
    at = at + lax.broadcasted_iota(jnp.int32, (rows, wide), 0)
    live = (at < lens_ref[start // width]).astype(f32)
    act = act_ref[...].T

    def weight(ref):
        return jnp.concatenate(
            [ref[wide : wide + full, :], ref[wide + full : wide + 2 * full, :]], axis=1
        )

    for k, ref in enumerate(refs):
        g = live * ref[:wide, :].T.astype(f32)
        bias = ref[wide + 2 * full :, :].astype(f32)
        bias = jnp.concatenate(
            [bias[0:1] + bias[1:2] + bias[2:3], bias[3:4] + bias[4:5] + bias[5:6]], axis=1
        )
        d_both = gated(mm(act, weight(ref)), bias, g)[1]
        d_keep[:, 2 * k * wide : 2 * (k + 1) * wide] = d_both
    weights = jnp.concatenate([weight(ref) for ref in refs], axis=1)
    dact_ref[...] = mm(weights, d_keep[...], NT).astype(bf16)


def output_kernel(
    seqs,
    rank_ref,
    lens_ref,
    order_ref,
    tokens_ref,
    cot_ref,
    wv_ref,
    wg_ref,
    bv_ref,
    bg_ref,
    *refs,
):
    micros, wide, width = tokens_ref.shape
    acts_in, refs = refs[:micros], refs[micros:]
    out_ref, keep_ref, send_refs = refs[0], refs[1], refs[2:-2]
    d_keep, grad = refs[-2:]
    full = wv_ref.shape[0]
    at = rank_ref[0] * width + lax.broadcasted_iota(jnp.int32, (width, wide), 0)
    place = rank_ref[0] * width + lanes((1, width))
    weights = jnp.concatenate([wv_ref[...], wg_ref[...]], axis=1)
    bias = jnp.concatenate([bv_ref[...], bg_ref[...]], axis=1)
    for k in range(micros):
        m = order_ref[k]
        g = (at < lens_ref[m]).astype(f32) * cot_ref[m].T.astype(f32)
        added, d_both = gated(mm(acts_in[k][...].T, weights), bias, g)
        live = (place < lens_ref[m]).astype(f32)
        out_ref[m] = (live * (tokens_ref[m].astype(f32) + added.T)).astype(bf16)
        d_keep[k * width : (k + 1) * width] = d_both
    d_both = d_keep[...]
    acts = jnp.concatenate([ref[...] for ref in acts_in], axis=1)
    grad_w = mm(acts, d_both)
    grad_b = mm(jnp.ones((8, micros * width), bf16), d_both)
    row = lax.broadcasted_iota(jnp.int32, (8, wide), 0)
    small = jnp.where(row == 0, grad_b[:, :wide], grad_b[:, wide:])
    count = full // seqs
    for k in range(seqs):
        part = grad_w[k * count : (k + 1) * count]
        grad[k, pl.ds(0, count), :] = part[:, :wide]
        grad[k, pl.ds(count, count), :] = part[:, wide:]
        grad[k, pl.ds(2 * count, 8), :] = small
    place = rank_ref[0] >> 1
    for j in range(2):
        keep_ref[j] = grad[2 * place + j]
        for k, ref in enumerate(send_refs):
            ref[j] = grad[2 * (place ^ (k + 1)) + j].astype(bf16)


def parts_kernel(bit_ref, keep_in_ref, *refs):
    got_refs, (keep_ref, send_ref, total) = refs[:-3], refs[-3:]
    value = keep_in_ref[...]
    for ref in got_refs:
        value = value + ref[...].astype(f32)
    total[...] = value
    keep_ref[...] = total[bit_ref[0]]
    send_ref[...] = total[1 - bit_ref[0]].astype(bf16)


def last_kernel(left_ref, right_ref, wv_ref, wg_ref, bv_ref, bg_ref):
    count = wv_ref.shape[0]
    total = left_ref[...] + right_ref[...].astype(f32)
    wv_ref[...] = total[:count]
    wg_ref[...] = total[count : 2 * count]
    bv_ref[...] = total[2 * count : 2 * count + 1]
    bg_ref[...] = total[2 * count + 1 : 2 * count + 2]


def normal(tokens_ref, norm_ref, m):
    micros = tokens_ref.shape[0]
    return (tokens_ref[m].astype(f32) - norm_ref[m : m + 1]) * norm_ref[
        micros + m : micros + m + 1
    ]


def sums_kernel(got_ref, tokens_ref, *refs):
    stats_refs, (out_ref, head_ref, norm_ref) = refs[:-3], refs[-3:]
    micros, wide, width = tokens_ref.shape
    seqs, stride, _ = head_ref.shape
    chans = wide // seqs
    mean, inverse = merge(
        [ref[pl.ds(0, micros), :] for ref in stats_refs],
        [ref[pl.ds(micros, micros), :] for ref in stats_refs],
        wide,
    )
    norm_ref[pl.ds(0, micros), :] = mean
    norm_ref[pl.ds(micros, micros), :] = inverse
    cut = micros * chans
    turned = got_ref[:, pl.ds(0, cut), :].reshape(seqs * cut, width)
    head_ref[:, pl.ds(0, cut), :] = mm(turned, mirror(width)).reshape(seqs, cut, width)
    head_ref[:, pl.ds(cut, stride - cut), :] = got_ref[:, pl.ds(cut, stride - cut), :].astype(f32)
    for m in range(micros):
        d_hat = head_ref[:, pl.ds(m * chans, chans), :].reshape(wide, width)
        x_hat = normal(tokens_ref, norm_ref, m)
        out_ref[pl.ds(m, 1), :] = jnp.sum(d_hat, axis=0, keepdims=True)
        out_ref[pl.ds(micros + m, 1), :] = jnp.sum(d_hat * x_hat, axis=0, keepdims=True)


def final_kernel(
    rank_ref,
    lens_ref,
    head_ref,
    tokens_ref,
    cot_ref,
    norm_ref,
    *refs,
):
    hat_refs, refs = refs[:-7], refs[-7:]
    d_in_ref, b_ref, e_ref, c_ref, skip_ref, gain_ref, norm_bias_ref = refs
    micros, wide, width = tokens_ref.shape
    seqs, stride, _ = head_ref.shape
    peers = len(hat_refs)
    chans = wide // seqs
    hats = [ref[...] for ref in hat_refs]
    hat = sum(hats[1:], hats[0]) * (1.0 / (peers * wide))
    at = rank_ref[0] * width + lanes((1, width))
    for m in range(micros):
        live = (at < lens_ref[m]).astype(f32)
        d_hat = head_ref[:, pl.ds(m * chans, chans), :].reshape(wide, width)
        x_hat = normal(tokens_ref, norm_ref, m)
        inside = d_hat - hat[m : m + 1] - x_hat * hat[micros + m : micros + m + 1]
        d_in_ref[m] = (
            live * cot_ref[m].astype(f32) + norm_ref[micros + m : micros + m + 1] * inside
        )
    cut = micros * chans
    for k, ref in enumerate((b_ref, e_ref, c_ref)):
        modes = head_ref[:, pl.ds(cut + k * chans, chans), :]
        ref[...] = modes.reshape(wide, -1).T.reshape(ref.shape)
    place = lanes((1, wide)) // chans
    last = cut + 3 * chans
    for k, ref in enumerate((skip_ref, gain_ref, norm_bias_ref)):
        line = jnp.zeros((1, wide), f32)
        for s in range(seqs):
            own = head_ref[s, pl.ds(last, 1), :] + head_ref[s, pl.ds(last + 1, 1), :]
            own = pltpu.roll(own, (s - k) * chans % own.shape[1], axis=1)[:, :wide]
            line = jnp.where(place == s, own, line)
        ref[...] = line


def smem():
    return pl.BlockSpec(memory_space=pltpu.SMEM)


def vmem():
    return pl.BlockSpec(memory_space=pltpu.VMEM)


def in_hbm(x):
    return pltpu.with_memory_space_constraint(x, pltpu.HBM)


def shape_of(shape, kind=f32):
    return jax.ShapeDtypeStruct(shape, kind)


def kernel_call(kernel, name, scalars, arrays, outs, micros_of_time, limit=8, **more):
    ins = [smem()] * len(scalars) + [vmem()] * len(arrays)
    return pl.pallas_call(
        kernel,
        in_specs=ins,
        out_specs=[vmem()] * len(outs),
        out_shape=outs,
        compiler_params=pltpu.CompilerParams(vmem_limit_bytes=limit * 1024 * 1024),
        cost_estimate=cost(micros_of_time),
        name=name,
        **more,
    )(*scalars, *arrays)


def cost(micros_of_time):
    return pl.CostEstimate(
        flops=int(micros_of_time * 1e9), bytes_accessed=int(micros_of_time * 3e6), transcendentals=0
    )


def shards(
    tokens,
    lengths,
    ln_gain,
    ln_bias,
    b_coef,
    e_coef,
    c_coef,
    skip_gain,
    decay_rate,
    rotation,
    w_value,
    w_gate,
    bias_value,
    bias_gate,
    out_cotangent,
):
    micros, wide, width = tokens.shape
    modes = decay_rate.shape[1]
    full = w_value.shape[0]
    seqs = lax.axis_size("seq")
    peers = lax.axis_size("chan")
    seq_rank = lax.axis_index("seq").astype(jnp.int32)
    chan_rank = lax.axis_index("chan").astype(jnp.int32)
    chans = wide // seqs
    rows = micros * seqs
    own = micros * width // peers
    parts = width // own
    both = ("chan", "seq")
    lane = 2 * modes
    spans = int(math.log2(seqs))
    levels = int(math.log2(width)) - 3
    rank = seq_rank.reshape(1)
    lens = lengths.reshape(micros)
    place = jnp.stack([seq_rank, chan_rank])
    bias_rows = (bias_value.reshape(1, wide), bias_gate.reshape(1, wide))

    def exchange(x, axis):
        return lax.all_to_all(x, axis, 0, 0, tiled=True)

    def cross(x, by):
        return lax.ppermute(x, "chan", [(i, i ^ by) for i in range(peers)])

    hbm = pl.BlockSpec(memory_space=pltpu.HBM)
    x_send, part_stats = pl.pallas_call(
        functools.partial(pack_kernel, seqs),
        in_specs=[hbm],
        out_specs=[vmem()] * 2,
        out_shape=[
            shape_of((seqs, micros * (chans + 6), width), bf16),
            shape_of((2 * micros, width)),
        ],
        scratch_shapes=[
            pltpu.VMEM(tokens.shape, bf16),
            pltpu.SemaphoreType.DMA((micros,)),
        ],
        compiler_params=pltpu.CompilerParams(vmem_limit_bytes=8 * 1024 * 1024),
        cost_estimate=cost(1),
        name="pack",
    )(in_hbm(tokens))
    x_mine = exchange(x_send, "seq")
    stats = [part_stats] + [cross(part_stats, k) for k in range(1, peers)]

    cot, wv, wg, _ = lax.optimization_barrier((out_cotangent, w_value, w_gate, part_stats))
    cot_own = cot.reshape(micros, wide, parts, own).transpose(0, 2, 1, 3).reshape(peers, wide, own)
    weights = pl.pallas_call(
        gather_kernel,
        in_specs=[smem()] + [vmem()] * 2 + [hbm] * 3,
        out_specs=[vmem()] * peers,
        out_shape=[shape_of((wide + 2 * full + 16, own), bf16)] * peers,
        scratch_shapes=[pltpu.SemaphoreType.DMA((3 * peers,))],
        compiler_params=pltpu.CompilerParams(vmem_limit_bytes=8 * 1024 * 1024),
        cost_estimate=cost(1),
        name="weights",
    )(chan_rank.reshape(1), *bias_rows, in_hbm(cot_own), in_hbm(wv), in_hbm(wg))

    turned = [jnp.transpose(z, (0, 2, 1)) for z in (b_coef, e_coef, c_coef)]
    const, rise, taps, live = pl.pallas_call(
        functools.partial(table_kernel, chans, seqs, width),
        in_specs=[smem()] * 5 + [hbm] * 5,
        out_specs=[vmem()] * 4,
        out_shape=[
            shape_of((12 + 2 * spans, chans, lane)),
            shape_of(((8 + 2 * levels) * chans, lane)),
            shape_of((chans, 16, width)),
            shape_of((rows, width)),
        ],
        scratch_shapes=[pltpu.VMEM(turned[0].shape, f32)] * 3
        + [pltpu.VMEM((modes, wide), f32)] * 2
        + [
            pltpu.VMEM((wide, lane), f32),
            pltpu.VMEM((16 * chans, lane), f32),
            pltpu.SemaphoreType.DMA((5,)),
        ],
        compiler_params=pltpu.CompilerParams(vmem_limit_bytes=8 * 1024 * 1024),
        cost_estimate=cost(2),
        name="tables",
    )(rank, lens, skip_gain, ln_gain, ln_bias, *[in_hbm(z) for z in (*turned, decay_rate.T, rotation.T)])

    x_mine, const, weights = lax.optimization_barrier((x_mine, const, weights))
    x_stats = x_mine[:, micros * chans :]
    x_stats = [cross(x_stats, k) for k in range(1, peers)]
    weights = [weights[0]] + [cross(weights[k], k) for k in range(1, peers)]
    arrays = (x_mine, const, rise, taps, live, *x_stats)
    act, norm_mine, y_mine, start_mine = pl.pallas_call(
        functools.partial(forward_kernel, micros, seqs, chans, peers),
        in_specs=[vmem()] * len(arrays),
        out_specs=[vmem()] * 4,
        out_shape=[
            shape_of((rows * chans, width), bf16),
            shape_of((2 * rows, width)),
            shape_of((chans, rows, width)),
            shape_of((chans, rows, lane)),
        ],
        scratch_shapes=forward_scratch(micros, seqs, chans, peers, width, lane),
        compiler_params=pltpu.CompilerParams(vmem_limit_bytes=16 * 1024 * 1024),
        cost_estimate=cost(5),
        name="mixer_forward",
    )(*arrays)

    act = (
        act.reshape(micros, seqs, chans, parts, own)
        .transpose(0, 3, 1, 2, 4)
        .reshape(peers * seqs, chans, own)
    )
    act = exchange(act, both).reshape(full, own)
    (d_act,) = kernel_call(
        functools.partial(project_kernel, width),
        "project",
        (place, lens),
        (act, *weights),
        [shape_of((full, own), bf16)],
        2,
        limit=12,
        scratch_shapes=[pltpu.VMEM((own, 2 * full), bf16)],
    )

    acts = [act] + [cross(act, k) for k in range(1, peers)]
    if parts == 1:
        order = chan_rank ^ jnp.arange(peers, dtype=jnp.int32)
    else:
        stacked = jnp.stack(acts)[chan_rank ^ jnp.arange(peers, dtype=jnp.int32)]
        stacked = stacked.reshape(micros, parts, full, own).transpose(0, 2, 1, 3)
        stacked = stacked.reshape(micros, full, width)
        acts = [stacked[m] for m in range(micros)]
        order = jnp.arange(micros, dtype=jnp.int32)

    d_act = exchange(d_act.reshape(peers * seqs, chans, own), both)
    d_act = (
        d_act.reshape(micros, parts, seqs, chans, own)
        .transpose(0, 2, 3, 1, 4)
        .reshape(rows * chans, width)
    )
    count = full // seqs
    part = (2, 2 * count + 8, wide)
    out, keep, *blocks = kernel_call(
        functools.partial(output_kernel, seqs),
        "output",
        (rank, lens, order),
        (tokens, out_cotangent, w_value, w_gate) + bias_rows + tuple(acts),
        [shape_of(tokens.shape, bf16), shape_of(part)] + [shape_of(part, bf16)] * (seqs // 2 - 1),
        2,
        limit=12,
        scratch_shapes=[
            pltpu.VMEM((micros * width, 2 * wide), bf16),
            pltpu.VMEM((seqs,) + part[1:], f32),
        ],
    )
    blocks = [
        lax.ppermute(block, "seq", [(i, i ^ ((k + 1) << 1)) for i in range(seqs)])
        for k, block in enumerate(blocks)
    ]
    d_act, keep, *stats = lax.optimization_barrier((d_act, keep, *stats))
    stride = -(-((micros + 3) * chans + 2) // 16) * 16
    arrays = (x_mine, d_act, norm_mine, const, rise, taps, live, y_mine, start_mine)
    d_hat = pl.pallas_call(
        functools.partial(backward_kernel, micros, seqs, chans),
        in_specs=[vmem()] * len(arrays),
        out_specs=vmem(),
        out_shape=shape_of((seqs, stride, width), bf16),
        scratch_shapes=backward_scratch(micros, seqs, chans, stride, width, lane),
        compiler_params=pltpu.CompilerParams(vmem_limit_bytes=20 * 1024 * 1024),
        cost_estimate=cost(5),
        name="mixer_backward",
    )(*arrays)
    d_hat, *blocks = lax.optimization_barrier((d_hat, *blocks))
    keep, send = kernel_call(
        parts_kernel,
        "parts",
        (seq_rank.reshape(1) & 1,),
        (keep, *blocks),
        [shape_of(part[1:]), shape_of(part[1:], bf16)],
        1,
        scratch_shapes=[pltpu.VMEM(part, f32)],
    )
    got = lax.ppermute(send, "seq", [(i, i ^ 1) for i in range(seqs)])
    d_wv, d_wg, d_bv, d_bg = kernel_call(
        last_kernel,
        "last",
        (),
        (keep, got),
        [shape_of((count, wide))] * 2 + [shape_of((1, wide))] * 2,
        1,
    )
    got = exchange(d_hat, "seq")
    own_sums, head, norm = kernel_call(
        sums_kernel,
        "sums",
        (),
        (got, tokens, *stats),
        [
            shape_of((2 * micros, width)),
            shape_of((seqs, stride, width)),
            shape_of((2 * micros, width)),
        ],
        1,
    )
    hat_sums = [own_sums] + [cross(own_sums, k) for k in range(1, peers)]
    mode_grad = shape_of((2, modes, wide))
    d_input, d_b, d_e, d_c, d_skip, d_gain, d_bias = kernel_call(
        final_kernel,
        "final",
        (rank, lens),
        (head, tokens, out_cotangent, norm, *hat_sums),
        [shape_of(tokens.shape)]
        + [mode_grad] * 3
        + [shape_of((1, wide))] * 3,
        2,
    )
    d_b, d_e, d_c = [jnp.transpose(z, (0, 2, 1)) for z in (d_b, d_e, d_c)]
    d_skip, d_gain, d_bias, d_bv, d_bg = [
        z.reshape(wide) for z in (d_skip, d_gain, d_bias, d_bv, d_bg)
    ]
    return (out, d_input, d_gain, d_bias, d_b, d_e, d_c, d_skip, d_wv, d_wg, d_bv, d_bg)


def solution(mesh):
    chan = P("chan")
    modes = P(None, "chan", None)
    table = P("chan", None)
    weight = P(None, "chan")
    rows = P(None, "chan", "seq")
    spread = P("seq", "chan")
    return jax.shard_map(
        shards,
        mesh=mesh,
        in_specs=(
            rows,
            P(),
            chan,
            chan,
            modes,
            modes,
            modes,
            chan,
            table,
            table,
            weight,
            weight,
            chan,
            chan,
            rows,
        ),
        out_specs=(
            rows,
            rows,
            chan,
            chan,
            modes,
            modes,
            modes,
            chan,
            spread,
            spread,
            chan,
            chan,
        ),
        check_vma=False,
    )
```

```python
import functools
import math

import jax
import jax.numpy as jnp
from jax import lax
from jax.experimental import pallas as pl
from jax.experimental.pallas import tpu as pltpu
from jax.sharding import PartitionSpec as P

f32 = jnp.float32
bf16 = jnp.bfloat16
epsilon = 1e-05
NN = (((1,), (0,)), ((), ()))
NT = (((1,), (1,)), ((), ()))
TN = (((0,), (0,)), ((), ()))


def mm(left, right, dims=NN):
    return lax.dot_general(left, right, dims, preferred_element_type=f32)


def split(x):
    high = x.astype(bf16)
    return high, (x - high.astype(f32)).astype(bf16)


def swap(x, half):
    return pltpu.roll(x, half, axis=x.ndim - 1)


def lanes(shape):
    return lax.broadcasted_iota(jnp.int32, shape, len(shape) - 1)


def pair(z, half):
    low = lanes(z.shape) < half
    turned = swap(z, half)
    return jnp.where(low, z, turned), jnp.where(low, -turned, z)


def cmul(x, z, half):
    return x * z[0] + swap(x, half) * z[1]


def normal_cdf(y):
    return 0.5 * (1.0 + lax.erf(y * (1.0 / math.sqrt(2.0))))


def mirror(width):
    shape = (width, width)
    at = lanes(shape) + lax.broadcasted_iota(jnp.int32, shape, 0)
    return (at == width - 1).astype(f32).astype(bf16)


def live_rows(lens_ref, micros, chunks, width):
    shape = (chunks, width)
    at = lax.broadcasted_iota(jnp.int32, shape, 0) * width + (width - 1 - lanes(shape))
    rows = [(at < lens_ref[m]).astype(f32) for m in range(micros)]
    return jnp.concatenate(rows, axis=0)


def merge(means, squares, count):
    parts = len(means)
    mean = sum(means[1:], means[0]) * (1.0 / parts)
    square = sum(squares[1:], squares[0])
    for part in means:
        square = square + count * jnp.square(part - mean)
    return mean, lax.rsqrt(square * (1.0 / (parts * count)) + epsilon)


def fetch(copies):
    for copy in copies:
        copy.start()


def shift_chunks(x, by, micros, chunks):
    cube = x.reshape(micros, chunks, x.shape[-1])
    place = lax.broadcasted_iota(jnp.int32, cube.shape, 1)
    if by > 0:
        moved = jnp.where(place >= by, pltpu.roll(cube, by, axis=1), 0.0)
    else:
        moved = jnp.where(place < chunks + by, pltpu.roll(cube, chunks + by, axis=1), 0.0)
    return moved.reshape(x.shape)


def previous(u, micros, chunks):
    width = u.shape[1]
    turned = pltpu.roll(u, width - 1, axis=1)
    return jnp.where(
        lanes(u.shape) == width - 1, shift_chunks(turned, 1, micros, chunks), turned
    )


def following(u, micros, chunks):
    turned = pltpu.roll(u, 1, axis=1)
    return jnp.where(lanes(u.shape) == 0, shift_chunks(turned, -1, micros, chunks), turned)


def hankel(first, width):
    blocks = []
    for k in range(width // 8):
        by = width - 8 - 8 * k
        blocks.append(pltpu.roll(first, by, axis=1) if by else first)
    table = jnp.concatenate(blocks, axis=0)
    at = lanes(table.shape) + lax.broadcasted_iota(jnp.int32, table.shape, 0)
    return split(jnp.where(at >= width - 1, table, 0.0))


def gather_kernel(rank_ref, bv_ref, bg_ref, cot_hbm, wv_hbm, wg_hbm, *refs):
    outs, sems = refs[:-1], refs[-1]
    peers, wide, _ = cot_hbm.shape
    full = wv_hbm.shape[0]
    copies = []
    for k, out in enumerate(outs):
        for source, start, count in (
            (cot_hbm.at[rank_ref[0] ^ k], 0, wide),
            (wv_hbm, wide, full),
            (wg_hbm, wide + full, full),
        ):
            copies.append(
                pltpu.make_async_copy(
                    source, out.at[pl.ds(start, count), :], sems.at[len(copies)]
                )
            )
    fetch(copies)
    pieces = []
    for value in (bv_ref[...], bg_ref[...]):
        for _ in range(3):
            high = value.astype(bf16).astype(f32)
            pieces.append(high)
            value = value - high
    pieces.append(jnp.zeros((10, wide), f32))
    biases = jnp.concatenate(pieces, axis=0).astype(bf16)
    for out in outs:
        out[pl.ds(wide + 2 * full, 16), :] = biases
    for copy in copies:
        copy.wait()


def pack_kernel(seqs, tokens_hbm, send_ref, stats_ref, tokens, sems):
    micros, wide, width = tokens.shape
    chans = wide // seqs
    copies = [
        pltpu.make_async_copy(tokens_hbm.at[m], tokens.at[m], sems.at[m]) for m in range(micros)
    ]
    fetch(copies)
    turn = mirror(width)
    means, squares = [], []
    for copy in copies:
        copy.wait()
    for m in range(micros):
        x = tokens[m].astype(f32)
        mean = jnp.sum(x, axis=0, keepdims=True) * (1.0 / wide)
        means.append(mean)
        squares.append(jnp.sum(jnp.square(x - mean), axis=0, keepdims=True))
        turned = mm(tokens[m], turn).astype(bf16)
        send_ref[:, pl.ds(m * chans, chans), :] = turned.reshape(seqs, chans, width)
    stats = jnp.concatenate(means + squares, axis=0)
    stats_ref[...] = stats
    rest, lines = stats, []
    for _ in range(3):
        high = rest.astype(bf16).astype(f32)
        lines.append(high)
        rest = rest - high
    tail = jnp.concatenate(lines, axis=0).astype(bf16)
    tail = mm(tail, turn).astype(bf16)
    for k in range(seqs):
        send_ref[k, pl.ds(micros * chans, 6 * micros), :] = tail


def table_kernel(
    chans,
    seqs,
    width,
    rank_ref,
    lens_ref,
    skip_ref,
    gain_ref,
    bias_ref,
    b_hbm,
    e_hbm,
    c_hbm,
    decay_hbm,
    turn_hbm,
    const_ref,
    rise,
    taps_ref,
    live_ref,
    b_ref,
    e_ref,
    c_ref,
    decay_ref,
    turn_ref,
    turned_keep,
    coefs,
    sems,
):
    half = decay_ref.shape[0]
    loads = [
        pltpu.make_async_copy(source, target, sems.at[k])
        for k, (source, target) in enumerate(
            (
                (b_hbm, b_ref),
                (e_hbm, e_ref),
                (c_hbm, c_ref),
                (decay_hbm, decay_ref),
                (turn_hbm, turn_ref),
            )
        )
    ]
    fetch(loads)
    for load in loads:
        load.wait()
    base = rank_ref[0] * chans
    levels = int(math.log2(width)) - 3
    spans = int(math.log2(seqs))

    def own(value):
        turned_keep[...] = value.T
        return turned_keep[pl.ds(base, chans), :]

    b = own(b_ref[...].reshape(2 * half, -1))
    e = own(e_ref[...].reshape(2 * half, -1))
    c = own(c_ref[...].reshape(2 * half, -1))
    mixed = own(jnp.concatenate([decay_ref[...], turn_ref[...]], axis=0))
    low = lanes(mixed.shape) < half
    other = swap(mixed, half)
    decay = jnp.where(low, mixed, other)
    turn = jnp.where(low, other, mixed)
    turned = jnp.where(low, jnp.cos(turn), jnp.sin(turn))
    a = jnp.exp(-decay) * turned
    inverse = pair(jnp.exp(decay) * jnp.where(low, turned, -turned), half)
    a_pair = pair(a, half)
    power = jnp.where(low, 1.0, 0.0)
    for k in range(8):
        rise[pl.ds(k * chans, chans), :] = power
        power = cmul(power, a_pair, half) if k else a
    for k in range(levels):
        power_pair = pair(power, half)
        rise[pl.ds((8 + 2 * k) * chans, chans), :] = power_pair[0]
        rise[pl.ds((9 + 2 * k) * chans, chans), :] = power_pair[1]
        power = cmul(power, power_pair, half)
    kept = [pair(b, half), pair(e, half), pair(cmul(a, pair(c, half), half), half)]
    for k in range(spans):
        kept.append(pair(power, half))
        power = cmul(power, kept[-1], half)
    kept += [pair(c, half), a_pair]
    for k, both in enumerate(kept):
        const_ref[2 * k] = both[0]
        const_ref[2 * k + 1] = both[1]
    sign = jnp.where(low, 1.0, -1.0)
    for j in range(2):
        coef = cmul(c, kept[j], half)
        for k in range(7, -1, -1):
            coefs[pl.ds((8 * j + k) * chans, chans), :] = coef * sign
            coef = cmul(coef, inverse, half)

    live_ref[...] = live_rows(lens_ref, lens_ref.shape[0], seqs, width)
    for channel in range(chans):
        for k, ref in enumerate((gain_ref, bias_ref)):
            const_ref[2 * len(kept) + k, channel : channel + 1, :] = jnp.full(
                (1, 2 * half), ref[base + channel], f32
            )
        high, low_part = mode_powers(rise, channel, chans, levels, half)
        coef = coefs[pl.ds(channel, 16, stride=chans), :]
        coef_hi = coef.astype(bf16).astype(f32)
        both = jnp.concatenate([coef_hi, coef - coef_hi], axis=0).astype(bf16)
        taps = mm(both, high, NT) + mm(both, low_part, NT)
        taps = taps[:16] + taps[16:]
        at = lanes(taps.shape) + lax.broadcasted_iota(jnp.int32, taps.shape, 0)
        taps_ref[channel] = taps + jnp.where(at == 7, skip_ref[base + channel], 0.0)


def mode_powers(rise_ref, channel, chans, levels, half):
    up = rise_ref[pl.ds(channel, 8, stride=chans), :]
    for k in range(levels):
        at = (8 + 2 * k) * chans + channel
        by = (rise_ref[at : at + 1, :], rise_ref[at + chans : at + chans + 1, :])
        up = jnp.concatenate([up, cmul(up, by, half)], axis=0)
    return split(up)


def own_rows(keep, at, stride, micros, chunks):
    return jnp.concatenate(
        [keep[pl.ds(at + m, chunks, stride=stride), :] for m in range(micros)], axis=0
    )


def channel_tokens(keep, channel, stride, micros, chunks, chans):
    return jnp.concatenate(
        [keep[pl.ds(m * chans + channel, chunks, stride=stride), :] for m in range(micros)],
        axis=0,
    )


def forward_kernel(
    micros,
    chunks,
    chans,
    peers,
    got_ref,
    const_ref,
    rise_ref,
    taps_ref,
    live_ref,
    *refs,
):
    stats_refs, refs = refs[: peers - 1], refs[peers - 1 :]
    act_ref, norm_ref, y_ref, start_ref, act_keep, x_keep, stats_keep = refs[:7]
    parts, wide_parts, sent_parts, kept_ref, power_ref = refs[7:]
    width = got_ref.shape[2]
    half = const_ref.shape[2] // 2
    spans = int(math.log2(chunks))
    rows = micros * chunks
    stride = got_ref.shape[1]
    flip = jnp.where(lanes((1, 2 * half)) < half, 1.0, -1.0)

    def const(channel, k):
        return (
            const_ref[2 * k, channel : channel + 1, :],
            const_ref[2 * k + 1, channel : channel + 1, :],
        )

    live = live_ref[...]
    gain, bias = 2 * (5 + spans), 2 * (5 + spans) + 1
    for k in range(chunks):
        x_keep[pl.ds(k * stride, stride), :] = got_ref[k].astype(f32)
    means, squares = [], []
    for j in range(peers):
        keep, step, at = x_keep, stride, micros * chans
        if j:
            keep, step, at = stats_keep.at[j - 1], 6 * micros, 0
            for k in range(chunks):
                keep[pl.ds(k * step, step), :] = stats_refs[j - 1][k].astype(f32)
        lines = [own_rows(keep, at + q * micros, step, micros, chunks) for q in range(5)]
        means.append(lines[0] + lines[2] + lines[4])
        squares.append(lines[1] + lines[3])
    mean, inverse = merge(means, squares, chans * chunks)
    norm_ref[pl.ds(0, rows), :] = mean
    norm_ref[pl.ds(rows, rows), :] = inverse

    for channel in range(chans):
        x_hat = channel_tokens(x_keep, channel, stride, micros, chunks, chans) - mean
        line = slice(channel, channel + 1)
        u = live * (x_hat * inverse * const_ref[gain, line] + const_ref[bias, line])
        u_hi, u_lo = split(u)
        v_hi, v_lo = split(u * previous(u, micros, chunks))
        for k, part in enumerate((u_hi, v_hi, u_lo, v_lo)):
            parts[channel, k * rows : (k + 1) * rows] = part
        wide_parts[channel, :rows, :width] = u_hi
        wide_parts[channel, :rows, width:] = v_hi
        wide_parts[channel, rows:, :width] = u_lo
        wide_parts[channel, rows:, width:] = v_lo

    levels = int(math.log2(width)) - 3
    for channel in range(chans):
        high, low_part = mode_powers(rise_ref, channel, chans, levels, half)
        power_ref[channel, :width] = high
        power_ref[channel, width:] = low_part

    for channel in range(chans):
        q = mm(parts[channel], power_ref[channel, :width])
        kept_ref[channel, : 2 * rows] = (
            q[: 2 * rows]
            + q[2 * rows :]
            + mm(parts[channel, : 2 * rows], power_ref[channel, width:])
        )

    for channel in range(chans):
        uq, vq = kept_ref[channel, :rows], kept_ref[channel, rows : 2 * rows]
        state = cmul(uq, const(channel, 0), half) + cmul(vq, const(channel, 1), half)
        for k in range(spans):
            moved = shift_chunks(state, 2**k, micros, chunks)
            state = state + cmul(moved, const(channel, 3 + k), half)
        start = shift_chunks(state, 1, micros, chunks)
        start_ref[channel] = start
        high, low_part = split(cmul(start, const(channel, 2), half) * flip)
        sent_parts[channel, :rows] = high
        sent_parts[channel, rows:] = low_part

    for channel in range(chans):
        tables = [hankel(taps_ref[channel, 8 * k : 8 * k + 8], width) for k in range(2)]
        both = wide_parts[channel]
        y = mm(both, jnp.concatenate([tables[0][0], tables[1][0]], axis=0))
        low_part = mm(both[:rows], jnp.concatenate([tables[0][1], tables[1][1]], axis=0))
        y_ref[channel] = y[:rows] + y[rows:] + low_part

    for channel in range(chans):
        both = sent_parts[channel]
        cross = mm(both, power_ref[channel, :width], NT)
        y = y_ref[channel] + cross[:rows] + cross[rows:]
        y = y + mm(both[:rows], power_ref[channel, width:], NT)
        y_ref[channel] = y
        act = y * normal_cdf(y)
        for m in range(micros):
            act_keep[pl.ds(m * chunks * chans + channel, chunks, stride=chans), :] = act[
                m * chunks : (m + 1) * chunks
            ]
    act_ref[...] = act_keep[: rows * chans].astype(bf16)


def forward_scratch(micros, chunks, chans, peers, width, lane):
    rows = micros * chunks
    return [
        pltpu.VMEM(((rows + 1) * chans, width), f32),
        pltpu.VMEM(((chunks + 1) * micros * (chans + 6), width), f32),
        pltpu.VMEM((peers - 1, 6 * (rows + micros), width), f32),
        pltpu.VMEM((chans, 4 * rows, width), bf16),
        pltpu.VMEM((chans, 2 * rows, 2 * width), bf16),
        pltpu.VMEM((chans, 2 * rows, lane), bf16),
        pltpu.VMEM((chans, 2 * rows, lane), f32),
        pltpu.VMEM((chans, 2 * width, lane), bf16),
    ]


def backward_kernel(
    micros,
    chunks,
    chans,
    got_ref,
    dact_ref,
    norm_ref,
    const_ref,
    rise_ref,
    taps_ref,
    live_ref,
    y_ref,
    start_ref,
    send_ref,
    sums_keep,
    head,
    x_keep,
    dact_keep,
    u_keep,
    prev_keep,
    dy_parts,
    uv_parts,
    yd_keep,
    duv_keep,
    lag_keep,
    adj_keep,
    sent_parts,
    dots,
    power_ref,
):
    width = got_ref.shape[2]
    half = const_ref.shape[2] // 2
    spans = int(math.log2(chunks))
    rows = micros * chunks
    stride = send_ref.shape[1]
    got_stride = got_ref.shape[1]
    shape = (width, width)
    passed = lanes(shape) <= lax.broadcasted_iota(jnp.int32, shape, 0)
    low = lanes((1, 2 * half)) < half
    flip = jnp.where(low, 1.0, -1.0)
    live = live_ref[...]
    gain, bias = 2 * (5 + spans), 2 * (5 + spans) + 1
    for k in range(chunks):
        x_keep[pl.ds(k * got_stride, got_stride), :] = got_ref[k].astype(f32)
    dact_keep[: rows * chans] = dact_ref[...].astype(f32)
    mean, inverse = norm_ref[:rows], norm_ref[rows:]

    def x_hat_of(channel):
        x = channel_tokens(x_keep, channel, got_stride, micros, chunks, chans)
        return (x - mean) * inverse

    def const(channel, k):
        return (
            const_ref[2 * k, channel : channel + 1, :],
            const_ref[2 * k + 1, channel : channel + 1, :],
        )

    def total(x):
        return jnp.sum(x, axis=0, keepdims=True)

    for channel in range(chans):
        line = slice(channel, channel + 1)
        u = live * (x_hat_of(channel) * const_ref[gain, line] + const_ref[bias, line])
        u_prev = previous(u, micros, chunks)
        u_keep[channel] = u
        prev_keep[channel] = u_prev
        u_hi, u_lo = split(u)
        v_hi, v_lo = split(u * u_prev)
        for k, (left, right) in enumerate(((u_hi, v_hi), (u_hi, v_hi), (u_lo, v_lo))):
            uv_parts[channel, k * rows : (k + 1) * rows, :width] = left
            uv_parts[channel, k * rows : (k + 1) * rows, width:] = right
        y = y_ref[channel]
        density = jnp.exp(-0.5 * y * y) * (1.0 / math.sqrt(2.0 * math.pi))
        d_y = dact_keep[pl.ds(channel, rows, stride=chans), :] * (normal_cdf(y) + y * density)
        high, low_part = split(d_y)
        dy_parts[channel, :rows] = high
        dy_parts[channel, rows : 2 * rows] = low_part
        dy_parts[channel, 2 * rows :] = high

    for channel in range(chans):
        tables = [hankel(taps_ref[channel, 8 * k : 8 * k + 8], width) for k in range(2)]
        both = dy_parts[channel, : 2 * rows]
        duv = mm(both, jnp.concatenate([tables[0][0], tables[1][0]], axis=1))
        low_part = mm(both[:rows], jnp.concatenate([tables[0][1], tables[1][1]], axis=1))
        duv_keep[channel] = duv[:rows] + duv[rows:] + low_part

    for channel in range(chans):
        outer = mm(dy_parts[channel], uv_parts[channel], TN)
        for k in range(2):
            rolled = pltpu.roll(
                outer[:, k * width : (k + 1) * width], 1, axis=1, stride=1, stride_axis=0
            )
            line = total(jnp.where(passed, rolled, 0.0))
            high = line.astype(bf16).astype(f32)
            lag_keep[channel, k : k + 1, :] = high
            lag_keep[channel, 2 + k : 3 + k, :] = line - high
            if k == 0:
                sums_keep[channel : channel + 1, :] = jnp.where(
                    lanes(line.shape) == 0, line, 0.0
                )

    levels = int(math.log2(width)) - 3
    for channel in range(chans):
        high, low_part = mode_powers(rise_ref, channel, chans, levels, half)
        power_ref[channel, :width] = high
        power_ref[channel, width:] = low_part

    for channel in range(chans):
        both = dy_parts[channel, : 2 * rows]
        yd = mm(both, power_ref[channel, :width])
        low_part = mm(both[:rows], power_ref[channel, width:])
        yd_keep[channel] = yd[:rows] + yd[rows:] + low_part

    for channel in range(chans):
        adj = cmul(yd_keep[channel], const(channel, 2), half)
        for k in range(spans):
            moved = shift_chunks(adj, -(2**k), micros, chunks)
            adj = adj + cmul(moved, const(channel, 3 + k), half)
        adj = shift_chunks(adj, -1, micros, chunks)
        adj_keep[channel] = adj
        sent = jnp.concatenate(
            [cmul(adj, const(channel, 0), half), cmul(adj, const(channel, 1), half)], axis=0
        )
        high, low_part = split(sent * flip)
        sent_parts[channel, : 2 * rows] = high
        sent_parts[channel, 2 * rows :] = low_part

    for channel in range(chans):
        both = sent_parts[channel]
        cross = mm(both, power_ref[channel, :width], NT)
        cross = cross[: 2 * rows] + cross[2 * rows :]
        cross = cross + mm(both[: 2 * rows], power_ref[channel, width:], NT)
        d_v = duv_keep[channel, :, width:] + cross[rows:]
        d_u = duv_keep[channel, :, :width] + cross[:rows] + d_v * prev_keep[channel]
        d_u = d_u + following(d_v * u_keep[channel], micros, chunks)
        d_q = live * d_u
        sums_keep[chans + channel : chans + channel + 1, :] = total(d_q * x_hat_of(channel))
        sums_keep[2 * chans + channel : 2 * chans + channel + 1, :] = total(d_q)
        d_h = d_q * const_ref[gain, channel : channel + 1]
        for m in range(micros):
            head[pl.ds(m * chans + channel, chunks, stride=stride), :] = d_h[
                m * chunks : (m + 1) * chunks
            ]

    lag_keep[:, 4:, :] = jnp.zeros((chans, 12, width), f32)
    for channel in range(chans):
        lags = lag_keep[channel].astype(bf16)
        tops = mm(lags, power_ref[channel, :width]) + mm(lags, power_ref[channel, width:])
        dots[6, channel : channel + 1, :] = tops[0:1] + tops[2:3]
        dots[7, channel : channel + 1, :] = tops[1:2] + tops[3:4]
        adj, yd = adj_keep[channel], yd_keep[channel]
        adj_swap = swap(adj, half)
        high, low_part = uv_parts[channel, :rows], uv_parts[channel, 2 * rows :]
        parts = jnp.concatenate(
            [high[:, :width], high[:, width:], low_part[:, :width], low_part[:, width:]], axis=0
        )
        q = mm(parts, power_ref[channel, :width])
        q = q[: 2 * rows] + q[2 * rows :] + mm(parts[: 2 * rows], power_ref[channel, width:])
        uq, vq, start = q[:rows], q[rows:], start_ref[channel]
        pairs = ((uq, adj), (uq, adj_swap), (vq, adj), (vq, adj_swap), (start, yd))
        for k, (left, right) in enumerate(pairs + ((start, swap(yd, half)),)):
            dots[k, channel : channel + 1, :] = total(left * right)

    def whole_const(k):
        return const_ref[2 * k], const_ref[2 * k + 1]

    def dot(k):
        same, other = dots[k], dots[k + 1]
        return jnp.where(low, same - swap(same, half), other + swap(other, half))

    top_u, top_v = dots[6], dots[7]
    c = whole_const(3 + spans)
    modes = jnp.concatenate(
        [
            flip * (cmul(top_u, c, half) + dot(0)),
            flip * (cmul(top_v, c, half) + dot(2)),
            flip
            * (
                cmul(top_u, whole_const(0), half)
                + cmul(top_v, whole_const(1), half)
                + cmul(dot(4), whole_const(4 + spans), half)
            ),
        ],
        axis=0,
    )
    sums = jnp.sum(sums_keep[...].T, axis=0, keepdims=True)
    sums_hi = sums.astype(bf16).astype(f32)
    cut = micros * chans
    for k in range(chunks):
        at = k * stride + cut
        head[pl.ds(at, 3 * chans), :] = modes
        head[pl.ds(at + 3 * chans, 1), pl.ds(0, 3 * chans)] = sums_hi
        head[pl.ds(at + 3 * chans + 1, 1), pl.ds(0, 3 * chans)] = sums - sums_hi
        send_ref[k] = head[pl.ds(k * stride, stride), :].astype(bf16)


def backward_scratch(micros, chunks, chans, stride, width, lane):
    rows = micros * chunks
    return [
        pltpu.VMEM((3 * chans, lane), f32),
        pltpu.VMEM(((chunks + 1) * stride, width), f32),
        pltpu.VMEM(((chunks + 1) * micros * (chans + 6), width), f32),
        pltpu.VMEM(((rows + 1) * chans, width), f32),
        pltpu.VMEM((chans, rows, width), f32),
        pltpu.VMEM((chans, rows, width), f32),
        pltpu.VMEM((chans, 3 * rows, width), bf16),
        pltpu.VMEM((chans, 3 * rows, 2 * width), bf16),
        pltpu.VMEM((chans, rows, lane), f32),
        pltpu.VMEM((chans, rows, 2 * width), f32),
        pltpu.VMEM((chans, 16, width), f32),
        pltpu.VMEM((chans, rows, lane), f32),
        pltpu.VMEM((chans, 4 * rows, lane), bf16),
        pltpu.VMEM((8, chans, lane), f32),
        pltpu.VMEM((chans, 2 * width, lane), bf16),
    ]


def gated(both, bias, g):
    wide = g.shape[1]
    value = both[:, :wide] + bias[:, :wide]
    gate = jax.nn.sigmoid(both[:, wide:] + bias[:, wide:])
    d_value = g * gate
    return value * gate, jnp.concatenate(
        [d_value.astype(bf16), (d_value * value * (1.0 - gate)).astype(bf16)], axis=1
    )


def project_kernel(width, place_ref, lens_ref, act_ref, *refs):
    refs, (dact_ref, d_keep) = refs[:-2], refs[-2:]
    full, rows = act_ref.shape
    peers = len(refs)
    wide = full // peers
    start = place_ref[1] * rows
    at = place_ref[0] * width + lax.rem(start, width)
    at = at + lax.broadcasted_iota(jnp.int32, (rows, wide), 0)
    live = (at < lens_ref[start // width]).astype(f32)
    act = act_ref[...].T

    def weight(ref):
        return jnp.concatenate(
            [ref[wide : wide + full, :], ref[wide + full : wide + 2 * full, :]], axis=1
        )

    for k, ref in enumerate(refs):
        g = live * ref[:wide, :].T.astype(f32)
        bias = ref[wide + 2 * full :, :].astype(f32)
        bias = jnp.concatenate(
            [bias[0:1] + bias[1:2] + bias[2:3], bias[3:4] + bias[4:5] + bias[5:6]], axis=1
        )
        d_both = gated(mm(act, weight(ref)), bias, g)[1]
        d_keep[:, 2 * k * wide : 2 * (k + 1) * wide] = d_both
    weights = jnp.concatenate([weight(ref) for ref in refs], axis=1)
    dact_ref[...] = mm(weights, d_keep[...], NT).astype(bf16)


def output_kernel(
    seqs,
    rank_ref,
    lens_ref,
    order_ref,
    tokens_ref,
    cot_ref,
    wv_ref,
    wg_ref,
    bv_ref,
    bg_ref,
    *refs,
):
    micros, wide, width = tokens_ref.shape
    acts_in, refs = refs[:micros], refs[micros:]
    out_ref, keep_ref, send_refs = refs[0], refs[1], refs[2:-2]
    d_keep, grad = refs[-2:]
    full = wv_ref.shape[0]
    at = rank_ref[0] * width + lax.broadcasted_iota(jnp.int32, (width, wide), 0)
    place = rank_ref[0] * width + lanes((1, width))
    weights = jnp.concatenate([wv_ref[...], wg_ref[...]], axis=1)
    bias = jnp.concatenate([bv_ref[...], bg_ref[...]], axis=1)
    for k in range(micros):
        m = order_ref[k]
        g = (at < lens_ref[m]).astype(f32) * cot_ref[m].T.astype(f32)
        added, d_both = gated(mm(acts_in[k][...].T, weights), bias, g)
        live = (place < lens_ref[m]).astype(f32)
        out_ref[m] = (live * (tokens_ref[m].astype(f32) + added.T)).astype(bf16)
        d_keep[k * width : (k + 1) * width] = d_both
    d_both = d_keep[...]
    acts = jnp.concatenate([ref[...] for ref in acts_in], axis=1)
    grad_w = mm(acts, d_both)
    grad_b = mm(jnp.ones((8, micros * width), bf16), d_both)
    row = lax.broadcasted_iota(jnp.int32, (8, wide), 0)
    small = jnp.where(row == 0, grad_b[:, :wide], grad_b[:, wide:])
    count = full // seqs
    for k in range(seqs):
        part = grad_w[k * count : (k + 1) * count]
        grad[k, pl.ds(0, count), :] = part[:, :wide]
        grad[k, pl.ds(count, count), :] = part[:, wide:]
        grad[k, pl.ds(2 * count, 8), :] = small
    place = rank_ref[0] >> 1
    for j in range(2):
        keep_ref[j] = grad[2 * place + j]
        for k, ref in enumerate(send_refs):
            ref[j] = grad[2 * (place ^ (k + 1)) + j].astype(bf16)


def parts_kernel(bit_ref, keep_in_ref, *refs):
    got_refs, (keep_ref, send_ref, total) = refs[:-3], refs[-3:]
    value = keep_in_ref[...]
    for ref in got_refs:
        value = value + ref[...].astype(f32)
    total[...] = value
    keep_ref[...] = total[bit_ref[0]]
    send_ref[...] = total[1 - bit_ref[0]].astype(bf16)


def last_kernel(left_ref, right_ref, wv_ref, wg_ref, bv_ref, bg_ref):
    count = wv_ref.shape[0]
    total = left_ref[...] + right_ref[...].astype(f32)
    wv_ref[...] = total[:count]
    wg_ref[...] = total[count : 2 * count]
    bv_ref[...] = total[2 * count : 2 * count + 1]
    bg_ref[...] = total[2 * count + 1 : 2 * count + 2]


def normal(tokens_ref, norm_ref, m):
    micros = tokens_ref.shape[0]
    return (tokens_ref[m].astype(f32) - norm_ref[m : m + 1]) * norm_ref[
        micros + m : micros + m + 1
    ]


def sums_kernel(got_ref, tokens_ref, *refs):
    stats_refs, (out_ref, head_ref, norm_ref) = refs[:-3], refs[-3:]
    micros, wide, width = tokens_ref.shape
    seqs, stride, _ = head_ref.shape
    chans = wide // seqs
    mean, inverse = merge(
        [ref[pl.ds(0, micros), :] for ref in stats_refs],
        [ref[pl.ds(micros, micros), :] for ref in stats_refs],
        wide,
    )
    norm_ref[pl.ds(0, micros), :] = mean
    norm_ref[pl.ds(micros, micros), :] = inverse
    cut = micros * chans
    turned = got_ref[:, pl.ds(0, cut), :].reshape(seqs * cut, width)
    head_ref[:, pl.ds(0, cut), :] = mm(turned, mirror(width)).reshape(seqs, cut, width)
    head_ref[:, pl.ds(cut, stride - cut), :] = got_ref[:, pl.ds(cut, stride - cut), :].astype(f32)
    for m in range(micros):
        d_hat = head_ref[:, pl.ds(m * chans, chans), :].reshape(wide, width)
        x_hat = normal(tokens_ref, norm_ref, m)
        out_ref[pl.ds(m, 1), :] = jnp.sum(d_hat, axis=0, keepdims=True)
        out_ref[pl.ds(micros + m, 1), :] = jnp.sum(d_hat * x_hat, axis=0, keepdims=True)


def final_kernel(
    rank_ref,
    lens_ref,
    head_ref,
    tokens_ref,
    cot_ref,
    norm_ref,
    *refs,
):
    hat_refs, refs = refs[:-7], refs[-7:]
    d_in_ref, b_ref, e_ref, c_ref, skip_ref, gain_ref, norm_bias_ref = refs
    micros, wide, width = tokens_ref.shape
    seqs, stride, _ = head_ref.shape
    peers = len(hat_refs)
    chans = wide // seqs
    hats = [ref[...] for ref in hat_refs]
    hat = sum(hats[1:], hats[0]) * (1.0 / (peers * wide))
    at = rank_ref[0] * width + lanes((1, width))
    for m in range(micros):
        live = (at < lens_ref[m]).astype(f32)
        d_hat = head_ref[:, pl.ds(m * chans, chans), :].reshape(wide, width)
        x_hat = normal(tokens_ref, norm_ref, m)
        inside = d_hat - hat[m : m + 1] - x_hat * hat[micros + m : micros + m + 1]
        d_in_ref[m] = (
            live * cot_ref[m].astype(f32) + norm_ref[micros + m : micros + m + 1] * inside
        )
    cut = micros * chans
    for k, ref in enumerate((b_ref, e_ref, c_ref)):
        modes = head_ref[:, pl.ds(cut + k * chans, chans), :]
        ref[...] = modes.reshape(wide, -1).T.reshape(ref.shape)
    place = lanes((1, wide)) // chans
    last = cut + 3 * chans
    for k, ref in enumerate((skip_ref, gain_ref, norm_bias_ref)):
        line = jnp.zeros((1, wide), f32)
        for s in range(seqs):
            own = head_ref[s, pl.ds(last, 1), :] + head_ref[s, pl.ds(last + 1, 1), :]
            own = pltpu.roll(own, (s - k) * chans % own.shape[1], axis=1)[:, :wide]
            line = jnp.where(place == s, own, line)
        ref[...] = line


def smem():
    return pl.BlockSpec(memory_space=pltpu.SMEM)


def vmem():
    return pl.BlockSpec(memory_space=pltpu.VMEM)


def in_hbm(x):
    return pltpu.with_memory_space_constraint(x, pltpu.HBM)


def shape_of(shape, kind=f32):
    return jax.ShapeDtypeStruct(shape, kind)


def kernel_call(kernel, name, scalars, arrays, outs, micros_of_time, limit=8, **more):
    ins = [smem()] * len(scalars) + [vmem()] * len(arrays)
    return pl.pallas_call(
        kernel,
        in_specs=ins,
        out_specs=[vmem()] * len(outs),
        out_shape=outs,
        compiler_params=pltpu.CompilerParams(vmem_limit_bytes=limit * 1024 * 1024),
        cost_estimate=cost(micros_of_time),
        name=name,
        **more,
    )(*scalars, *arrays)


def cost(micros_of_time):
    return pl.CostEstimate(
        flops=int(micros_of_time * 1e9), bytes_accessed=int(micros_of_time * 3e6), transcendentals=0
    )


def shards(
    tokens,
    lengths,
    ln_gain,
    ln_bias,
    b_coef,
    e_coef,
    c_coef,
    skip_gain,
    decay_rate,
    rotation,
    w_value,
    w_gate,
    bias_value,
    bias_gate,
    out_cotangent,
):
    micros, wide, width = tokens.shape
    modes = decay_rate.shape[1]
    full = w_value.shape[0]
    seqs = lax.axis_size("seq")
    peers = lax.axis_size("chan")
    seq_rank = lax.axis_index("seq").astype(jnp.int32)
    chan_rank = lax.axis_index("chan").astype(jnp.int32)
    chans = wide // seqs
    rows = micros * seqs
    own = micros * width // peers
    parts = width // own
    both = ("chan", "seq")
    lane = 2 * modes
    spans = int(math.log2(seqs))
    levels = int(math.log2(width)) - 3
    rank = seq_rank.reshape(1)
    lens = lengths.reshape(micros)
    place = jnp.stack([seq_rank, chan_rank])
    bias_rows = (bias_value.reshape(1, wide), bias_gate.reshape(1, wide))

    def exchange(x, axis):
        return lax.all_to_all(x, axis, 0, 0, tiled=True)

    def cross(x, by):
        return lax.ppermute(x, "chan", [(i, i ^ by) for i in range(peers)])

    hbm = pl.BlockSpec(memory_space=pltpu.HBM)
    x_send, part_stats = pl.pallas_call(
        functools.partial(pack_kernel, seqs),
        in_specs=[hbm],
        out_specs=[vmem()] * 2,
        out_shape=[
            shape_of((seqs, micros * (chans + 6), width), bf16),
            shape_of((2 * micros, width)),
        ],
        scratch_shapes=[
            pltpu.VMEM(tokens.shape, bf16),
            pltpu.SemaphoreType.DMA((micros,)),
        ],
        compiler_params=pltpu.CompilerParams(vmem_limit_bytes=8 * 1024 * 1024),
        cost_estimate=cost(1),
        name="pack",
    )(in_hbm(tokens))
    x_mine = exchange(x_send, "seq")
    stats = [part_stats] + [cross(part_stats, k) for k in range(1, peers)]

    cot, wv, wg, _ = lax.optimization_barrier((out_cotangent, w_value, w_gate, part_stats))
    cot_own = cot.reshape(micros, wide, parts, own).transpose(0, 2, 1, 3).reshape(peers, wide, own)
    weights = pl.pallas_call(
        gather_kernel,
        in_specs=[smem()] + [vmem()] * 2 + [hbm] * 3,
        out_specs=[vmem()] * peers,
        out_shape=[shape_of((wide + 2 * full + 16, own), bf16)] * peers,
        scratch_shapes=[pltpu.SemaphoreType.DMA((3 * peers,))],
        compiler_params=pltpu.CompilerParams(vmem_limit_bytes=8 * 1024 * 1024),
        cost_estimate=cost(1),
        name="weights",
    )(chan_rank.reshape(1), *bias_rows, in_hbm(cot_own), in_hbm(wv), in_hbm(wg))

    turned = [jnp.transpose(z, (0, 2, 1)) for z in (b_coef, e_coef, c_coef)]
    const, rise, taps, live = pl.pallas_call(
        functools.partial(table_kernel, chans, seqs, width),
        in_specs=[smem()] * 5 + [hbm] * 5,
        out_specs=[vmem()] * 4,
        out_shape=[
            shape_of((12 + 2 * spans, chans, lane)),
            shape_of(((8 + 2 * levels) * chans, lane)),
            shape_of((chans, 16, width)),
            shape_of((rows, width)),
        ],
        scratch_shapes=[pltpu.VMEM(turned[0].shape, f32)] * 3
        + [pltpu.VMEM((modes, wide), f32)] * 2
        + [
            pltpu.VMEM((wide, lane), f32),
            pltpu.VMEM((17 * chans, lane), f32),
            pltpu.SemaphoreType.DMA((5,)),
        ],
        compiler_params=pltpu.CompilerParams(vmem_limit_bytes=8 * 1024 * 1024),
        cost_estimate=cost(2),
        name="tables",
    )(rank, lens, skip_gain, ln_gain, ln_bias, *[in_hbm(z) for z in (*turned, decay_rate.T, rotation.T)])

    x_mine, const, weights = lax.optimization_barrier((x_mine, const, weights))
    x_stats = x_mine[:, micros * chans :]
    x_stats = [cross(x_stats, k) for k in range(1, peers)]
    weights = [weights[0]] + [cross(weights[k], k) for k in range(1, peers)]
    arrays = (x_mine, const, rise, taps, live, *x_stats)
    act, norm_mine, y_mine, start_mine = pl.pallas_call(
        functools.partial(forward_kernel, micros, seqs, chans, peers),
        in_specs=[vmem()] * len(arrays),
        out_specs=[vmem()] * 4,
        out_shape=[
            shape_of((rows * chans, width), bf16),
            shape_of((2 * rows, width)),
            shape_of((chans, rows, width)),
            shape_of((chans, rows, lane)),
        ],
        scratch_shapes=forward_scratch(micros, seqs, chans, peers, width, lane),
        compiler_params=pltpu.CompilerParams(vmem_limit_bytes=16 * 1024 * 1024),
        cost_estimate=cost(5),
        name="mixer_forward",
    )(*arrays)

    act = (
        act.reshape(micros, seqs, chans, parts, own)
        .transpose(0, 3, 1, 2, 4)
        .reshape(peers * seqs, chans, own)
    )
    act = exchange(act, both).reshape(full, own)
    (d_act,) = kernel_call(
        functools.partial(project_kernel, width),
        "project",
        (place, lens),
        (act, *weights),
        [shape_of((full, own), bf16)],
        2,
        limit=12,
        scratch_shapes=[pltpu.VMEM((own, 2 * full), bf16)],
    )

    acts = [act] + [cross(act, k) for k in range(1, peers)]
    if parts == 1:
        order = chan_rank ^ jnp.arange(peers, dtype=jnp.int32)
    else:
        stacked = jnp.stack(acts)[chan_rank ^ jnp.arange(peers, dtype=jnp.int32)]
        stacked = stacked.reshape(micros, parts, full, own).transpose(0, 2, 1, 3)
        stacked = stacked.reshape(micros, full, width)
        acts = [stacked[m] for m in range(micros)]
        order = jnp.arange(micros, dtype=jnp.int32)

    d_act = exchange(d_act.reshape(peers * seqs, chans, own), both)
    d_act = (
        d_act.reshape(micros, parts, seqs, chans, own)
        .transpose(0, 2, 3, 1, 4)
        .reshape(rows * chans, width)
    )
    count = full // seqs
    part = (2, 2 * count + 8, wide)
    out, keep, *blocks = kernel_call(
        functools.partial(output_kernel, seqs),
        "output",
        (rank, lens, order),
        (tokens, out_cotangent, w_value, w_gate) + bias_rows + tuple(acts),
        [shape_of(tokens.shape, bf16), shape_of(part)] + [shape_of(part, bf16)] * (seqs // 2 - 1),
        2,
        limit=12,
        scratch_shapes=[
            pltpu.VMEM((micros * width, 2 * wide), bf16),
            pltpu.VMEM((seqs,) + part[1:], f32),
        ],
    )
    blocks = [
        lax.ppermute(block, "seq", [(i, i ^ ((k + 1) << 1)) for i in range(seqs)])
        for k, block in enumerate(blocks)
    ]
    d_act, keep, *stats = lax.optimization_barrier((d_act, keep, *stats))
    stride = -(-((micros + 3) * chans + 2) // 16) * 16
    arrays = (x_mine, d_act, norm_mine, const, rise, taps, live, y_mine, start_mine)
    d_hat = pl.pallas_call(
        functools.partial(backward_kernel, micros, seqs, chans),
        in_specs=[vmem()] * len(arrays),
        out_specs=vmem(),
        out_shape=shape_of((seqs, stride, width), bf16),
        scratch_shapes=backward_scratch(micros, seqs, chans, stride, width, lane),
        compiler_params=pltpu.CompilerParams(vmem_limit_bytes=20 * 1024 * 1024),
        cost_estimate=cost(5),
        name="mixer_backward",
    )(*arrays)
    d_hat, *blocks = lax.optimization_barrier((d_hat, *blocks))
    keep, send = kernel_call(
        parts_kernel,
        "parts",
        (seq_rank.reshape(1) & 1,),
        (keep, *blocks),
        [shape_of(part[1:]), shape_of(part[1:], bf16)],
        1,
        scratch_shapes=[pltpu.VMEM(part, f32)],
    )
    got = lax.ppermute(send, "seq", [(i, i ^ 1) for i in range(seqs)])
    d_wv, d_wg, d_bv, d_bg = kernel_call(
        last_kernel,
        "last",
        (),
        (keep, got),
        [shape_of((count, wide))] * 2 + [shape_of((1, wide))] * 2,
        1,
    )
    got = exchange(d_hat, "seq")
    own_sums, head, norm = kernel_call(
        sums_kernel,
        "sums",
        (),
        (got, tokens, *stats),
        [
            shape_of((2 * micros, width)),
            shape_of((seqs, stride, width)),
            shape_of((2 * micros, width)),
        ],
        1,
    )
    hat_sums = [own_sums] + [cross(own_sums, k) for k in range(1, peers)]
    mode_grad = shape_of((2, modes, wide))
    d_input, d_b, d_e, d_c, d_skip, d_gain, d_bias = kernel_call(
        final_kernel,
        "final",
        (rank, lens),
        (head, tokens, out_cotangent, norm, *hat_sums),
        [shape_of(tokens.shape)]
        + [mode_grad] * 3
        + [shape_of((1, wide))] * 3,
        2,
    )
    d_b, d_e, d_c = [jnp.transpose(z, (0, 2, 1)) for z in (d_b, d_e, d_c)]
    d_skip, d_gain, d_bias, d_bv, d_bg = [
        z.reshape(wide) for z in (d_skip, d_gain, d_bias, d_bv, d_bg)
    ]
    return (out, d_input, d_gain, d_bias, d_b, d_e, d_c, d_skip, d_wv, d_wg, d_bv, d_bg)


def solution(mesh):
    chan = P("chan")
    modes = P(None, "chan", None)
    table = P("chan", None)
    weight = P(None, "chan")
    rows = P(None, "chan", "seq")
    spread = P("seq", "chan")
    return jax.shard_map(
        shards,
        mesh=mesh,
        in_specs=(
            rows,
            P(),
            chan,
            chan,
            modes,
            modes,
            modes,
            chan,
            table,
            table,
            weight,
            weight,
            chan,
            chan,
            rows,
        ),
        out_specs=(
            rows,
            rows,
            chan,
            chan,
            modes,
            modes,
            modes,
            chan,
            spread,
            spread,
            chan,
            chan,
        ),
        check_vma=False,
    )
```
